128 devices in a mesh: atm: 16 (over y, x), ocn: 8 (over z, core).
Axes of the slice: x: 4, y: 4, z: 4, core: 2. Of those that a mesh axis runs over, the one named last changes fastest.
Arguments:
- atm_state: float32 [13824, 3, 1024], P('atm', None, 'ocn'), may hold values from -6 to 6
- diffusivity: float32 [13824, 3, 1024], P('atm', None, 'ocn'), may hold values from 0.1 to 0.24
- ocean_state: float32 [32768, 3, 128], P(('atm', 'ocn')), may hold values from -6 to 6
- land_mask: int32 [32768, 128], P(('atm', 'ocn')), may hold values 0 or 1
- intersection_area: float32 [65536, 128], P(('atm', 'ocn')), may hold values from 0.2 to 1
- intersection_seg: int32 [65536], P(('atm', 'ocn')), may hold values from 0 to 255
- intersection_dest: int32 [65536, 1], P(('atm', 'ocn')), may hold values from 0 to 127; in each aligned block of 512 rows (0 to 511, 512 to 1023, ...) at most 8 rows name the same one
- intersection_row: int32 [65536], P(('atm', 'ocn')), may hold values from 0 to 863
Outputs:
- atm_next: float32 [13824, 3, 1024], P('atm', None, 'ocn')
- ocean_flux: float32 [32768, 3, 128], P(('atm', 'ocn'))
The draws below stay inside these ranges and needn't reach their ends.
Inputs may be any that keep to these rules, and one draw needn't show every extreme that they name: intersection_seg indexes the segments owned by the same device as the intersection row. `intersection_dest`: among the 512 intersection rows of one device, no device is named by more than 8 rows, and some device is named by exactly 8.
All inputs are finite; a program needn't handle non-finite values. No bound on the sum of `land_mask` on one device may be relied on, other than what follows from the above.
Results may differ from the reference program's by a relative error of at most 0.00002.
Values sent between devices are 32-bit elements; how exact they have to be, the bound alone decides.
A program may use at most 64 MiB of HBM per device.

```python
import math
import jax
import jax.numpy as jnp
import numpy as np

BY = 864
SEG_W = 128
SEG_DEV = 256
ITERS = 3
OV_DEV = 512
CAP = 8
AY = 13824
AX = 1024
NSEG = 32768
NOV = 65536
N_ATM = 16
N_OCN = 8
DEVICES = 128


def place_ends(entries, own_key, least, high):
    index_at = [jax.random.randint(jax.random.fold_in(own_key, axis), (), 0, length) for axis, length in enumerate(entries.shape)]
    longest = entries.shape.index(max(entries.shape))
    next_to = index_at[:longest] + [(index_at[longest] + 1) % entries.shape[longest]] + index_at[longest + 1:]
    return entries.at[tuple(index_at)].set(least).at[tuple(next_to)].set(high)


def level_of(key, extent, shards, low, largest):
    def one(axis_at, shards_of):
        heights = jax.random.uniform(jax.random.fold_in(jax.random.fold_in(key, 6), axis_at), (shards_of,), jnp.float32, low / len(shards), largest / len(shards))
        return jnp.repeat(jnp.exp(heights), extent[axis_at] // shards_of).reshape((-1,) + (1,) * (len(extent) - axis_at - 1))

    level = one(*shards[0])
    for cut in shards[1:]:
        level = level * one(*cut)
    return level


def routed_block(rng, own, number, rows, count, top, limit, skew):
    ranking = jax.random.permutation(rng, count)
    packed, ordinary = shares(count, rows * top, limit, skew, True), shares(count, rows * top, limit, skew, False)
    places = jnp.arange(count)

    def named(lengths, offset_by):
        used = int((lengths > 0).sum())
        fixed = max(1, used // 4)
        moved = fixed + (places - fixed + offset_by * (used - fixed)) % max(1, count - fixed)
        return jnp.zeros((count,), jnp.int32).at[ranking[jnp.where(places < fixed, places, moved)]].set(jnp.asarray(lengths, jnp.int32))

    lengths = jnp.where(number % 4 == 0, named(packed, number // 4), named(ordinary, number - number // 4 - 1))
    mixed = jax.random.permutation(jax.random.fold_in(own, 3), count)
    source_of, taker = mixed[0:count // 2 * 2:2], mixed[1:count // 2 * 2:2]
    slack = jnp.minimum(lengths[source_of] - 1, limit - lengths[taker]) // 2
    slack = jnp.where((source_of == ranking[0]) | (taker == ranking[0]) | (lengths[taker] == 0), 0, jnp.maximum(slack, 0))
    moved = jax.random.randint(jax.random.fold_in(own, 4), (count // 2,), 0, 1 << 20) % (slack + 1)
    lengths = lengths.at[source_of].add(-moved).at[taker].add(moved)
    labels = jnp.searchsorted(jnp.cumsum(lengths), jnp.arange(rows * top), side="right").astype(jnp.int32)
    listing = labels.reshape(top, rows).T
    listing = listing[jax.random.permutation(jax.random.fold_in(own, 1), rows)]
    offset_by = jax.random.randint(jax.random.fold_in(own, 2), (rows, 1), 0, top)
    return jnp.take_along_axis(listing, (jnp.arange(top)[None, :] + offset_by) % top, axis=1)


def shares(number_of, total, reach, skew, full):
    loads = [(1 << 20) // math.isqrt(grade ** skew) + 1 for grade in range(1, number_of + 1)]
    largest = reach if full else min(reach, max(-(-total // number_of), total * loads[0] // sum(loads)))
    least = 1 if total - largest >= number_of - 1 else 0
    counts, surplus = [largest] + [least] * (number_of - 1), total - largest - least * (number_of - 1)
    while surplus > 0:
        candidates = [i for i in range(1, number_of) if counts[i] < largest] or [i for i in range(1, number_of) if counts[i] < reach]
        pool, left = sum([loads[i] for i in candidates]), surplus
        for i in candidates:
            addition = min(reach - counts[i], max(1, left * loads[i] // pool), surplus)
            counts[i] = counts[i] + addition
            surplus = surplus - addition
    return np.array(counts)


def normal_values(own_key, shape, deviation, most, pieces=(), kind=jnp.bfloat16):
    result = deviation * jax.random.normal(own_key, shape, jnp.float32)
    if pieces:
        result = result * level_of(own_key, shape, pieces, -0.22, 0.18)
    return jnp.clip(result, -most, most).astype(kind)


def setup_inputs(seed: int = 0) -> dict:
    streams_of = jax.random.split(jax.random.key(seed), 9)
    atm_state = normal_values(streams_of[0], (AY, 3, AX), 1.0, 6.0, ((0, 16), (2, 8)), jnp.float32)
    diffusivity = jnp.clip(jnp.exp(math.log(0.24) - 0.8754687 * jax.random.uniform(streams_of[1], (AY, 3, AX), jnp.float32) ** level_of(streams_of[1], (AY, 3, AX), ((0, 16), (2, 8)), -0.2, 0.2)), 0.1, 0.24)
    ocean_state = normal_values(streams_of[2], (NSEG, 3, SEG_W), 1.0, 6.0, ((0, 128),), jnp.float32)
    land_mask = place_ends((jax.random.randint(streams_of[3], (NSEG, SEG_W), 0, 4) < 3).astype(jnp.int32), jax.random.fold_in(streams_of[3], 1), 0, 1)
    intersection_area = jnp.clip(0.2 + 0.8 * jax.random.uniform(streams_of[4], (NOV, SEG_W), jnp.float32) ** level_of(streams_of[4], (NOV, SEG_W), ((0, 128),), -0.2, 0.2), 0.2, 1.0)
    intersection_seg = place_ends(jax.random.randint(streams_of[5], (NOV,), 0, SEG_DEV), jax.random.fold_in(streams_of[5], 1), 0, SEG_DEV - 1).astype(jnp.int32)
    intersection_dest_keys = jax.random.split(jax.random.fold_in(streams_of[6], 1), NOV // OV_DEV)
    intersection_dest_turns = jax.random.permutation(jax.random.fold_in(streams_of[6], 3), NOV // OV_DEV)
    intersection_dest = jax.vmap(lambda own, number: routed_block(jax.random.fold_in(streams_of[6], 2), own, number, OV_DEV, DEVICES, 1, CAP, 2))(intersection_dest_keys, intersection_dest_turns).reshape((NOV, 1))
    intersection_row = place_ends(jax.random.randint(streams_of[7], (NOV,), 0, BY), jax.random.fold_in(streams_of[7], 1), 0, BY - 1).astype(jnp.int32)
    return dict(atm_state=atm_state, diffusivity=diffusivity, ocean_state=ocean_state, land_mask=land_mask, intersection_area=intersection_area, intersection_seg=intersection_seg, intersection_dest=intersection_dest, intersection_row=intersection_row)


def neighbours(grid_field):
    padded = jnp.pad(grid_field, ((1, 1), (0, 0), (1, 1)))
    return padded[2:, :, 1:-1] + padded[:-2, :, 1:-1] + padded[1:-1, :, 2:] + padded[1:-1, :, :-2]

def fluxes(ocean_part, air_part):
    wind_east = air_part[:, 1] - ocean_part[:, 1]
    wind_north = air_part[:, 2] - ocean_part[:, 2]
    wind_speed = jnp.sqrt(wind_east * wind_east + wind_north * wind_north + 0.5)
    temp_gap = ocean_part[:, 0] - air_part[:, 0]
    factor = 1.0 + 0.5 * jnp.tanh(temp_gap / wind_speed)
    return jnp.stack([0.8 * factor * wind_speed * temp_gap, 0.6 * factor * wind_speed * wind_east, 0.6 * factor * wind_speed * wind_north], axis=1)

def reference(atm_state, diffusivity, ocean_state, land_mask, intersection_area, intersection_seg, intersection_dest, intersection_row):
    dev_count = N_ATM * N_OCN
    smoothed = 0.5 * atm_state + 0.125 * neighbours(atm_state)
    blocks = smoothed.reshape(N_ATM, BY, 3, N_OCN, SEG_W).transpose(0, 3, 1, 2, 4).reshape(dev_count * BY, 3, SEG_W)
    owner_dev = jnp.arange(dev_count * OV_DEV, dtype=jnp.int32) // OV_DEV
    seg_global = (owner_dev * SEG_DEV + intersection_seg).astype(jnp.int32)
    row_global = (intersection_dest[:, 0] * BY + intersection_row).astype(jnp.int32)
    weight = intersection_area * land_mask[seg_global].astype(jnp.float32)
    weighted = weight[:, None, :] * fluxes(ocean_state[seg_global], blocks[row_global])
    ocean_flux = jax.ops.segment_sum(weighted, seg_global, num_segments=dev_count * SEG_DEV)
    air_sum = jax.ops.segment_sum(weighted, row_global, num_segments=dev_count * BY)
    air_sum = air_sum.reshape(N_ATM, N_OCN, BY, 3, SEG_W).transpose(0, 2, 3, 1, 4).reshape(N_ATM * BY, 3, N_OCN * SEG_W)
    direction_sign = jnp.array([1.0, -1.0, -1.0], dtype=jnp.float32)[None, :, None]
    current = atm_state + direction_sign * air_sum
    for iteration in range(ITERS):
        current = current + diffusivity * (neighbours(current) - 4.0 * current)
    return (current, ocean_flux)
```

```python
import jax
import jax.numpy as jnp
from jax import lax
from jax.sharding import PartitionSpec as P

ITERS = 3
HIGHEST = lax.Precision.HIGHEST


def with_halo(block, sides, width):
    for axis, dim in sides:
        count = lax.axis_size(axis)
        forward = [(i, i + 1) for i in range(count - 1)]
        backward = [(target, source) for source, target in forward]
        low = lax.ppermute(
            lax.slice_in_dim(block, block.shape[dim] - width, None, axis=dim), axis, forward
        )
        high = lax.ppermute(lax.slice_in_dim(block, 0, width, axis=dim), axis, backward)
        block = jnp.concatenate([low, block, high], axis=dim)
    return block


def beside_all(padded):
    return padded[2:, :, 1:-1] + padded[:-2, :, 1:-1] + padded[1:-1, :, 2:] + padded[1:-1, :, :-2]


def fluxes(ocean_part, air_part):
    wind_east = air_part[:, 1] - ocean_part[:, 1]
    wind_north = air_part[:, 2] - ocean_part[:, 2]
    wind_speed = jnp.sqrt(wind_east * wind_east + wind_north * wind_north + 0.5)
    temp_gap = ocean_part[:, 0] - air_part[:, 0]
    factor = 1.0 + 0.5 * jnp.tanh(temp_gap / wind_speed)
    return jnp.stack(
        [
            0.8 * factor * wind_speed * temp_gap,
            0.6 * factor * wind_speed * wind_east,
            0.6 * factor * wind_speed * wind_north,
        ],
        axis=1,
    )


def one_hot_sum(labels, count, values):
    chosen = (labels[None, :] == jnp.arange(count, dtype=jnp.int32)[:, None]).astype(jnp.float32)
    flat = values.reshape(values.shape[0], -1)
    total = jnp.dot(chosen, flat, precision=HIGHEST, preferred_element_type=jnp.float32)
    return total.reshape((count,) + values.shape[1:])


def per_device(
    atm_state,
    diffusivity,
    ocean_state,
    land_mask,
    intersection_area,
    intersection_seg,
    intersection_dest,
    intersection_row,
):
    atm_count = lax.axis_size("atm")
    ocn_count = lax.axis_size("ocn")
    devices = atm_count * ocn_count
    row_count, chan_count, seg_width = atm_state.shape
    ov_rows = intersection_seg.shape[0]
    capacity = max(2, 2 * ov_rows // devices)
    slots = devices * capacity
    padded = with_halo(atm_state, (("atm", 0), ("ocn", 2)), 1)
    smoothed = 0.5 * atm_state + 0.125 * beside_all(padded)
    target = intersection_dest[:, 0]
    matches = (target[:, None] == jnp.arange(devices, dtype=jnp.int32)[None, :]).astype(jnp.int32)
    position = jnp.sum((jnp.cumsum(matches, axis=0) - matches) * matches, axis=1)
    slot_index = target * capacity + position
    hit = slot_index[:, None] == jnp.arange(slots, dtype=jnp.int32)[None, :]
    source = jnp.sum(jnp.where(hit, jnp.arange(ov_rows, dtype=jnp.int32)[:, None], 0), axis=0)
    used = jnp.any(hit, axis=0)
    seg_rows = jnp.take(ocean_state, intersection_seg, axis=0)
    weight = intersection_area * jnp.take(land_mask, intersection_seg, axis=0).astype(jnp.float32)
    row_label = jnp.broadcast_to(intersection_row.astype(jnp.float32)[:, None, None], (ov_rows, 1, seg_width))
    payload = jnp.concatenate([seg_rows, weight[:, None, :], row_label], axis=1)
    outgoing = jnp.where(used[:, None, None], jnp.take(payload, source, axis=0), 0.0)
    incoming = lax.all_to_all(outgoing, ("atm", "ocn"), split_axis=0, concat_axis=0, tiled=True)
    in_labels = incoming[:, chan_count + 1, 0].astype(jnp.int32)
    air_rows = jnp.take(smoothed, in_labels, axis=0)
    weighted = incoming[:, chan_count : chan_count + 1, :] * fluxes(
        incoming[:, :chan_count, :], air_rows
    )
    air_sum = one_hot_sum(in_labels, row_count, weighted)
    returned = lax.all_to_all(weighted, ("atm", "ocn"), split_axis=0, concat_axis=0, tiled=True)
    slot_seg = jnp.where(used, jnp.take(intersection_seg, source), -1)
    ocean_flux = one_hot_sum(slot_seg, ocean_state.shape[0], returned)
    direction_sign = jnp.array([1.0, -1.0, -1.0], dtype=jnp.float32)[None, :, None]
    current = atm_state + direction_sign * air_sum
    for iteration in range(ITERS):
        bordered = with_halo(current, (("atm", 0), ("ocn", 2)), 1)
        current = current + diffusivity * (beside_all(bordered) - 4.0 * current)
    return (current, ocean_flux)


def solution(mesh):
    placed = (
        P("atm", None, "ocn"),
        P("atm", None, "ocn"),
        P(("atm", "ocn"), None, None),
        P(("atm", "ocn"), None),
        P(("atm", "ocn"), None),
        P(("atm", "ocn")),
        P(("atm", "ocn"), None),
        P(("atm", "ocn")),
    )
    return jax.shard_map(
        per_device,
        mesh=mesh,
        in_specs=placed,
        out_specs=(P("atm", None, "ocn"), P(("atm", "ocn"), None, None)),
        check_vma=False,
    )
```

```python
import functools

import jax
import jax.numpy as jnp
from jax import lax
from jax.experimental import pallas as pl
from jax.experimental.pallas import tpu as pltpu
from jax.sharding import PartitionSpec as P

ITERS = 3
HIGHEST = lax.Precision.HIGHEST
HALO = ITERS


def with_halo(block, sides, width):
    for axis, dim in sides:
        count = lax.axis_size(axis)
        forward = [(i, i + 1) for i in range(count - 1)]
        backward = [(target, source) for source, target in forward]
        low = lax.ppermute(
            lax.slice_in_dim(block, block.shape[dim] - width, None, axis=dim), axis, forward
        )
        high = lax.ppermute(lax.slice_in_dim(block, 0, width, axis=dim), axis, backward)
        block = jnp.concatenate([low, block, high], axis=dim)
    return block


def beside_all(padded):
    return padded[2:, :, 1:-1] + padded[:-2, :, 1:-1] + padded[1:-1, :, 2:] + padded[1:-1, :, :-2]


def fluxes(ocean_part, air_part):
    wind_east = air_part[:, 1] - ocean_part[:, 1]
    wind_north = air_part[:, 2] - ocean_part[:, 2]
    wind_speed = jnp.sqrt(wind_east * wind_east + wind_north * wind_north + 0.5)
    temp_gap = ocean_part[:, 0] - air_part[:, 0]
    factor = 1.0 + 0.5 * jnp.tanh(temp_gap / wind_speed)
    return jnp.stack(
        [
            0.8 * factor * wind_speed * temp_gap,
            0.6 * factor * wind_speed * wind_east,
            0.6 * factor * wind_speed * wind_north,
        ],
        axis=1,
    )


def select_rows(chosen, values, precision=HIGHEST):
    flat = values.reshape(values.shape[0], -1)
    total = jnp.dot(chosen, flat, precision=precision, preferred_element_type=jnp.float32)
    return total.reshape((chosen.shape[0],) + values.shape[1:])


def planes_with_halo(block, rows_padded, lanes):
    chans, rows, width = block.shape
    atm_n = lax.axis_size("atm")
    ocn_n = lax.axis_size("ocn")
    fwd = [(i, i + 1) for i in range(atm_n - 1)]
    bwd = [(t, s) for s, t in fwd]
    up = lax.ppermute(block[:, rows - HALO :, :], "atm", fwd)
    down = lax.ppermute(block[:, :HALO, :], "atm", bwd)
    extra = rows_padded - rows - 2 * HALO
    tall = jnp.concatenate(
        [up, block, down, jnp.zeros((chans, extra, width), block.dtype)], axis=1
    )
    fwd = [(i, i + 1) for i in range(ocn_n - 1)]
    bwd = [(t, s) for s, t in fwd]
    left = lax.ppermute(tall[:, :, width - HALO :], "ocn", fwd)
    right = lax.ppermute(tall[:, :, :HALO], "ocn", bwd)
    gap = lanes - width - 2 * HALO
    return jnp.concatenate(
        [tall, right, jnp.zeros((chans, rows_padded, gap), block.dtype), left], axis=2
    )


def diffuse_kernel(rows, width, state_ref, diff_ref, out_ref):
    rows_padded, lanes = state_ref.shape[1], state_ref.shape[2]
    for chan in range(state_ref.shape[0]):
        state = state_ref[chan]
        diff = diff_ref[chan]
        for iteration in range(ITERS):
            around = (
                pltpu.roll(state, rows_padded - 1, 0)
                + pltpu.roll(state, 1, 0)
                + pltpu.roll(state, lanes - 1, 1)
                + pltpu.roll(state, 1, 1)
            )
            state = state + diff * (around - 4.0 * state)
        out_ref[chan] = state[HALO : HALO + rows, :width]


def diffuse(state_ext, diff_ext, rows, width):
    chans = state_ext.shape[0]
    return pl.pallas_call(
        functools.partial(diffuse_kernel, rows, width),
        out_shape=jax.ShapeDtypeStruct((chans, rows, width), jnp.float32),
        in_specs=[pl.BlockSpec(memory_space=pltpu.VMEM)] * 2,
        out_specs=pl.BlockSpec(memory_space=pltpu.VMEM),
    )(state_ext, diff_ext)


def per_device(
    atm_state,
    diffusivity,
    ocean_state,
    land_mask,
    intersection_area,
    intersection_seg,
    intersection_dest,
    intersection_row,
):
    atm_count = lax.axis_size("atm")
    ocn_count = lax.axis_size("ocn")
    devices = atm_count * ocn_count
    row_count, chan_count, seg_width = atm_state.shape
    seg_count = ocean_state.shape[0]
    ov_rows = intersection_seg.shape[0]
    capacity = max(2, 2 * ov_rows // devices)
    slots = devices * capacity
    rows_padded = -(-(row_count + 2 * HALO) // 8) * 8
    lanes = 2 * seg_width

    diff_ext = planes_with_halo(jnp.transpose(diffusivity, (1, 0, 2)), rows_padded, lanes)

    padded = with_halo(atm_state, (("atm", 0), ("ocn", 2)), 1)
    smoothed = 0.5 * atm_state + 0.125 * beside_all(padded)

    target = intersection_dest[:, 0]
    matches = (target[:, None] == jnp.arange(devices, dtype=jnp.int32)[None, :]).astype(jnp.int32)
    position = jnp.sum((jnp.cumsum(matches, axis=0) - matches) * matches, axis=1)
    slot_index = target * capacity + position
    slot_pick = (
        jnp.arange(slots, dtype=jnp.int32)[:, None] == slot_index[None, :]
    ).astype(jnp.bfloat16)
    seg_pick = (
        intersection_seg[:, None] == jnp.arange(seg_count, dtype=jnp.int32)[None, :]
    ).astype(jnp.bfloat16)
    slot_seg = jnp.dot(slot_pick, seg_pick, preferred_element_type=jnp.float32)
    out_ocean = select_rows(slot_seg, ocean_state)
    out_mask = select_rows(slot_seg, land_mask.astype(jnp.float32), None)
    row_high = (intersection_row // 32).astype(jnp.bfloat16)
    row_low = (intersection_row % 32).astype(jnp.bfloat16)
    row_parts = jnp.concatenate(
        [jnp.broadcast_to(row_high[:, None], (ov_rows, seg_width)),
         jnp.broadcast_to(row_low[:, None], (ov_rows, seg_width))], axis=1
    )
    out_rows = jnp.dot(slot_pick, row_parts, preferred_element_type=jnp.float32)
    out_label = 32.0 * out_rows[:, :seg_width] + out_rows[:, seg_width:]
    out_area = select_rows(slot_pick.astype(jnp.float32), intersection_area)
    out_weight = out_area * out_mask
    outgoing = jnp.concatenate(
        [out_ocean, out_weight[:, None, :], out_label[:, None, :]], axis=1
    )
    incoming = lax.all_to_all(outgoing, ("atm", "ocn"), split_axis=0, concat_axis=0, tiled=True)
    in_labels = jnp.max(incoming[:, chan_count + 1, :], axis=1).astype(jnp.int32)
    row_pick = (
        jnp.arange(row_count, dtype=jnp.int32)[:, None] == in_labels[None, :]
    ).astype(jnp.float32)
    air_rows = select_rows(row_pick.T, smoothed)
    weighted = incoming[:, chan_count : chan_count + 1, :] * fluxes(
        incoming[:, :chan_count, :], air_rows
    )
    air_sum = select_rows(row_pick, weighted)
    returned = lax.all_to_all(weighted, ("atm", "ocn"), split_axis=0, concat_axis=0, tiled=True)
    ocean_flux = select_rows(slot_seg.T, returned)
    direction_sign = jnp.array([1.0, -1.0, -1.0], dtype=jnp.float32)[None, :, None]
    forced = atm_state + direction_sign * air_sum
    state_ext = planes_with_halo(jnp.transpose(forced, (1, 0, 2)), rows_padded, lanes)
    current = diffuse(state_ext, diff_ext, row_count, seg_width)
    return (jnp.transpose(current, (1, 0, 2)), ocean_flux)


def solution(mesh):
    placed = (
        P("atm", None, "ocn"),
        P("atm", None, "ocn"),
        P(("atm", "ocn"), None, None),
        P(("atm", "ocn"), None),
        P(("atm", "ocn"), None),
        P(("atm", "ocn")),
        P(("atm", "ocn"), None),
        P(("atm", "ocn")),
    )
    return jax.shard_map(
        per_device,
        mesh=mesh,
        in_specs=placed,
        out_specs=(P("atm", None, "ocn"), P(("atm", "ocn"), None, None)),
        check_vma=False,
    )
```

```python
import functools

import jax
import jax.numpy as jnp
from jax import lax
from jax.experimental import pallas as pl
from jax.experimental.pallas import tpu as pltpu
from jax.sharding import PartitionSpec as P

ITERS = 3
HIGHEST = lax.Precision.HIGHEST
HALO = ITERS


def with_halo(block, sides, width):
    for axis, dim in sides:
        count = lax.axis_size(axis)
        forward = [(i, i + 1) for i in range(count - 1)]
        backward = [(target, source) for source, target in forward]
        low = lax.ppermute(
            lax.slice_in_dim(block, block.shape[dim] - width, None, axis=dim), axis, forward
        )
        high = lax.ppermute(lax.slice_in_dim(block, 0, width, axis=dim), axis, backward)
        block = jnp.concatenate([low, block, high], axis=dim)
    return block


def beside_all(padded):
    return padded[2:, :, 1:-1] + padded[:-2, :, 1:-1] + padded[1:-1, :, 2:] + padded[1:-1, :, :-2]


def fluxes(ocean_part, air_part):
    wind_east = air_part[:, 1] - ocean_part[:, 1]
    wind_north = air_part[:, 2] - ocean_part[:, 2]
    wind_speed = jnp.sqrt(wind_east * wind_east + wind_north * wind_north + 0.5)
    temp_gap = ocean_part[:, 0] - air_part[:, 0]
    factor = 1.0 + 0.5 * jnp.tanh(temp_gap / wind_speed)
    return jnp.stack(
        [
            0.8 * factor * wind_speed * temp_gap,
            0.6 * factor * wind_speed * wind_east,
            0.6 * factor * wind_speed * wind_north,
        ],
        axis=1,
    )


def select_rows(chosen, values, precision=HIGHEST):
    flat = values.reshape(values.shape[0], -1)
    total = jnp.dot(chosen, flat, precision=precision, preferred_element_type=jnp.float32)
    return total.reshape((chosen.shape[0],) + values.shape[1:])


def planes_with_halo(block, rows_padded, lanes):
    chans, rows, width = block.shape
    atm_n = lax.axis_size("atm")
    ocn_n = lax.axis_size("ocn")
    fwd = [(i, i + 1) for i in range(atm_n - 1)]
    bwd = [(t, s) for s, t in fwd]
    up = lax.ppermute(block[:, rows - HALO :, :], "atm", fwd)
    down = lax.ppermute(block[:, :HALO, :], "atm", bwd)
    extra = rows_padded - rows - 2 * HALO
    tall = jnp.concatenate(
        [up, block, down, jnp.zeros((chans, extra, width), block.dtype)], axis=1
    )
    fwd = [(i, i + 1) for i in range(ocn_n - 1)]
    bwd = [(t, s) for s, t in fwd]
    left = lax.ppermute(tall[:, :, width - HALO :], "ocn", fwd)
    right = lax.ppermute(tall[:, :, :HALO], "ocn", bwd)
    gap = lanes - width - 2 * HALO
    return jnp.concatenate(
        [tall, right, jnp.zeros((chans, rows_padded, gap), block.dtype), left], axis=2
    )


def diffuse_kernel(rows, width, state_ref, diff_ref, out_ref):
    rows_padded, lanes = state_ref.shape[1], state_ref.shape[2]
    for chan in range(state_ref.shape[0]):
        state = state_ref[chan]
        diff = diff_ref[chan]
        for iteration in range(ITERS):
            around = (
                pltpu.roll(state, rows_padded - 1, 0)
                + pltpu.roll(state, 1, 0)
                + pltpu.roll(state, lanes - 1, 1)
                + pltpu.roll(state, 1, 1)
            )
            state = state + diff * (around - 4.0 * state)
        out_ref[chan] = state[HALO : HALO + rows, :width]


def diffuse(state_ext, diff_ext, rows, width):
    chans = state_ext.shape[0]
    return pl.pallas_call(
        functools.partial(diffuse_kernel, rows, width),
        out_shape=jax.ShapeDtypeStruct((chans, rows, width), jnp.float32),
        in_specs=[pl.BlockSpec(memory_space=pltpu.VMEM)] * 2,
        out_specs=pl.BlockSpec(memory_space=pltpu.VMEM),
    )(state_ext, diff_ext)


def per_device(
    atm_state,
    diffusivity,
    ocean_state,
    land_mask,
    intersection_area,
    intersection_seg,
    intersection_dest,
    intersection_row,
):
    atm_count = lax.axis_size("atm")
    ocn_count = lax.axis_size("ocn")
    devices = atm_count * ocn_count
    row_count, chan_count, seg_width = atm_state.shape
    seg_count = ocean_state.shape[0]
    ov_rows = intersection_seg.shape[0]
    capacity = max(2, 2 * ov_rows // devices)
    slots = devices * capacity
    rows_padded = -(-(row_count + 2 * HALO) // 8) * 8
    lanes = 2 * seg_width

    diff_ext = planes_with_halo(jnp.transpose(diffusivity, (1, 0, 2)), rows_padded, lanes)
    padded = with_halo(atm_state, (("atm", 0), ("ocn", 2)), 1)

    target = intersection_dest[:, 0]
    matches = (target[:, None] == jnp.arange(devices, dtype=jnp.int32)[None, :]).astype(jnp.int32)
    position = jnp.sum((jnp.cumsum(matches, axis=0) - matches) * matches, axis=1)
    slot_index = target * capacity + position
    slot_pick = (
        jnp.arange(slots, dtype=jnp.int32)[:, None] == slot_index[None, :]
    ).astype(jnp.bfloat16)
    seg_pick = (
        intersection_seg[:, None] == jnp.arange(seg_count, dtype=jnp.int32)[None, :]
    ).astype(jnp.bfloat16)
    slot_seg = jnp.dot(slot_pick, seg_pick, preferred_element_type=jnp.float32)
    plane = chan_count * seg_width
    out_ocean = select_rows(slot_seg, ocean_state.reshape(seg_count, plane))
    out_mask = select_rows(slot_seg, land_mask.astype(jnp.float32), None)
    row_high = (intersection_row // 32).astype(jnp.bfloat16)
    row_low = (intersection_row % 32).astype(jnp.bfloat16)
    row_parts = jnp.concatenate(
        [jnp.broadcast_to(row_high[:, None], (ov_rows, seg_width)),
         jnp.broadcast_to(row_low[:, None], (ov_rows, seg_width))], axis=1
    )
    out_rows = jnp.dot(slot_pick, row_parts, preferred_element_type=jnp.float32)
    out_label = 32.0 * out_rows[:, :seg_width] + out_rows[:, seg_width:]
    out_area = select_rows(slot_pick.astype(jnp.float32), intersection_area)
    out_weight = out_area * out_mask
    outgoing = jnp.concatenate([out_ocean, out_weight, out_label], axis=1)
    outgoing, padded, diff_ext = lax.optimization_barrier((outgoing, padded, diff_ext))
    smoothed = 0.5 * atm_state + 0.125 * beside_all(padded)
    incoming = lax.all_to_all(outgoing, ("atm", "ocn"), split_axis=0, concat_axis=0, tiled=True)
    in_labels = jnp.max(incoming[:, plane + seg_width :], axis=1).astype(jnp.int32)
    row_pick = (
        jnp.arange(row_count, dtype=jnp.int32)[:, None] == in_labels[None, :]
    ).astype(jnp.float32)
    air_rows = select_rows(row_pick.T, smoothed.reshape(row_count, plane))
    in_ocean = incoming[:, :plane].reshape(slots, chan_count, seg_width)
    in_weight = incoming[:, plane : plane + seg_width]
    weighted = in_weight[:, None, :] * fluxes(
        in_ocean, air_rows.reshape(slots, chan_count, seg_width)
    )
    weighted = weighted.reshape(slots, plane)
    air_sum = select_rows(row_pick, weighted).reshape(row_count, chan_count, seg_width)
    returned = lax.all_to_all(weighted, ("atm", "ocn"), split_axis=0, concat_axis=0, tiled=True)
    ocean_flux = select_rows(slot_seg.T, returned).reshape(seg_count, chan_count, seg_width)
    direction_sign = jnp.array([1.0, -1.0, -1.0], dtype=jnp.float32)[None, :, None]
    forced = atm_state + direction_sign * air_sum
    state_ext = planes_with_halo(jnp.transpose(forced, (1, 0, 2)), rows_padded, lanes)
    current = diffuse(state_ext, diff_ext, row_count, seg_width)
    return (jnp.transpose(current, (1, 0, 2)), ocean_flux)


def solution(mesh):
    placed = (
        P("atm", None, "ocn"),
        P("atm", None, "ocn"),
        P(("atm", "ocn"), None, None),
        P(("atm", "ocn"), None),
        P(("atm", "ocn"), None),
        P(("atm", "ocn")),
        P(("atm", "ocn"), None),
        P(("atm", "ocn")),
    )
    return jax.shard_map(
        per_device,
        mesh=mesh,
        in_specs=placed,
        out_specs=(P("atm", None, "ocn"), P(("atm", "ocn"), None, None)),
        check_vma=False,
    )
```

```python
import functools

import jax
import jax.numpy as jnp
from jax import lax
from jax.experimental import pallas as pl
from jax.experimental.pallas import tpu as pltpu
from jax.sharding import PartitionSpec as P

ITERS = 3
HIGHEST = lax.Precision.HIGHEST
HALO = ITERS


def with_halo(block, sides, width):
    for axis, dim in sides:
        count = lax.axis_size(axis)
        forward = [(i, i + 1) for i in range(count - 1)]
        backward = [(target, source) for source, target in forward]
        low = lax.ppermute(
            lax.slice_in_dim(block, block.shape[dim] - width, None, axis=dim), axis, forward
        )
        high = lax.ppermute(lax.slice_in_dim(block, 0, width, axis=dim), axis, backward)
        block = jnp.concatenate([low, block, high], axis=dim)
    return block


def beside_all(padded):
    return padded[2:, :, 1:-1] + padded[:-2, :, 1:-1] + padded[1:-1, :, 2:] + padded[1:-1, :, :-2]


def fluxes(ocean_part, air_part):
    wind_east = air_part[:, 1] - ocean_part[:, 1]
    wind_north = air_part[:, 2] - ocean_part[:, 2]
    wind_speed = jnp.sqrt(wind_east * wind_east + wind_north * wind_north + 0.5)
    temp_gap = ocean_part[:, 0] - air_part[:, 0]
    factor = 1.0 + 0.5 * jnp.tanh(temp_gap / wind_speed)
    return jnp.stack(
        [
            0.8 * factor * wind_speed * temp_gap,
            0.6 * factor * wind_speed * wind_east,
            0.6 * factor * wind_speed * wind_north,
        ],
        axis=1,
    )


def select_rows(chosen, values, precision=HIGHEST):
    flat = values.reshape(values.shape[0], -1)
    total = jnp.dot(chosen, flat, precision=precision, preferred_element_type=jnp.float32)
    return total.reshape((chosen.shape[0],) + values.shape[1:])


def planes_with_halo(block, rows_padded, lanes):
    chans, rows, width = block.shape
    atm_n = lax.axis_size("atm")
    ocn_n = lax.axis_size("ocn")
    fwd = [(i, i + 1) for i in range(atm_n - 1)]
    bwd = [(t, s) for s, t in fwd]
    up = lax.ppermute(block[:, rows - HALO :, :], "atm", fwd)
    down = lax.ppermute(block[:, :HALO, :], "atm", bwd)
    extra = rows_padded - rows - 2 * HALO
    tall = jnp.concatenate(
        [up, block, down, jnp.zeros((chans, extra, width), block.dtype)], axis=1
    )
    fwd = [(i, i + 1) for i in range(ocn_n - 1)]
    bwd = [(t, s) for s, t in fwd]
    left = lax.ppermute(tall[:, :, width - HALO :], "ocn", fwd)
    right = lax.ppermute(tall[:, :, :HALO], "ocn", bwd)
    gap = lanes - width - 2 * HALO
    return jnp.concatenate(
        [tall, right, jnp.zeros((chans, rows_padded, gap), block.dtype), left], axis=2
    )


def diffuse_kernel(rows, width, state_ref, diff_ref, out_ref):
    rows_padded, lanes = state_ref.shape[1], state_ref.shape[2]
    for chan in range(state_ref.shape[0]):
        state = state_ref[chan]
        diff = diff_ref[chan]
        for iteration in range(ITERS):
            around = (
                pltpu.roll(state, rows_padded - 1, 0)
                + pltpu.roll(state, 1, 0)
                + pltpu.roll(state, lanes - 1, 1)
                + pltpu.roll(state, 1, 1)
            )
            state = state + diff * (around - 4.0 * state)
        out_ref[chan] = state[HALO : HALO + rows, :width]


def smooth_kernel(rows, width, state_ref, out_ref):
    rows_padded, lanes = state_ref.shape[1], state_ref.shape[2]
    for chan in range(out_ref.shape[0]):
        state = state_ref[chan]
        around = (
            pltpu.roll(state, rows_padded - 1, 0)
            + pltpu.roll(state, 1, 0)
            + pltpu.roll(state, lanes - 1, 1)
            + pltpu.roll(state, 1, 1)
        )
        out_ref[chan] = (0.5 * state + 0.125 * around)[HALO : HALO + rows, :width]


def smooth(state_ext, chans, rows, width):
    return pl.pallas_call(
        functools.partial(smooth_kernel, rows, width),
        out_shape=jax.ShapeDtypeStruct((chans, rows, width), jnp.float32),
        in_specs=[pl.BlockSpec(memory_space=pltpu.VMEM)],
        out_specs=pl.BlockSpec(memory_space=pltpu.VMEM),
    )(state_ext)


def diffuse(state_ext, diff_ext, rows, width):
    chans = state_ext.shape[0]
    return pl.pallas_call(
        functools.partial(diffuse_kernel, rows, width),
        out_shape=jax.ShapeDtypeStruct((chans, rows, width), jnp.float32),
        in_specs=[pl.BlockSpec(memory_space=pltpu.VMEM)] * 2,
        out_specs=pl.BlockSpec(memory_space=pltpu.VMEM),
    )(state_ext, diff_ext)


def per_device(
    atm_state,
    diffusivity,
    ocean_state,
    land_mask,
    intersection_area,
    intersection_seg,
    intersection_dest,
    intersection_row,
):
    atm_count = lax.axis_size("atm")
    ocn_count = lax.axis_size("ocn")
    devices = atm_count * ocn_count
    row_count, chan_count, seg_width = atm_state.shape
    seg_count = ocean_state.shape[0]
    ov_rows = intersection_seg.shape[0]
    capacity = max(2, 2 * ov_rows // devices)
    slots = devices * capacity
    rows_padded = -(-(row_count + 2 * HALO) // 8) * 8
    lanes = 2 * seg_width

    target = intersection_dest[:, 0]
    matches = (target[:, None] == jnp.arange(devices, dtype=jnp.int32)[None, :]).astype(jnp.int32)
    position = jnp.sum((jnp.cumsum(matches, axis=0) - matches) * matches, axis=1)
    slot_index = target * capacity + position
    slot_pick = (
        jnp.arange(slots, dtype=jnp.int32)[:, None] == slot_index[None, :]
    ).astype(jnp.bfloat16)
    seg_pick = (
        intersection_seg[:, None] == jnp.arange(seg_count, dtype=jnp.int32)[None, :]
    ).astype(jnp.bfloat16)
    slot_seg = jnp.dot(slot_pick, seg_pick, preferred_element_type=jnp.float32)
    plane = chan_count * seg_width
    out_ocean = select_rows(slot_seg, ocean_state.reshape(seg_count, plane))
    out_mask = select_rows(slot_seg, land_mask.astype(jnp.float32), None)
    row_high = (intersection_row // 32).astype(jnp.bfloat16)
    row_low = (intersection_row % 32).astype(jnp.bfloat16)
    row_parts = jnp.concatenate(
        [jnp.broadcast_to(row_high[:, None], (ov_rows, seg_width)),
         jnp.broadcast_to(row_low[:, None], (ov_rows, seg_width))], axis=1
    )
    out_rows = jnp.dot(slot_pick, row_parts, preferred_element_type=jnp.float32)
    out_label = 32.0 * out_rows[:, :seg_width] + out_rows[:, seg_width:]
    out_area = select_rows(slot_pick.astype(jnp.float32), intersection_area)
    out_weight = out_area * out_mask
    outgoing = jnp.concatenate([out_ocean, out_weight, out_label], axis=1)
    incoming = lax.all_to_all(outgoing, ("atm", "ocn"), split_axis=0, concat_axis=0, tiled=True)

    atm_planes = jnp.transpose(atm_state, (1, 0, 2))
    both = jnp.concatenate([atm_planes, jnp.transpose(diffusivity, (1, 0, 2))], axis=0)
    both_ext = planes_with_halo(both, rows_padded, lanes)
    diff_ext = both_ext[chan_count:]
    smoothed = smooth(both_ext, chan_count, row_count, seg_width)

    in_labels = jnp.max(incoming[:, plane + seg_width :], axis=1).astype(jnp.int32)
    row_pick = (
        jnp.arange(row_count, dtype=jnp.int32)[:, None] == in_labels[None, :]
    ).astype(jnp.float32)
    pick_rows = row_pick.T
    air = [jnp.dot(pick_rows, smoothed[c], precision=HIGHEST, preferred_element_type=jnp.float32)
           for c in range(chan_count)]
    ocean = [incoming[:, c * seg_width : (c + 1) * seg_width] for c in range(chan_count)]
    in_weight = incoming[:, plane : plane + seg_width]
    wind_east = air[1] - ocean[1]
    wind_north = air[2] - ocean[2]
    wind_speed = jnp.sqrt(wind_east * wind_east + wind_north * wind_north + 0.5)
    temp_gap = ocean[0] - air[0]
    factor = 1.0 + 0.5 * jnp.tanh(temp_gap / wind_speed)
    weighted = [
        in_weight * (0.8 * factor * wind_speed * temp_gap),
        in_weight * (0.6 * factor * wind_speed * wind_east),
        in_weight * (0.6 * factor * wind_speed * wind_north),
    ]
    returned = lax.all_to_all(
        jnp.concatenate(weighted, axis=1), ("atm", "ocn"), split_axis=0, concat_axis=0, tiled=True
    )
    ocean_flux = select_rows(slot_seg.T, returned).reshape(seg_count, chan_count, seg_width)
    signs = (1.0, -1.0, -1.0)
    forced = jnp.stack(
        [atm_planes[c] + signs[c] * jnp.dot(row_pick, weighted[c], precision=HIGHEST,
                                             preferred_element_type=jnp.float32)
         for c in range(chan_count)]
    )
    state_ext = planes_with_halo(forced, rows_padded, lanes)
    current = diffuse(state_ext, diff_ext, row_count, seg_width)
    return (jnp.transpose(current, (1, 0, 2)), ocean_flux)


def solution(mesh):
    placed = (
        P("atm", None, "ocn"),
        P("atm", None, "ocn"),
        P(("atm", "ocn"), None, None),
        P(("atm", "ocn"), None),
        P(("atm", "ocn"), None),
        P(("atm", "ocn")),
        P(("atm", "ocn"), None),
        P(("atm", "ocn")),
    )
    return jax.shard_map(
        per_device,
        mesh=mesh,
        in_specs=placed,
        out_specs=(P("atm", None, "ocn"), P(("atm", "ocn"), None, None)),
        check_vma=False,
    )
```

```python
import functools

import jax
import jax.numpy as jnp
from jax import lax
from jax.experimental import pallas as pl
from jax.experimental.pallas import tpu as pltpu
from jax.sharding import PartitionSpec as P

ITERS = 3
HIGHEST = lax.Precision.HIGHEST
HALO = ITERS
EDGE = 8


def with_halo(block, sides, width):
    for axis, dim in sides:
        count = lax.axis_size(axis)
        forward = [(i, i + 1) for i in range(count - 1)]
        backward = [(target, source) for source, target in forward]
        low = lax.ppermute(
            lax.slice_in_dim(block, block.shape[dim] - width, None, axis=dim), axis, forward
        )
        high = lax.ppermute(lax.slice_in_dim(block, 0, width, axis=dim), axis, backward)
        block = jnp.concatenate([low, block, high], axis=dim)
    return block


def beside_all(padded):
    return padded[2:, :, 1:-1] + padded[:-2, :, 1:-1] + padded[1:-1, :, 2:] + padded[1:-1, :, :-2]


def fluxes(ocean_part, air_part):
    wind_east = air_part[:, 1] - ocean_part[:, 1]
    wind_north = air_part[:, 2] - ocean_part[:, 2]
    wind_speed = jnp.sqrt(wind_east * wind_east + wind_north * wind_north + 0.5)
    temp_gap = ocean_part[:, 0] - air_part[:, 0]
    factor = 1.0 + 0.5 * jnp.tanh(temp_gap / wind_speed)
    return jnp.stack(
        [
            0.8 * factor * wind_speed * temp_gap,
            0.6 * factor * wind_speed * wind_east,
            0.6 * factor * wind_speed * wind_north,
        ],
        axis=1,
    )


def select_rows(chosen, values, precision=HIGHEST):
    flat = values.reshape(values.shape[0], -1)
    total = jnp.dot(chosen, flat, precision=precision, preferred_element_type=jnp.float32)
    return total.reshape((chosen.shape[0],) + values.shape[1:])


def halo_parts(block):
    chans, rows, width = block.shape
    atm_n = lax.axis_size("atm")
    ocn_n = lax.axis_size("ocn")
    fwd = [(i, i + 1) for i in range(atm_n - 1)]
    bwd = [(t, s) for s, t in fwd]
    up = lax.ppermute(block[:, rows - EDGE :, :], "atm", fwd)
    down = lax.ppermute(block[:, :EDGE, :], "atm", bwd)
    tall = jnp.concatenate([up, block, down], axis=1)
    fwd = [(i, i + 1) for i in range(ocn_n - 1)]
    bwd = [(t, s) for s, t in fwd]
    left = lax.ppermute(tall[:, :, width - HALO :], "ocn", fwd)
    right = lax.ppermute(tall[:, :, :HALO], "ocn", bwd)
    side = jnp.concatenate(
        [right, jnp.zeros((chans, rows + 2 * EDGE, width - 2 * HALO), block.dtype), left], axis=2
    )
    return up, down, side


def assemble(block, up, down, side):
    tall = jnp.concatenate([up, block, down], axis=0)
    return jnp.concatenate([tall, side], axis=1)


def stencil_sum(state):
    rows_padded, lanes = state.shape
    return (
        pltpu.roll(state, rows_padded - 1, 0)
        + pltpu.roll(state, 1, 0)
        + pltpu.roll(state, lanes - 1, 1)
        + pltpu.roll(state, 1, 1)
    )


def smooth_kernel(block_ref, up_ref, down_ref, side_ref, out_ref):
    rows, width = out_ref.shape[1], out_ref.shape[2]
    for chan in range(out_ref.shape[0]):
        state = assemble(block_ref[chan], up_ref[chan], down_ref[chan], side_ref[chan])
        out_ref[chan] = (0.5 * state + 0.125 * stencil_sum(state))[EDGE : EDGE + rows, :width]


def diffuse_kernel(block_ref, up_ref, down_ref, side_ref, dblock_ref, dup_ref, ddown_ref,
                   dside_ref, out_ref):
    rows, width = out_ref.shape[1], out_ref.shape[2]
    first = dblock_ref.shape[0] - out_ref.shape[0]
    for chan in range(out_ref.shape[0]):
        state = assemble(block_ref[chan], up_ref[chan], down_ref[chan], side_ref[chan])
        dc = first + chan
        diff = assemble(dblock_ref[dc], dup_ref[dc], ddown_ref[dc], dside_ref[dc])
        for iteration in range(ITERS):
            state = state + diff * (stencil_sum(state) - 4.0 * state)
        out_ref[chan] = state[EDGE : EDGE + rows, :width]


def vmem_call(kernel, out_shape, args):
    return pl.pallas_call(
        kernel,
        out_shape=out_shape,
        in_specs=[pl.BlockSpec(memory_space=pltpu.VMEM)] * len(args),
        out_specs=pl.BlockSpec(memory_space=pltpu.VMEM),
    )(*args)


def per_device(
    atm_state,
    diffusivity,
    ocean_state,
    land_mask,
    intersection_area,
    intersection_seg,
    intersection_dest,
    intersection_row,
):
    atm_count = lax.axis_size("atm")
    ocn_count = lax.axis_size("ocn")
    devices = atm_count * ocn_count
    row_count, chan_count, seg_width = atm_state.shape
    seg_count = ocean_state.shape[0]
    ov_rows = intersection_seg.shape[0]
    capacity = max(2, 2 * ov_rows // devices)
    slots = devices * capacity
    rows_padded = -(-(row_count + 2 * HALO) // 8) * 8
    lanes = 2 * seg_width

    target = intersection_dest[:, 0]
    matches = (target[:, None] == jnp.arange(devices, dtype=jnp.int32)[None, :]).astype(jnp.int32)
    position = jnp.sum((jnp.cumsum(matches, axis=0) - matches) * matches, axis=1)
    slot_index = target * capacity + position
    slot_pick = (
        jnp.arange(slots, dtype=jnp.int32)[:, None] == slot_index[None, :]
    ).astype(jnp.bfloat16)
    seg_pick = (
        intersection_seg[:, None] == jnp.arange(seg_count, dtype=jnp.int32)[None, :]
    ).astype(jnp.bfloat16)
    slot_seg = jnp.dot(slot_pick, seg_pick, preferred_element_type=jnp.float32)
    plane = chan_count * seg_width
    out_ocean = select_rows(slot_seg, ocean_state.reshape(seg_count, plane))
    out_mask = select_rows(slot_seg, land_mask.astype(jnp.float32), None)
    row_high = (intersection_row // 32).astype(jnp.bfloat16)
    row_low = (intersection_row % 32).astype(jnp.bfloat16)
    row_parts = jnp.concatenate(
        [jnp.broadcast_to(row_high[:, None], (ov_rows, seg_width)),
         jnp.broadcast_to(row_low[:, None], (ov_rows, seg_width))], axis=1
    )
    out_rows = jnp.dot(slot_pick, row_parts, preferred_element_type=jnp.float32)
    out_label = 32.0 * out_rows[:, :seg_width] + out_rows[:, seg_width:]
    out_area = select_rows(slot_pick.astype(jnp.float32), intersection_area)
    out_weight = out_area * out_mask
    outgoing = jnp.concatenate([out_ocean, out_weight, out_label], axis=1)
    incoming = lax.all_to_all(outgoing, ("atm", "ocn"), split_axis=0, concat_axis=0, tiled=True)

    atm_planes = jnp.transpose(atm_state, (1, 0, 2))
    both = jnp.concatenate([atm_planes, jnp.transpose(diffusivity, (1, 0, 2))], axis=0)
    both_parts = halo_parts(both)
    plane_shape = jax.ShapeDtypeStruct((chan_count, row_count, seg_width), jnp.float32)
    smoothed = vmem_call(smooth_kernel, plane_shape, (both,) + both_parts)

    in_labels = jnp.max(incoming[:, plane + seg_width :], axis=1).astype(jnp.int32)
    row_pick = (
        jnp.arange(row_count, dtype=jnp.int32)[:, None] == in_labels[None, :]
    ).astype(jnp.float32)
    pick_rows = row_pick.T
    air = [jnp.dot(pick_rows, smoothed[c], precision=HIGHEST, preferred_element_type=jnp.float32)
           for c in range(chan_count)]
    ocean = [incoming[:, c * seg_width : (c + 1) * seg_width] for c in range(chan_count)]
    in_weight = incoming[:, plane : plane + seg_width]
    wind_east = air[1] - ocean[1]
    wind_north = air[2] - ocean[2]
    wind_speed = jnp.sqrt(wind_east * wind_east + wind_north * wind_north + 0.5)
    temp_gap = ocean[0] - air[0]
    factor = 1.0 + 0.5 * jnp.tanh(temp_gap / wind_speed)
    weighted = [
        in_weight * (0.8 * factor * wind_speed * temp_gap),
        in_weight * (0.6 * factor * wind_speed * wind_east),
        in_weight * (0.6 * factor * wind_speed * wind_north),
    ]
    returned = lax.all_to_all(
        jnp.concatenate(weighted, axis=1), ("atm", "ocn"), split_axis=0, concat_axis=0, tiled=True
    )
    ocean_flux = select_rows(slot_seg.T, returned).reshape(seg_count, chan_count, seg_width)
    signs = (1.0, -1.0, -1.0)
    forced = jnp.stack(
        [atm_planes[c] + signs[c] * jnp.dot(row_pick, weighted[c], precision=HIGHEST,
                                             preferred_element_type=jnp.float32)
         for c in range(chan_count)]
    )
    forced_parts = halo_parts(forced)
    ocean_flux, forced, forced_parts = lax.optimization_barrier((ocean_flux, forced, forced_parts))
    current = vmem_call(diffuse_kernel, plane_shape, (forced,) + forced_parts + (both,) + both_parts)
    return (jnp.transpose(current, (1, 0, 2)), ocean_flux)


def solution(mesh):
    placed = (
        P("atm", None, "ocn"),
        P("atm", None, "ocn"),
        P(("atm", "ocn"), None, None),
        P(("atm", "ocn"), None),
        P(("atm", "ocn"), None),
        P(("atm", "ocn")),
        P(("atm", "ocn"), None),
        P(("atm", "ocn")),
    )
    return jax.shard_map(
        per_device,
        mesh=mesh,
        in_specs=placed,
        out_specs=(P("atm", None, "ocn"), P(("atm", "ocn"), None, None)),
        check_vma=False,
    )
```

```python
import functools

import jax
import jax.numpy as jnp
from jax import lax
from jax.experimental import pallas as pl
from jax.experimental.pallas import tpu as pltpu
from jax.sharding import PartitionSpec as P

ITERS = 3
HIGHEST = lax.Precision.HIGHEST
HALO = ITERS
EDGE = 8


def with_halo(block, sides, width):
    for axis, dim in sides:
        count = lax.axis_size(axis)
        forward = [(i, i + 1) for i in range(count - 1)]
        backward = [(target, source) for source, target in forward]
        low = lax.ppermute(
            lax.slice_in_dim(block, block.shape[dim] - width, None, axis=dim), axis, forward
        )
        high = lax.ppermute(lax.slice_in_dim(block, 0, width, axis=dim), axis, backward)
        block = jnp.concatenate([low, block, high], axis=dim)
    return block


def beside_all(padded):
    return padded[2:, :, 1:-1] + padded[:-2, :, 1:-1] + padded[1:-1, :, 2:] + padded[1:-1, :, :-2]


def fluxes(ocean_part, air_part):
    wind_east = air_part[:, 1] - ocean_part[:, 1]
    wind_north = air_part[:, 2] - ocean_part[:, 2]
    wind_speed = jnp.sqrt(wind_east * wind_east + wind_north * wind_north + 0.5)
    temp_gap = ocean_part[:, 0] - air_part[:, 0]
    factor = 1.0 + 0.5 * jnp.tanh(temp_gap / wind_speed)
    return jnp.stack(
        [
            0.8 * factor * wind_speed * temp_gap,
            0.6 * factor * wind_speed * wind_east,
            0.6 * factor * wind_speed * wind_north,
        ],
        axis=1,
    )


def select_rows(chosen, values, precision=HIGHEST):
    flat = values.reshape(values.shape[0], -1)
    total = jnp.dot(chosen, flat, precision=precision, preferred_element_type=jnp.float32)
    return total.reshape((chosen.shape[0],) + values.shape[1:])


MESH = pl.DeviceIdType.MESH


def exchange(sizes, x_ref, rows_buf, cols_buf, colsend, tall_s, side_s, send_sem, recv_sem):
    atm_n, ocn_n = sizes
    chans, rows, width = x_ref.shape
    rows_padded = tall_s.shape[1]
    me_a = lax.axis_index("atm")
    me_o = lax.axis_index("ocn")
    up = lax.rem(me_a + atm_n - 1, atm_n)
    down = lax.rem(me_a + 1, atm_n)
    left = lax.rem(me_o + ocn_n - 1, ocn_n)
    right = lax.rem(me_o + 1, ocn_n)
    barrier = pltpu.get_barrier_semaphore()
    for peer in ((up, me_o), (down, me_o), (me_a, left), (me_a, right)):
        pl.semaphore_signal(barrier, 1, device_id=peer, device_id_type=MESH)
    pl.semaphore_wait(barrier, 4)

    to_down = pltpu.make_async_remote_copy(
        x_ref.at[:, rows - EDGE :, :], rows_buf.at[0], send_sem.at[0], recv_sem.at[0],
        device_id=(down, me_o), device_id_type=MESH)
    to_up = pltpu.make_async_remote_copy(
        x_ref.at[:, :EDGE, :], rows_buf.at[1], send_sem.at[1], recv_sem.at[1],
        device_id=(up, me_o), device_id_type=MESH)
    to_down.start()
    to_up.start()
    to_down.wait()
    to_up.wait()

    has_up = me_a > 0
    has_down = me_a < atm_n - 1
    has_left = me_o > 0
    has_right = me_o < ocn_n - 1
    spare = jnp.zeros((rows_padded - rows - 2 * EDGE, width), jnp.float32)
    for c in range(chans):
        top = jnp.where(has_up, rows_buf[0, c], 0.0)
        bottom = jnp.where(has_down, rows_buf[1, c], 0.0)
        tall = jnp.concatenate([top, x_ref[c], bottom, spare], axis=0)
        tall_s[c] = tall
        flipped = tall.T
        colsend[0, c] = flipped[:EDGE]
        colsend[1, c] = flipped[width - EDGE :]

    to_left = pltpu.make_async_remote_copy(
        colsend.at[0], cols_buf.at[1], send_sem.at[2], recv_sem.at[2],
        device_id=(me_a, left), device_id_type=MESH)
    to_right = pltpu.make_async_remote_copy(
        colsend.at[1], cols_buf.at[0], send_sem.at[3], recv_sem.at[3],
        device_id=(me_a, right), device_id_type=MESH)
    to_left.start()
    to_right.start()
    to_left.wait()
    to_right.wait()

    middle = jnp.zeros((width - 2 * EDGE, rows_padded), jnp.float32)
    for c in range(chans):
        from_left = jnp.where(has_left, cols_buf[0, c], 0.0)
        from_right = jnp.where(has_right, cols_buf[1, c], 0.0)
        side_s[c] = jnp.concatenate([from_right, middle, from_left], axis=0).T


def exchange_scratch(chans, rows_padded, width):
    return [
        pltpu.VMEM((2, chans, EDGE, width), jnp.float32),
        pltpu.VMEM((2, chans, EDGE, rows_padded), jnp.float32),
        pltpu.VMEM((2, chans, EDGE, rows_padded), jnp.float32),
        pltpu.VMEM((chans, rows_padded, width), jnp.float32),
        pltpu.VMEM((chans, rows_padded, width), jnp.float32),
        pltpu.SemaphoreType.DMA((4,)),
        pltpu.SemaphoreType.DMA((4,)),
    ]


def stencil_sum(state):
    rows_padded, lanes = state.shape
    return (
        pltpu.roll(state, rows_padded - 1, 0)
        + pltpu.roll(state, 1, 0)
        + pltpu.roll(state, lanes - 1, 1)
        + pltpu.roll(state, 1, 1)
    )


def smooth_kernel(sizes, x_ref, out_ref, tall_out, side_out, *scratch):
    rows_buf, cols_buf, colsend, tall_s, side_s, send_sem, recv_sem = scratch
    exchange(sizes, x_ref, rows_buf, cols_buf, colsend, tall_s, side_s, send_sem, recv_sem)
    rows, width = out_ref.shape[1], out_ref.shape[2]
    tall_out[...] = tall_s[...]
    side_out[...] = side_s[...]
    for chan in range(out_ref.shape[0]):
        state = jnp.concatenate([tall_s[chan], side_s[chan]], axis=1)
        out_ref[chan] = (0.5 * state + 0.125 * stencil_sum(state))[EDGE : EDGE + rows, :width]


def diffuse_kernel(sizes, x_ref, dtall_ref, dside_ref, out_ref, *scratch):
    rows_buf, cols_buf, colsend, tall_s, side_s, send_sem, recv_sem = scratch
    exchange(sizes, x_ref, rows_buf, cols_buf, colsend, tall_s, side_s, send_sem, recv_sem)
    rows, width = out_ref.shape[1], out_ref.shape[2]
    first = dtall_ref.shape[0] - out_ref.shape[0]
    for chan in range(out_ref.shape[0]):
        state = jnp.concatenate([tall_s[chan], side_s[chan]], axis=1)
        diff = jnp.concatenate([dtall_ref[first + chan], dside_ref[first + chan]], axis=1)
        for iteration in range(ITERS):
            state = state + diff * (stencil_sum(state) - 4.0 * state)
        out_ref[chan] = state[EDGE : EDGE + rows, :width]


def smooth_call(sizes, both, chans, rows_padded):
    total, rows, width = both.shape
    vmem = pl.BlockSpec(memory_space=pltpu.VMEM)
    return pl.pallas_call(
        functools.partial(smooth_kernel, sizes),
        out_shape=(
            jax.ShapeDtypeStruct((chans, rows, width), jnp.float32),
            jax.ShapeDtypeStruct((total, rows_padded, width), jnp.float32),
            jax.ShapeDtypeStruct((total, rows_padded, width), jnp.float32),
        ),
        in_specs=[vmem],
        out_specs=(vmem, vmem, vmem),
        scratch_shapes=exchange_scratch(total, rows_padded, width),
        compiler_params=pltpu.CompilerParams(collective_id=0, has_side_effects=True),
    )(both)


def diffuse_call(sizes, forced, dtall, dside):
    chans, rows, width = forced.shape
    rows_padded = dtall.shape[1]
    vmem = pl.BlockSpec(memory_space=pltpu.VMEM)
    return pl.pallas_call(
        functools.partial(diffuse_kernel, sizes),
        out_shape=jax.ShapeDtypeStruct((chans, rows, width), jnp.float32),
        in_specs=[vmem] * 3,
        out_specs=vmem,
        scratch_shapes=exchange_scratch(chans, rows_padded, width),
        compiler_params=pltpu.CompilerParams(collective_id=1, has_side_effects=True),
    )(forced, dtall, dside)


def per_device(
    atm_state,
    diffusivity,
    ocean_state,
    land_mask,
    intersection_area,
    intersection_seg,
    intersection_dest,
    intersection_row,
):
    atm_count = lax.axis_size("atm")
    ocn_count = lax.axis_size("ocn")
    devices = atm_count * ocn_count
    row_count, chan_count, seg_width = atm_state.shape
    seg_count = ocean_state.shape[0]
    ov_rows = intersection_seg.shape[0]
    capacity = max(2, 2 * ov_rows // devices)
    slots = devices * capacity

    target = intersection_dest[:, 0]
    matches = (target[:, None] == jnp.arange(devices, dtype=jnp.int32)[None, :]).astype(jnp.int32)
    position = jnp.sum((jnp.cumsum(matches, axis=0) - matches) * matches, axis=1)
    slot_index = target * capacity + position
    slot_pick = (
        jnp.arange(slots, dtype=jnp.int32)[:, None] == slot_index[None, :]
    ).astype(jnp.bfloat16)
    seg_pick = (
        intersection_seg[:, None] == jnp.arange(seg_count, dtype=jnp.int32)[None, :]
    ).astype(jnp.bfloat16)
    slot_seg = jnp.dot(slot_pick, seg_pick, preferred_element_type=jnp.float32)
    plane = chan_count * seg_width
    out_ocean = select_rows(slot_seg, ocean_state.reshape(seg_count, plane))
    out_mask = select_rows(slot_seg, land_mask.astype(jnp.float32), None)
    row_high = (intersection_row // 32).astype(jnp.bfloat16)
    row_low = (intersection_row % 32).astype(jnp.bfloat16)
    row_parts = jnp.concatenate(
        [jnp.broadcast_to(row_high[:, None], (ov_rows, seg_width)),
         jnp.broadcast_to(row_low[:, None], (ov_rows, seg_width))], axis=1
    )
    out_rows = jnp.dot(slot_pick, row_parts, preferred_element_type=jnp.float32)
    out_label = 32.0 * out_rows[:, :seg_width] + out_rows[:, seg_width:]
    out_area = select_rows(slot_pick.astype(jnp.float32), intersection_area)
    out_weight = out_area * out_mask
    outgoing = jnp.concatenate([out_ocean, out_weight, out_label], axis=1)
    incoming = lax.all_to_all(outgoing, ("atm", "ocn"), split_axis=0, concat_axis=0, tiled=True)

    atm_planes = jnp.transpose(atm_state, (1, 0, 2))
    both = jnp.concatenate([atm_planes, jnp.transpose(diffusivity, (1, 0, 2))], axis=0)
    sizes = (atm_count, ocn_count)
    rows_padded = -(-(row_count + 2 * EDGE) // 128) * 128
    smoothed, dtall, dside = smooth_call(sizes, both, chan_count, rows_padded)

    in_labels = jnp.max(incoming[:, plane + seg_width :], axis=1).astype(jnp.int32)
    row_pick = (
        jnp.arange(row_count, dtype=jnp.int32)[:, None] == in_labels[None, :]
    ).astype(jnp.float32)
    pick_rows = row_pick.T
    air = [jnp.dot(pick_rows, smoothed[c], precision=HIGHEST, preferred_element_type=jnp.float32)
           for c in range(chan_count)]
    ocean = [incoming[:, c * seg_width : (c + 1) * seg_width] for c in range(chan_count)]
    in_weight = incoming[:, plane : plane + seg_width]
    wind_east = air[1] - ocean[1]
    wind_north = air[2] - ocean[2]
    wind_speed = jnp.sqrt(wind_east * wind_east + wind_north * wind_north + 0.5)
    temp_gap = ocean[0] - air[0]
    factor = 1.0 + 0.5 * jnp.tanh(temp_gap / wind_speed)
    weighted = [
        in_weight * (0.8 * factor * wind_speed * temp_gap),
        in_weight * (0.6 * factor * wind_speed * wind_east),
        in_weight * (0.6 * factor * wind_speed * wind_north),
    ]
    returned = lax.all_to_all(
        jnp.concatenate(weighted, axis=1), ("atm", "ocn"), split_axis=0, concat_axis=0, tiled=True
    )
    ocean_flux = select_rows(slot_seg.T, returned).reshape(seg_count, chan_count, seg_width)
    signs = (1.0, -1.0, -1.0)
    forced = jnp.stack(
        [atm_planes[c] + signs[c] * jnp.dot(row_pick, weighted[c], precision=HIGHEST,
                                             preferred_element_type=jnp.float32)
         for c in range(chan_count)]
    )
    ocean_flux, forced = lax.optimization_barrier((ocean_flux, forced))
    current = diffuse_call(sizes, forced, dtall, dside)
    return (jnp.transpose(current, (1, 0, 2)), ocean_flux)


def solution(mesh):
    placed = (
        P("atm", None, "ocn"),
        P("atm", None, "ocn"),
        P(("atm", "ocn"), None, None),
        P(("atm", "ocn"), None),
        P(("atm", "ocn"), None),
        P(("atm", "ocn")),
        P(("atm", "ocn"), None),
        P(("atm", "ocn")),
    )
    return jax.shard_map(
        per_device,
        mesh=mesh,
        in_specs=placed,
        out_specs=(P("atm", None, "ocn"), P(("atm", "ocn"), None, None)),
        check_vma=False,
    )
```

```python
import functools

import jax
import jax.numpy as jnp
from jax import lax
from jax.experimental import pallas as pl
from jax.experimental.pallas import tpu as pltpu
from jax.sharding import PartitionSpec as P

ITERS = 3
HIGHEST = lax.Precision.HIGHEST
HALO = ITERS
EDGE = 8


def with_halo(block, sides, width):
    for axis, dim in sides:
        count = lax.axis_size(axis)
        forward = [(i, i + 1) for i in range(count - 1)]
        backward = [(target, source) for source, target in forward]
        low = lax.ppermute(
            lax.slice_in_dim(block, block.shape[dim] - width, None, axis=dim), axis, forward
        )
        high = lax.ppermute(lax.slice_in_dim(block, 0, width, axis=dim), axis, backward)
        block = jnp.concatenate([low, block, high], axis=dim)
    return block


def beside_all(padded):
    return padded[2:, :, 1:-1] + padded[:-2, :, 1:-1] + padded[1:-1, :, 2:] + padded[1:-1, :, :-2]


def fluxes(ocean_part, air_part):
    wind_east = air_part[:, 1] - ocean_part[:, 1]
    wind_north = air_part[:, 2] - ocean_part[:, 2]
    wind_speed = jnp.sqrt(wind_east * wind_east + wind_north * wind_north + 0.5)
    temp_gap = ocean_part[:, 0] - air_part[:, 0]
    factor = 1.0 + 0.5 * jnp.tanh(temp_gap / wind_speed)
    return jnp.stack(
        [
            0.8 * factor * wind_speed * temp_gap,
            0.6 * factor * wind_speed * wind_east,
            0.6 * factor * wind_speed * wind_north,
        ],
        axis=1,
    )


def select_rows(chosen, values, precision=HIGHEST):
    flat = values.reshape(values.shape[0], -1)
    total = jnp.dot(chosen, flat, precision=precision, preferred_element_type=jnp.float32)
    return total.reshape((chosen.shape[0],) + values.shape[1:])


MESH = pl.DeviceIdType.MESH


def exchange(sizes, x_ref, rows_buf, cols_buf, colsend, tall_s, side_s, send_sem, recv_sem):
    atm_n, ocn_n = sizes
    chans, rows, width = x_ref.shape
    rows_padded = tall_s.shape[1]
    me_a = lax.axis_index("atm")
    me_o = lax.axis_index("ocn")
    up = lax.rem(me_a + atm_n - 1, atm_n)
    down = lax.rem(me_a + 1, atm_n)
    left = lax.rem(me_o + ocn_n - 1, ocn_n)
    right = lax.rem(me_o + 1, ocn_n)
    barrier = pltpu.get_barrier_semaphore()
    for peer in ((up, me_o), (down, me_o), (me_a, left), (me_a, right)):
        pl.semaphore_signal(barrier, 1, device_id=peer, device_id_type=MESH)
    pl.semaphore_wait(barrier, 4)

    to_down = pltpu.make_async_remote_copy(
        x_ref.at[:, rows - EDGE :, :], rows_buf.at[0], send_sem.at[0], recv_sem.at[0],
        device_id=(down, me_o), device_id_type=MESH)
    to_up = pltpu.make_async_remote_copy(
        x_ref.at[:, :EDGE, :], rows_buf.at[1], send_sem.at[1], recv_sem.at[1],
        device_id=(up, me_o), device_id_type=MESH)
    to_down.start()
    to_up.start()
    to_down.wait()
    to_up.wait()

    has_up = me_a > 0
    has_down = me_a < atm_n - 1
    has_left = me_o > 0
    has_right = me_o < ocn_n - 1
    spare = jnp.zeros((rows_padded - rows - 2 * EDGE, width), jnp.float32)
    for c in range(chans):
        top = jnp.where(has_up, rows_buf[0, c], 0.0)
        bottom = jnp.where(has_down, rows_buf[1, c], 0.0)
        tall = jnp.concatenate([top, x_ref[c], bottom, spare], axis=0)
        tall_s[c] = tall
        flipped = tall.T
        colsend[0, c] = flipped[:EDGE]
        colsend[1, c] = flipped[width - EDGE :]

    to_left = pltpu.make_async_remote_copy(
        colsend.at[0], cols_buf.at[1], send_sem.at[2], recv_sem.at[2],
        device_id=(me_a, left), device_id_type=MESH)
    to_right = pltpu.make_async_remote_copy(
        colsend.at[1], cols_buf.at[0], send_sem.at[3], recv_sem.at[3],
        device_id=(me_a, right), device_id_type=MESH)
    to_left.start()
    to_right.start()
    to_left.wait()
    to_right.wait()

    middle = jnp.zeros((width - 2 * EDGE, rows_padded), jnp.float32)
    for c in range(chans):
        from_left = jnp.where(has_left, cols_buf[0, c], 0.0)
        from_right = jnp.where(has_right, cols_buf[1, c], 0.0)
        side_s[c] = jnp.concatenate([from_right, middle, from_left], axis=0).T


def exchange_scratch(chans, rows_padded, width):
    return [
        pltpu.VMEM((2, chans, EDGE, width), jnp.float32),
        pltpu.VMEM((2, chans, EDGE, rows_padded), jnp.float32),
        pltpu.VMEM((2, chans, EDGE, rows_padded), jnp.float32),
        pltpu.VMEM((chans, rows_padded, width), jnp.float32),
        pltpu.VMEM((chans, rows_padded, width), jnp.float32),
        pltpu.SemaphoreType.DMA((4,)),
        pltpu.SemaphoreType.DMA((4,)),
    ]


def stencil_sum(state):
    rows_padded, lanes = state.shape
    return (
        pltpu.roll(state, rows_padded - 1, 0)
        + pltpu.roll(state, 1, 0)
        + pltpu.roll(state, lanes - 1, 1)
        + pltpu.roll(state, 1, 1)
    )


def smooth_kernel(sizes, x_ref, out_ref, tall_out, side_out, *scratch):
    rows_buf, cols_buf, colsend, tall_s, side_s, send_sem, recv_sem = scratch
    exchange(sizes, x_ref, rows_buf, cols_buf, colsend, tall_s, side_s, send_sem, recv_sem)
    rows, width = out_ref.shape[1], out_ref.shape[2]
    tall_out[...] = tall_s[...]
    side_out[...] = side_s[...]
    for chan in range(out_ref.shape[0]):
        state = jnp.concatenate([tall_s[chan], side_s[chan]], axis=1)
        out_ref[chan] = (0.5 * state + 0.125 * stencil_sum(state))[EDGE : EDGE + rows, :width]


def diffuse_kernel(sizes, x_ref, dtall_ref, dside_ref, out_ref, *scratch):
    rows_buf, cols_buf, colsend, tall_s, side_s, send_sem, recv_sem = scratch
    exchange(sizes, x_ref, rows_buf, cols_buf, colsend, tall_s, side_s, send_sem, recv_sem)
    rows, width = out_ref.shape[1], out_ref.shape[2]
    first = dtall_ref.shape[0] - out_ref.shape[0]
    for chan in range(out_ref.shape[0]):
        state = jnp.concatenate([tall_s[chan], side_s[chan]], axis=1)
        diff = jnp.concatenate([dtall_ref[first + chan], dside_ref[first + chan]], axis=1)
        for iteration in range(ITERS):
            state = state + diff * (stencil_sum(state) - 4.0 * state)
        out_ref[chan] = state[EDGE : EDGE + rows, :width]


def smooth_call(sizes, both, chans, rows_padded):
    total, rows, width = both.shape
    vmem = pl.BlockSpec(memory_space=pltpu.VMEM)
    return pl.pallas_call(
        functools.partial(smooth_kernel, sizes),
        out_shape=(
            jax.ShapeDtypeStruct((chans, rows, width), jnp.float32),
            jax.ShapeDtypeStruct((total, rows_padded, width), jnp.float32),
            jax.ShapeDtypeStruct((total, rows_padded, width), jnp.float32),
        ),
        in_specs=[vmem],
        out_specs=(vmem, vmem, vmem),
        scratch_shapes=exchange_scratch(total, rows_padded, width),
        compiler_params=pltpu.CompilerParams(collective_id=0, has_side_effects=True),
    )(both)


def diffuse_call(sizes, forced, dtall, dside):
    chans, rows, width = forced.shape
    rows_padded = dtall.shape[1]
    vmem = pl.BlockSpec(memory_space=pltpu.VMEM)
    return pl.pallas_call(
        functools.partial(diffuse_kernel, sizes),
        out_shape=jax.ShapeDtypeStruct((chans, rows, width), jnp.float32),
        in_specs=[vmem] * 3,
        out_specs=vmem,
        scratch_shapes=exchange_scratch(chans, rows_padded, width),
        compiler_params=pltpu.CompilerParams(collective_id=1, has_side_effects=True),
    )(forced, dtall, dside)


def per_device(
    atm_state,
    diffusivity,
    ocean_state,
    land_mask,
    intersection_area,
    intersection_seg,
    intersection_dest,
    intersection_row,
):
    atm_count = lax.axis_size("atm")
    ocn_count = lax.axis_size("ocn")
    devices = atm_count * ocn_count
    row_count, chan_count, seg_width = atm_state.shape
    seg_count = ocean_state.shape[0]
    ov_rows = intersection_seg.shape[0]
    capacity = max(2, 2 * ov_rows // devices)
    slots = devices * capacity

    target = intersection_dest[:, 0]
    matches = (target[:, None] == jnp.arange(devices, dtype=jnp.int32)[None, :]).astype(jnp.int32)
    position = jnp.sum((jnp.cumsum(matches, axis=0) - matches) * matches, axis=1)
    slot_index = target * capacity + position
    slot_pick = (
        jnp.arange(slots, dtype=jnp.int32)[:, None] == slot_index[None, :]
    ).astype(jnp.bfloat16)
    seg_pick = (
        intersection_seg[:, None] == jnp.arange(seg_count, dtype=jnp.int32)[None, :]
    ).astype(jnp.bfloat16)
    slot_seg = jnp.dot(slot_pick, seg_pick, preferred_element_type=jnp.float32)
    plane = chan_count * seg_width
    out_ocean = select_rows(slot_seg, ocean_state.reshape(seg_count, plane))
    out_mask = select_rows(slot_seg, land_mask.astype(jnp.float32), None)
    row_high = (intersection_row // 32).astype(jnp.bfloat16)
    row_low = (intersection_row % 32).astype(jnp.bfloat16)
    row_parts = jnp.concatenate(
        [jnp.broadcast_to(row_high[:, None], (ov_rows, seg_width)),
         jnp.broadcast_to(row_low[:, None], (ov_rows, seg_width))], axis=1
    )
    out_rows = jnp.dot(slot_pick, row_parts, preferred_element_type=jnp.float32)
    out_label = 32.0 * out_rows[:, :seg_width] + out_rows[:, seg_width:]
    out_area = select_rows(slot_pick.astype(jnp.float32), intersection_area)
    out_weight = out_area * out_mask
    outgoing = jnp.concatenate([out_ocean, out_weight, out_label], axis=1)
    incoming = lax.all_to_all(outgoing, ("atm", "ocn"), split_axis=0, concat_axis=0, tiled=True)

    atm_planes = jnp.transpose(atm_state, (1, 0, 2))
    both = jnp.concatenate([atm_planes, jnp.transpose(diffusivity, (1, 0, 2))], axis=0)
    sizes = (atm_count, ocn_count)
    rows_padded = -(-(row_count + 2 * EDGE) // 128) * 128
    smoothed, dtall, dside = smooth_call(sizes, both, chan_count, rows_padded)

    in_labels = jnp.max(incoming[:, plane + seg_width :], axis=1).astype(jnp.int32)
    row_pick = (
        jnp.arange(row_count, dtype=jnp.int32)[:, None] == in_labels[None, :]
    ).astype(jnp.float32)
    pick_rows = row_pick.T
    air = [jnp.dot(pick_rows, smoothed[c], precision=HIGHEST, preferred_element_type=jnp.float32)
           for c in range(chan_count)]
    ocean = [incoming[:, c * seg_width : (c + 1) * seg_width] for c in range(chan_count)]
    in_weight = incoming[:, plane : plane + seg_width]
    wind_east = air[1] - ocean[1]
    wind_north = air[2] - ocean[2]
    wind_speed = jnp.sqrt(wind_east * wind_east + wind_north * wind_north + 0.5)
    temp_gap = ocean[0] - air[0]
    factor = 1.0 + 0.5 * jnp.tanh(temp_gap / wind_speed)
    weighted = [
        in_weight * (0.8 * factor * wind_speed * temp_gap),
        in_weight * (0.6 * factor * wind_speed * wind_east),
        in_weight * (0.6 * factor * wind_speed * wind_north),
    ]
    returned = lax.all_to_all(
        jnp.concatenate(weighted, axis=1), ("atm", "ocn"), split_axis=0, concat_axis=0, tiled=True
    )
    ocean_flux = select_rows(slot_seg.T, returned).reshape(seg_count, chan_count, seg_width)
    signs = (1.0, -1.0, -1.0)
    forced = jnp.stack(
        [atm_planes[c] + signs[c] * jnp.dot(row_pick, weighted[c], precision=HIGHEST,
                                             preferred_element_type=jnp.float32)
         for c in range(chan_count)]
    )
    current = diffuse_call(sizes, forced, dtall, dside)
    return (jnp.transpose(current, (1, 0, 2)), ocean_flux)


def solution(mesh):
    placed = (
        P("atm", None, "ocn"),
        P("atm", None, "ocn"),
        P(("atm", "ocn"), None, None),
        P(("atm", "ocn"), None),
        P(("atm", "ocn"), None),
        P(("atm", "ocn")),
        P(("atm", "ocn"), None),
        P(("atm", "ocn")),
    )
    return jax.shard_map(
        per_device,
        mesh=mesh,
        in_specs=placed,
        out_specs=(P("atm", None, "ocn"), P(("atm", "ocn"), None, None)),
        check_vma=False,
    )
```

```python
import functools

import jax
import jax.numpy as jnp
from jax import lax
from jax.experimental import pallas as pl
from jax.experimental.pallas import tpu as pltpu
from jax.sharding import PartitionSpec as P

ITERS = 3
HIGHEST = lax.Precision.HIGHEST
HALO = ITERS
EDGE = 8


def with_halo(block, sides, width):
    for axis, dim in sides:
        count = lax.axis_size(axis)
        forward = [(i, i + 1) for i in range(count - 1)]
        backward = [(target, source) for source, target in forward]
        low = lax.ppermute(
            lax.slice_in_dim(block, block.shape[dim] - width, None, axis=dim), axis, forward
        )
        high = lax.ppermute(lax.slice_in_dim(block, 0, width, axis=dim), axis, backward)
        block = jnp.concatenate([low, block, high], axis=dim)
    return block


def beside_all(padded):
    return padded[2:, :, 1:-1] + padded[:-2, :, 1:-1] + padded[1:-1, :, 2:] + padded[1:-1, :, :-2]


def fluxes(ocean_part, air_part):
    wind_east = air_part[:, 1] - ocean_part[:, 1]
    wind_north = air_part[:, 2] - ocean_part[:, 2]
    wind_speed = jnp.sqrt(wind_east * wind_east + wind_north * wind_north + 0.5)
    temp_gap = ocean_part[:, 0] - air_part[:, 0]
    factor = 1.0 + 0.5 * jnp.tanh(temp_gap / wind_speed)
    return jnp.stack(
        [
            0.8 * factor * wind_speed * temp_gap,
            0.6 * factor * wind_speed * wind_east,
            0.6 * factor * wind_speed * wind_north,
        ],
        axis=1,
    )


def select_rows(chosen, values, precision=HIGHEST):
    flat = values.reshape(values.shape[0], -1)
    total = jnp.dot(chosen, flat, precision=precision, preferred_element_type=jnp.float32)
    return total.reshape((chosen.shape[0],) + values.shape[1:])


MESH = pl.DeviceIdType.MESH


def exchange(sizes, x_ref, rows_buf, cols_buf, colsend, tall_s, side_s, send_sem, recv_sem):
    atm_n, ocn_n = sizes
    chans, rows, width = x_ref.shape
    rows_padded = tall_s.shape[1]
    me_a = lax.axis_index("atm")
    me_o = lax.axis_index("ocn")
    up = lax.rem(me_a + atm_n - 1, atm_n)
    down = lax.rem(me_a + 1, atm_n)
    left = lax.rem(me_o + ocn_n - 1, ocn_n)
    right = lax.rem(me_o + 1, ocn_n)
    barrier = pltpu.get_barrier_semaphore()
    for peer in ((up, me_o), (down, me_o), (me_a, left), (me_a, right)):
        pl.semaphore_signal(barrier, 1, device_id=peer, device_id_type=MESH)
    pl.semaphore_wait(barrier, 4)

    to_down = pltpu.make_async_remote_copy(
        x_ref.at[:, rows - EDGE :, :], rows_buf.at[0], send_sem.at[0], recv_sem.at[0],
        device_id=(down, me_o), device_id_type=MESH)
    to_up = pltpu.make_async_remote_copy(
        x_ref.at[:, :EDGE, :], rows_buf.at[1], send_sem.at[1], recv_sem.at[1],
        device_id=(up, me_o), device_id_type=MESH)
    to_down.start()
    to_up.start()
    to_down.wait()
    to_up.wait()

    has_up = me_a > 0
    has_down = me_a < atm_n - 1
    has_left = me_o > 0
    has_right = me_o < ocn_n - 1
    spare = jnp.zeros((rows_padded - rows - 2 * EDGE, width), jnp.float32)
    for c in range(chans):
        top = jnp.where(has_up, rows_buf[0, c], 0.0)
        bottom = jnp.where(has_down, rows_buf[1, c], 0.0)
        tall = jnp.concatenate([top, x_ref[c], bottom, spare], axis=0)
        tall_s[c] = tall
        flipped = tall.T
        colsend[0, c] = flipped[:EDGE]
        colsend[1, c] = flipped[width - EDGE :]

    to_left = pltpu.make_async_remote_copy(
        colsend.at[0], cols_buf.at[1], send_sem.at[2], recv_sem.at[2],
        device_id=(me_a, left), device_id_type=MESH)
    to_right = pltpu.make_async_remote_copy(
        colsend.at[1], cols_buf.at[0], send_sem.at[3], recv_sem.at[3],
        device_id=(me_a, right), device_id_type=MESH)
    to_left.start()
    to_right.start()
    to_left.wait()
    to_right.wait()

    middle = jnp.zeros((width - 2 * EDGE, rows_padded), jnp.float32)
    for c in range(chans):
        from_left = jnp.where(has_left, cols_buf[0, c], 0.0)
        from_right = jnp.where(has_right, cols_buf[1, c], 0.0)
        side_s[c] = jnp.concatenate([from_right, middle, from_left], axis=0).T


def exchange_scratch(chans, rows_padded, width):
    return [
        pltpu.VMEM((2, chans, EDGE, width), jnp.float32),
        pltpu.VMEM((2, chans, EDGE, rows_padded), jnp.float32),
        pltpu.VMEM((2, chans, EDGE, rows_padded), jnp.float32),
        pltpu.VMEM((chans, rows_padded, width), jnp.float32),
        pltpu.VMEM((chans, rows_padded, width), jnp.float32),
        pltpu.SemaphoreType.DMA((4,)),
        pltpu.SemaphoreType.DMA((4,)),
    ]


def stencil_sum(state):
    rows_padded, lanes = state.shape
    return (
        pltpu.roll(state, rows_padded - 1, 0)
        + pltpu.roll(state, 1, 0)
        + pltpu.roll(state, lanes - 1, 1)
        + pltpu.roll(state, 1, 1)
    )


def smooth_kernel(sizes, x_ref, out_ref, tall_out, side_out, *scratch):
    rows_buf, cols_buf, colsend, tall_s, side_s, send_sem, recv_sem = scratch
    exchange(sizes, x_ref, rows_buf, cols_buf, colsend, tall_s, side_s, send_sem, recv_sem)
    rows, width = out_ref.shape[1], out_ref.shape[2]
    tall_out[...] = tall_s[...]
    side_out[...] = side_s[...]
    for chan in range(out_ref.shape[0]):
        state = jnp.concatenate([tall_s[chan], side_s[chan]], axis=1)
        out_ref[chan] = (0.5 * state + 0.125 * stencil_sum(state))[EDGE : EDGE + rows, :width]


def diffuse_kernel(sizes, x_ref, dtall_ref, dside_ref, out_ref, *scratch):
    rows_buf, cols_buf, colsend, tall_s, side_s, send_sem, recv_sem = scratch
    exchange(sizes, x_ref, rows_buf, cols_buf, colsend, tall_s, side_s, send_sem, recv_sem)
    rows, width = out_ref.shape[1], out_ref.shape[2]
    first = dtall_ref.shape[0] - out_ref.shape[0]
    for chan in range(out_ref.shape[0]):
        state = jnp.concatenate([tall_s[chan], side_s[chan]], axis=1)
        diff = jnp.concatenate([dtall_ref[first + chan], dside_ref[first + chan]], axis=1)
        for iteration in range(ITERS):
            state = state + diff * (stencil_sum(state) - 4.0 * state)
        out_ref[chan] = state[EDGE : EDGE + rows, :width]


def smooth_call(sizes, both, chans, rows_padded):
    total, rows, width = both.shape
    vmem = pl.BlockSpec(memory_space=pltpu.VMEM)
    return pl.pallas_call(
        functools.partial(smooth_kernel, sizes),
        out_shape=(
            jax.ShapeDtypeStruct((chans, rows, width), jnp.float32),
            jax.ShapeDtypeStruct((total, rows_padded, width), jnp.float32),
            jax.ShapeDtypeStruct((total, rows_padded, width), jnp.float32),
        ),
        in_specs=[vmem],
        out_specs=(vmem, vmem, vmem),
        scratch_shapes=exchange_scratch(total, rows_padded, width),
        compiler_params=pltpu.CompilerParams(collective_id=0, has_side_effects=True),
    )(both)


def diffuse_call(sizes, forced, dtall, dside):
    chans, rows, width = forced.shape
    rows_padded = dtall.shape[1]
    vmem = pl.BlockSpec(memory_space=pltpu.VMEM)
    return pl.pallas_call(
        functools.partial(diffuse_kernel, sizes),
        out_shape=jax.ShapeDtypeStruct((chans, rows, width), jnp.float32),
        in_specs=[vmem] * 3,
        out_specs=vmem,
        scratch_shapes=exchange_scratch(chans, rows_padded, width),
        compiler_params=pltpu.CompilerParams(collective_id=1, has_side_effects=True),
    )(forced, dtall, dside)


def per_device(
    atm_state,
    diffusivity,
    ocean_state,
    land_mask,
    intersection_area,
    intersection_seg,
    intersection_dest,
    intersection_row,
):
    atm_count = lax.axis_size("atm")
    ocn_count = lax.axis_size("ocn")
    devices = atm_count * ocn_count
    row_count, chan_count, seg_width = atm_state.shape
    seg_count = ocean_state.shape[0]
    ov_rows = intersection_seg.shape[0]
    capacity = max(2, 2 * ov_rows // devices)
    slots = devices * capacity

    target = intersection_dest[:, 0]
    matches = (target[:, None] == jnp.arange(devices, dtype=jnp.int32)[None, :]).astype(jnp.int32)
    position = jnp.sum((jnp.cumsum(matches, axis=0) - matches) * matches, axis=1)
    slot_index = target * capacity + position
    slot_pick = (
        jnp.arange(slots, dtype=jnp.int32)[:, None] == slot_index[None, :]
    ).astype(jnp.bfloat16)
    seg_pick = (
        intersection_seg[:, None] == jnp.arange(seg_count, dtype=jnp.int32)[None, :]
    ).astype(jnp.bfloat16)
    slot_seg = jnp.dot(slot_pick, seg_pick, preferred_element_type=jnp.float32)
    plane = chan_count * seg_width
    out_ocean = select_rows(slot_seg, ocean_state.reshape(seg_count, plane))
    out_mask = select_rows(slot_seg, land_mask.astype(jnp.float32), None)
    row_high = (intersection_row // 32).astype(jnp.bfloat16)
    row_low = (intersection_row % 32).astype(jnp.bfloat16)
    row_parts = jnp.concatenate(
        [jnp.broadcast_to(row_high[:, None], (ov_rows, seg_width)),
         jnp.broadcast_to(row_low[:, None], (ov_rows, seg_width))], axis=1
    )
    out_rows = jnp.dot(slot_pick, row_parts, preferred_element_type=jnp.float32)
    out_label = 32.0 * out_rows[:, :seg_width] + out_rows[:, seg_width:]
    out_area = select_rows(slot_pick.astype(jnp.float32), intersection_area)
    out_weight = out_area * out_mask
    outgoing = jnp.concatenate([out_ocean, out_weight, out_label], axis=1)

    atm_planes = jnp.transpose(atm_state, (1, 0, 2))
    both = jnp.concatenate([atm_planes, jnp.transpose(diffusivity, (1, 0, 2))], axis=0)
    sizes = (atm_count, ocn_count)
    rows_padded = -(-(row_count + 2 * EDGE) // 128) * 128
    smoothed, dtall, dside = smooth_call(sizes, both, chan_count, rows_padded)
    outgoing, smoothed = lax.optimization_barrier((outgoing, smoothed))
    incoming = lax.all_to_all(outgoing, ("atm", "ocn"), split_axis=0, concat_axis=0, tiled=True)

    in_labels = jnp.max(incoming[:, plane + seg_width :], axis=1).astype(jnp.int32)
    row_pick = (
        jnp.arange(row_count, dtype=jnp.int32)[:, None] == in_labels[None, :]
    ).astype(jnp.float32)
    pick_rows = row_pick.T
    air = [jnp.dot(pick_rows, smoothed[c], precision=HIGHEST, preferred_element_type=jnp.float32)
           for c in range(chan_count)]
    ocean = [incoming[:, c * seg_width : (c + 1) * seg_width] for c in range(chan_count)]
    in_weight = incoming[:, plane : plane + seg_width]
    wind_east = air[1] - ocean[1]
    wind_north = air[2] - ocean[2]
    wind_speed = jnp.sqrt(wind_east * wind_east + wind_north * wind_north + 0.5)
    temp_gap = ocean[0] - air[0]
    factor = 1.0 + 0.5 * jnp.tanh(temp_gap / wind_speed)
    weighted = [
        in_weight * (0.8 * factor * wind_speed * temp_gap),
        in_weight * (0.6 * factor * wind_speed * wind_east),
        in_weight * (0.6 * factor * wind_speed * wind_north),
    ]
    returned = lax.all_to_all(
        jnp.concatenate(weighted, axis=1), ("atm", "ocn"), split_axis=0, concat_axis=0, tiled=True
    )
    ocean_flux = select_rows(slot_seg.T, returned).reshape(seg_count, chan_count, seg_width)
    signs = (1.0, -1.0, -1.0)
    forced = jnp.stack(
        [atm_planes[c] + signs[c] * jnp.dot(row_pick, weighted[c], precision=HIGHEST,
                                             preferred_element_type=jnp.float32)
         for c in range(chan_count)]
    )
    current = diffuse_call(sizes, forced, dtall, dside)
    return (jnp.transpose(current, (1, 0, 2)), ocean_flux)


def solution(mesh):
    placed = (
        P("atm", None, "ocn"),
        P("atm", None, "ocn"),
        P(("atm", "ocn"), None, None),
        P(("atm", "ocn"), None),
        P(("atm", "ocn"), None),
        P(("atm", "ocn")),
        P(("atm", "ocn"), None),
        P(("atm", "ocn")),
    )
    return jax.shard_map(
        per_device,
        mesh=mesh,
        in_specs=placed,
        out_specs=(P("atm", None, "ocn"), P(("atm", "ocn"), None, None)),
        check_vma=False,
    )
```

```python
import functools

import jax
import jax.numpy as jnp
from jax import lax
from jax.experimental import pallas as pl
from jax.experimental.pallas import tpu as pltpu
from jax.sharding import PartitionSpec as P

ITERS = 3
HIGHEST = lax.Precision.HIGHEST
HALO = ITERS
EDGE = 8


def with_halo(block, sides, width):
    for axis, dim in sides:
        count = lax.axis_size(axis)
        forward = [(i, i + 1) for i in range(count - 1)]
        backward = [(target, source) for source, target in forward]
        low = lax.ppermute(
            lax.slice_in_dim(block, block.shape[dim] - width, None, axis=dim), axis, forward
        )
        high = lax.ppermute(lax.slice_in_dim(block, 0, width, axis=dim), axis, backward)
        block = jnp.concatenate([low, block, high], axis=dim)
    return block


def beside_all(padded):
    return padded[2:, :, 1:-1] + padded[:-2, :, 1:-1] + padded[1:-1, :, 2:] + padded[1:-1, :, :-2]


def fluxes(ocean_part, air_part):
    wind_east = air_part[:, 1] - ocean_part[:, 1]
    wind_north = air_part[:, 2] - ocean_part[:, 2]
    wind_speed = jnp.sqrt(wind_east * wind_east + wind_north * wind_north + 0.5)
    temp_gap = ocean_part[:, 0] - air_part[:, 0]
    factor = 1.0 + 0.5 * jnp.tanh(temp_gap / wind_speed)
    return jnp.stack(
        [
            0.8 * factor * wind_speed * temp_gap,
            0.6 * factor * wind_speed * wind_east,
            0.6 * factor * wind_speed * wind_north,
        ],
        axis=1,
    )


def select_rows(chosen, values, precision=HIGHEST):
    flat = values.reshape(values.shape[0], -1)
    total = jnp.dot(chosen, flat, precision=precision, preferred_element_type=jnp.float32)
    return total.reshape((chosen.shape[0],) + values.shape[1:])


MESH = pl.DeviceIdType.MESH


def exchange(sizes, x_ref, rows_buf, cols_buf, colsend, tall_s, side_s, send_sem, recv_sem):
    atm_n, ocn_n = sizes
    chans, rows, width = x_ref.shape
    rows_padded = tall_s.shape[1]
    me_a = lax.axis_index("atm")
    me_o = lax.axis_index("ocn")
    up = lax.rem(me_a + atm_n - 1, atm_n)
    down = lax.rem(me_a + 1, atm_n)
    left = lax.rem(me_o + ocn_n - 1, ocn_n)
    right = lax.rem(me_o + 1, ocn_n)
    peers = ((up, me_o), (down, me_o), (me_a, left), (me_a, right),
             (up, left), (up, right), (down, left), (down, right))
    barrier = pltpu.get_barrier_semaphore()
    for peer in peers:
        pl.semaphore_signal(barrier, 1, device_id=peer, device_id_type=MESH)
    pl.semaphore_wait(barrier, len(peers))

    spare = jnp.zeros((rows_padded - rows, width), jnp.float32)
    for c in range(chans):
        flipped = jnp.concatenate([x_ref[c], spare], axis=0).T
        colsend[0, c] = flipped[:EDGE]
        colsend[1, c] = flipped[width - EDGE :]

    last = x_ref.at[:, rows - EDGE :, :]
    first = x_ref.at[:, :EDGE, :]
    plan = (
        (last, rows_buf.at[0], (down, me_o)),
        (first, rows_buf.at[1], (up, me_o)),
        (last, rows_buf.at[2], (down, right)),
        (last, rows_buf.at[3], (down, left)),
        (first, rows_buf.at[4], (up, right)),
        (first, rows_buf.at[5], (up, left)),
        (colsend.at[0], cols_buf.at[1], (me_a, left)),
        (colsend.at[1], cols_buf.at[0], (me_a, right)),
    )
    copies = []
    for k, (src, dst, peer) in enumerate(plan):
        copy = pltpu.make_async_remote_copy(
            src, dst, send_sem.at[k], recv_sem.at[k], device_id=peer, device_id_type=MESH)
        copy.start()
        copies.append(copy)
    for copy in copies:
        copy.wait()

    has_up = me_a > 0
    has_down = me_a < atm_n - 1
    has_left = me_o > 0
    has_right = me_o < ocn_n - 1
    lane = lax.broadcasted_iota(jnp.int32, (EDGE, width), 1)
    low_lanes = lane < EDGE
    high_lanes = lane >= width - EDGE
    tail = jnp.zeros((rows_padded - rows - 2 * EDGE, width), jnp.float32)
    middle = jnp.zeros((width - 2 * EDGE, rows_padded), jnp.float32)
    for c in range(chans):
        top = jnp.where(has_up, rows_buf[0, c], 0.0)
        bottom = jnp.where(has_down, rows_buf[1, c], 0.0)
        tall_s[c] = jnp.concatenate([top, x_ref[c], bottom, tail], axis=0)
        from_left = jnp.where(has_left, cols_buf[0, c], 0.0)
        from_right = jnp.where(has_right, cols_buf[1, c], 0.0)
        own = jnp.concatenate([from_right, middle, from_left], axis=0).T
        corner_top = jnp.where(
            low_lanes & (has_up & has_right), rows_buf[3, c],
            jnp.where(high_lanes & (has_up & has_left), rows_buf[2, c], 0.0))
        corner_bottom = jnp.where(
            low_lanes & (has_down & has_right), rows_buf[5, c],
            jnp.where(high_lanes & (has_down & has_left), rows_buf[4, c], 0.0))
        side_s[c] = jnp.concatenate([corner_top, own[:rows], corner_bottom, tail], axis=0)


def exchange_scratch(chans, rows_padded, width):
    return [
        pltpu.VMEM((6, chans, EDGE, width), jnp.float32),
        pltpu.VMEM((2, chans, EDGE, rows_padded), jnp.float32),
        pltpu.VMEM((2, chans, EDGE, rows_padded), jnp.float32),
        pltpu.VMEM((chans, rows_padded, width), jnp.float32),
        pltpu.VMEM((chans, rows_padded, width), jnp.float32),
        pltpu.SemaphoreType.DMA((8,)),
        pltpu.SemaphoreType.DMA((8,)),
    ]


def stencil_sum(state):
    rows_padded, lanes = state.shape
    return (
        pltpu.roll(state, rows_padded - 1, 0)
        + pltpu.roll(state, 1, 0)
        + pltpu.roll(state, lanes - 1, 1)
        + pltpu.roll(state, 1, 1)
    )


def smooth_kernel(sizes, x_ref, out_ref, tall_out, side_out, *scratch):
    rows_buf, cols_buf, colsend, tall_s, side_s, send_sem, recv_sem = scratch
    exchange(sizes, x_ref, rows_buf, cols_buf, colsend, tall_s, side_s, send_sem, recv_sem)
    rows, width = out_ref.shape[1], out_ref.shape[2]
    kept = tall_out.shape[0]
    tall_out[...] = tall_s[kept:]
    side_out[...] = side_s[kept:]
    for chan in range(out_ref.shape[0]):
        state = jnp.concatenate([tall_s[chan], side_s[chan]], axis=1)
        out_ref[chan] = (0.5 * state + 0.125 * stencil_sum(state))[EDGE : EDGE + rows, :width]


def diffuse_kernel(sizes, x_ref, dtall_ref, dside_ref, out_ref, *scratch):
    rows_buf, cols_buf, colsend, tall_s, side_s, send_sem, recv_sem = scratch
    exchange(sizes, x_ref, rows_buf, cols_buf, colsend, tall_s, side_s, send_sem, recv_sem)
    rows, width = out_ref.shape[1], out_ref.shape[2]
    first = dtall_ref.shape[0] - out_ref.shape[0]
    for chan in range(out_ref.shape[0]):
        state = jnp.concatenate([tall_s[chan], side_s[chan]], axis=1)
        diff = jnp.concatenate([dtall_ref[first + chan], dside_ref[first + chan]], axis=1)
        for iteration in range(ITERS):
            state = state + diff * (stencil_sum(state) - 4.0 * state)
        out_ref[chan] = state[EDGE : EDGE + rows, :width]


def smooth_call(sizes, both, chans, rows_padded):
    total, rows, width = both.shape
    vmem = pl.BlockSpec(memory_space=pltpu.VMEM)
    return pl.pallas_call(
        functools.partial(smooth_kernel, sizes),
        out_shape=(
            jax.ShapeDtypeStruct((chans, rows, width), jnp.float32),
            jax.ShapeDtypeStruct((total - chans, rows_padded, width), jnp.float32),
            jax.ShapeDtypeStruct((total - chans, rows_padded, width), jnp.float32),
        ),
        in_specs=[vmem],
        out_specs=(vmem, vmem, vmem),
        scratch_shapes=exchange_scratch(total, rows_padded, width),
        compiler_params=pltpu.CompilerParams(collective_id=0, has_side_effects=True),
    )(both)


def diffuse_call(sizes, forced, dtall, dside):
    chans, rows, width = forced.shape
    rows_padded = dtall.shape[1]
    vmem = pl.BlockSpec(memory_space=pltpu.VMEM)
    return pl.pallas_call(
        functools.partial(diffuse_kernel, sizes),
        out_shape=jax.ShapeDtypeStruct((chans, rows, width), jnp.float32),
        in_specs=[vmem] * 3,
        out_specs=vmem,
        scratch_shapes=exchange_scratch(chans, rows_padded, width),
        compiler_params=pltpu.CompilerParams(collective_id=1, has_side_effects=True),
    )(forced, dtall, dside)


def per_device(
    atm_state,
    diffusivity,
    ocean_state,
    land_mask,
    intersection_area,
    intersection_seg,
    intersection_dest,
    intersection_row,
):
    atm_count = lax.axis_size("atm")
    ocn_count = lax.axis_size("ocn")
    devices = atm_count * ocn_count
    row_count, chan_count, seg_width = atm_state.shape
    seg_count = ocean_state.shape[0]
    ov_rows = intersection_seg.shape[0]
    capacity = max(2, 2 * ov_rows // devices)
    slots = devices * capacity

    target = intersection_dest[:, 0]
    matches = (target[:, None] == jnp.arange(devices, dtype=jnp.int32)[None, :]).astype(jnp.int32)
    position = jnp.sum((jnp.cumsum(matches, axis=0) - matches) * matches, axis=1)
    slot_index = target * capacity + position
    slot_pick = (
        jnp.arange(slots, dtype=jnp.int32)[:, None] == slot_index[None, :]
    ).astype(jnp.bfloat16)
    seg_pick = (
        intersection_seg[:, None] == jnp.arange(seg_count, dtype=jnp.int32)[None, :]
    ).astype(jnp.bfloat16)
    slot_seg = jnp.dot(slot_pick, seg_pick, preferred_element_type=jnp.float32)
    plane = chan_count * seg_width
    out_ocean = select_rows(slot_seg, ocean_state.reshape(seg_count, plane))
    out_mask = select_rows(slot_seg, land_mask.astype(jnp.float32), None)
    row_high = (intersection_row // 32).astype(jnp.bfloat16)
    row_low = (intersection_row % 32).astype(jnp.bfloat16)
    row_parts = jnp.concatenate(
        [jnp.broadcast_to(row_high[:, None], (ov_rows, seg_width)),
         jnp.broadcast_to(row_low[:, None], (ov_rows, seg_width))], axis=1
    )
    out_rows = jnp.dot(slot_pick, row_parts, preferred_element_type=jnp.float32)
    out_label = 32.0 * out_rows[:, :seg_width] + out_rows[:, seg_width:]
    out_area = select_rows(slot_pick.astype(jnp.float32), intersection_area)
    out_weight = out_area * out_mask
    outgoing = jnp.concatenate([out_ocean, out_weight, out_label], axis=1)
    incoming = lax.all_to_all(outgoing, ("atm", "ocn"), split_axis=0, concat_axis=0, tiled=True)

    atm_planes = jnp.transpose(atm_state, (1, 0, 2))
    both = jnp.concatenate([atm_planes, jnp.transpose(diffusivity, (1, 0, 2))], axis=0)
    sizes = (atm_count, ocn_count)
    rows_padded = -(-(row_count + 2 * EDGE) // 128) * 128
    smoothed, dtall, dside = smooth_call(sizes, both, chan_count, rows_padded)

    in_labels = jnp.max(incoming[:, plane + seg_width :], axis=1).astype(jnp.int32)
    row_pick = (
        jnp.arange(row_count, dtype=jnp.int32)[:, None] == in_labels[None, :]
    ).astype(jnp.float32)
    pick_rows = row_pick.T
    air = [jnp.dot(pick_rows, smoothed[c], precision=HIGHEST, preferred_element_type=jnp.float32)
           for c in range(chan_count)]
    ocean = [incoming[:, c * seg_width : (c + 1) * seg_width] for c in range(chan_count)]
    in_weight = incoming[:, plane : plane + seg_width]
    wind_east = air[1] - ocean[1]
    wind_north = air[2] - ocean[2]
    wind_speed = jnp.sqrt(wind_east * wind_east + wind_north * wind_north + 0.5)
    temp_gap = ocean[0] - air[0]
    factor = 1.0 + 0.5 * jnp.tanh(temp_gap / wind_speed)
    weighted = [
        in_weight * (0.8 * factor * wind_speed * temp_gap),
        in_weight * (0.6 * factor * wind_speed * wind_east),
        in_weight * (0.6 * factor * wind_speed * wind_north),
    ]
    returned = lax.all_to_all(
        jnp.concatenate(weighted, axis=1), ("atm", "ocn"), split_axis=0, concat_axis=0, tiled=True
    )
    ocean_flux = select_rows(slot_seg.T, returned).reshape(seg_count, chan_count, seg_width)
    signs = (1.0, -1.0, -1.0)
    forced = jnp.stack(
        [atm_planes[c] + signs[c] * jnp.dot(row_pick, weighted[c], precision=HIGHEST,
                                             preferred_element_type=jnp.float32)
         for c in range(chan_count)]
    )
    current = diffuse_call(sizes, forced, dtall, dside)
    return (jnp.transpose(current, (1, 0, 2)), ocean_flux)


def solution(mesh):
    placed = (
        P("atm", None, "ocn"),
        P("atm", None, "ocn"),
        P(("atm", "ocn"), None, None),
        P(("atm", "ocn"), None),
        P(("atm", "ocn"), None),
        P(("atm", "ocn")),
        P(("atm", "ocn"), None),
        P(("atm", "ocn")),
    )
    return jax.shard_map(
        per_device,
        mesh=mesh,
        in_specs=placed,
        out_specs=(P("atm", None, "ocn"), P(("atm", "ocn"), None, None)),
        check_vma=False,
    )
```

```python
import functools

import jax
import jax.numpy as jnp
from jax import lax
from jax.experimental import pallas as pl
from jax.experimental.pallas import tpu as pltpu
from jax.sharding import PartitionSpec as P

ITERS = 3
HIGHEST = lax.Precision.HIGHEST
HALO = ITERS
EDGE = 8


def with_halo(block, sides, width):
    for axis, dim in sides:
        count = lax.axis_size(axis)
        forward = [(i, i + 1) for i in range(count - 1)]
        backward = [(target, source) for source, target in forward]
        low = lax.ppermute(
            lax.slice_in_dim(block, block.shape[dim] - width, None, axis=dim), axis, forward
        )
        high = lax.ppermute(lax.slice_in_dim(block, 0, width, axis=dim), axis, backward)
        block = jnp.concatenate([low, block, high], axis=dim)
    return block


def beside_all(padded):
    return padded[2:, :, 1:-1] + padded[:-2, :, 1:-1] + padded[1:-1, :, 2:] + padded[1:-1, :, :-2]


def fluxes(ocean_part, air_part):
    wind_east = air_part[:, 1] - ocean_part[:, 1]
    wind_north = air_part[:, 2] - ocean_part[:, 2]
    wind_speed = jnp.sqrt(wind_east * wind_east + wind_north * wind_north + 0.5)
    temp_gap = ocean_part[:, 0] - air_part[:, 0]
    factor = 1.0 + 0.5 * jnp.tanh(temp_gap / wind_speed)
    return jnp.stack(
        [
            0.8 * factor * wind_speed * temp_gap,
            0.6 * factor * wind_speed * wind_east,
            0.6 * factor * wind_speed * wind_north,
        ],
        axis=1,
    )


def pick_dot(pick, values):
    parts = []
    rest = values
    for part in range(3):
        high = lax.reduce_precision(rest, exponent_bits=8, mantissa_bits=7)
        parts.append(high.astype(jnp.bfloat16))
        rest = rest - high
    total = None
    for part in parts:
        term = jnp.dot(pick, part, preferred_element_type=jnp.float32)
        total = term if total is None else total + term
    return total


def select_rows(chosen, values, precision=HIGHEST):
    flat = values.reshape(values.shape[0], -1)
    total = jnp.dot(chosen, flat, precision=precision, preferred_element_type=jnp.float32)
    return total.reshape((chosen.shape[0],) + values.shape[1:])


MESH = pl.DeviceIdType.MESH


def exchange(sizes, x_ref, rows_buf, cols_buf, colsend, tall_s, side_s, send_sem, recv_sem):
    atm_n, ocn_n = sizes
    chans, rows, width = x_ref.shape
    rows_padded = tall_s.shape[1]
    me_a = lax.axis_index("atm")
    me_o = lax.axis_index("ocn")
    up = lax.rem(me_a + atm_n - 1, atm_n)
    down = lax.rem(me_a + 1, atm_n)
    left = lax.rem(me_o + ocn_n - 1, ocn_n)
    right = lax.rem(me_o + 1, ocn_n)
    peers = ((up, me_o), (down, me_o), (me_a, left), (me_a, right),
             (up, left), (up, right), (down, left), (down, right))
    barrier = pltpu.get_barrier_semaphore()
    for peer in peers:
        pl.semaphore_signal(barrier, 1, device_id=peer, device_id_type=MESH)
    pl.semaphore_wait(barrier, len(peers))

    spare = jnp.zeros((rows_padded - rows, width), jnp.float32)
    for c in range(chans):
        flipped = jnp.concatenate([x_ref[c], spare], axis=0).T
        colsend[0, c] = flipped[:EDGE]
        colsend[1, c] = flipped[width - EDGE :]

    last = x_ref.at[:, rows - EDGE :, :]
    first = x_ref.at[:, :EDGE, :]
    plan = (
        (last, rows_buf.at[0], (down, me_o)),
        (first, rows_buf.at[1], (up, me_o)),
        (last, rows_buf.at[2], (down, right)),
        (last, rows_buf.at[3], (down, left)),
        (first, rows_buf.at[4], (up, right)),
        (first, rows_buf.at[5], (up, left)),
        (colsend.at[0], cols_buf.at[1], (me_a, left)),
        (colsend.at[1], cols_buf.at[0], (me_a, right)),
    )
    copies = []
    for k, (src, dst, peer) in enumerate(plan):
        copy = pltpu.make_async_remote_copy(
            src, dst, send_sem.at[k], recv_sem.at[k], device_id=peer, device_id_type=MESH)
        copy.start()
        copies.append(copy)
    for copy in copies:
        copy.wait()

    has_up = me_a > 0
    has_down = me_a < atm_n - 1
    has_left = me_o > 0
    has_right = me_o < ocn_n - 1
    lane = lax.broadcasted_iota(jnp.int32, (EDGE, width), 1)
    low_lanes = lane < EDGE
    high_lanes = lane >= width - EDGE
    tail = jnp.zeros((rows_padded - rows - 2 * EDGE, width), jnp.float32)
    middle = jnp.zeros((width - 2 * EDGE, rows_padded), jnp.float32)
    for c in range(chans):
        top = jnp.where(has_up, rows_buf[0, c], 0.0)
        bottom = jnp.where(has_down, rows_buf[1, c], 0.0)
        tall_s[c] = jnp.concatenate([top, x_ref[c], bottom, tail], axis=0)
        from_left = jnp.where(has_left, cols_buf[0, c], 0.0)
        from_right = jnp.where(has_right, cols_buf[1, c], 0.0)
        own = jnp.concatenate([from_right, middle, from_left], axis=0).T
        corner_top = jnp.where(
            low_lanes & (has_up & has_right), rows_buf[3, c],
            jnp.where(high_lanes & (has_up & has_left), rows_buf[2, c], 0.0))
        corner_bottom = jnp.where(
            low_lanes & (has_down & has_right), rows_buf[5, c],
            jnp.where(high_lanes & (has_down & has_left), rows_buf[4, c], 0.0))
        side_s[c] = jnp.concatenate([corner_top, own[:rows], corner_bottom, tail], axis=0)


def exchange_scratch(chans, rows_padded, width):
    return [
        pltpu.VMEM((6, chans, EDGE, width), jnp.float32),
        pltpu.VMEM((2, chans, EDGE, rows_padded), jnp.float32),
        pltpu.VMEM((2, chans, EDGE, rows_padded), jnp.float32),
        pltpu.VMEM((chans, rows_padded, width), jnp.float32),
        pltpu.VMEM((chans, rows_padded, width), jnp.float32),
        pltpu.SemaphoreType.DMA((8,)),
        pltpu.SemaphoreType.DMA((8,)),
    ]


def stencil_sum(state):
    rows_padded, lanes = state.shape
    return (
        pltpu.roll(state, rows_padded - 1, 0)
        + pltpu.roll(state, 1, 0)
        + pltpu.roll(state, lanes - 1, 1)
        + pltpu.roll(state, 1, 1)
    )


def smooth_kernel(sizes, x_ref, out_ref, tall_out, side_out, *scratch):
    rows_buf, cols_buf, colsend, tall_s, side_s, send_sem, recv_sem = scratch
    exchange(sizes, x_ref, rows_buf, cols_buf, colsend, tall_s, side_s, send_sem, recv_sem)
    rows, width = out_ref.shape[1], out_ref.shape[2]
    kept = tall_out.shape[0]
    tall_out[...] = tall_s[kept:]
    side_out[...] = side_s[kept:]
    for chan in range(out_ref.shape[0]):
        state = jnp.concatenate([tall_s[chan], side_s[chan]], axis=1)
        out_ref[chan] = (0.5 * state + 0.125 * stencil_sum(state))[EDGE : EDGE + rows, :width]


def diffuse_kernel(sizes, x_ref, dtall_ref, dside_ref, out_ref, *scratch):
    rows_buf, cols_buf, colsend, tall_s, side_s, send_sem, recv_sem = scratch
    exchange(sizes, x_ref, rows_buf, cols_buf, colsend, tall_s, side_s, send_sem, recv_sem)
    rows, width = out_ref.shape[1], out_ref.shape[2]
    first = dtall_ref.shape[0] - out_ref.shape[0]
    for chan in range(out_ref.shape[0]):
        state = jnp.concatenate([tall_s[chan], side_s[chan]], axis=1)
        diff = jnp.concatenate([dtall_ref[first + chan], dside_ref[first + chan]], axis=1)
        for iteration in range(ITERS):
            state = state + diff * (stencil_sum(state) - 4.0 * state)
        out_ref[chan] = state[EDGE : EDGE + rows, :width]


def smooth_call(sizes, both, chans, rows_padded):
    total, rows, width = both.shape
    vmem = pl.BlockSpec(memory_space=pltpu.VMEM)
    return pl.pallas_call(
        functools.partial(smooth_kernel, sizes),
        out_shape=(
            jax.ShapeDtypeStruct((chans, rows, width), jnp.float32),
            jax.ShapeDtypeStruct((total - chans, rows_padded, width), jnp.float32),
            jax.ShapeDtypeStruct((total - chans, rows_padded, width), jnp.float32),
        ),
        in_specs=[vmem],
        out_specs=(vmem, vmem, vmem),
        scratch_shapes=exchange_scratch(total, rows_padded, width),
        compiler_params=pltpu.CompilerParams(collective_id=0, has_side_effects=True),
    )(both)


def diffuse_call(sizes, forced, dtall, dside):
    chans, rows, width = forced.shape
    rows_padded = dtall.shape[1]
    vmem = pl.BlockSpec(memory_space=pltpu.VMEM)
    return pl.pallas_call(
        functools.partial(diffuse_kernel, sizes),
        out_shape=jax.ShapeDtypeStruct((chans, rows, width), jnp.float32),
        in_specs=[vmem] * 3,
        out_specs=vmem,
        scratch_shapes=exchange_scratch(chans, rows_padded, width),
        compiler_params=pltpu.CompilerParams(collective_id=1, has_side_effects=True),
    )(forced, dtall, dside)


def per_device(
    atm_state,
    diffusivity,
    ocean_state,
    land_mask,
    intersection_area,
    intersection_seg,
    intersection_dest,
    intersection_row,
):
    atm_count = lax.axis_size("atm")
    ocn_count = lax.axis_size("ocn")
    devices = atm_count * ocn_count
    row_count, chan_count, seg_width = atm_state.shape
    seg_count = ocean_state.shape[0]
    ov_rows = intersection_seg.shape[0]
    capacity = max(2, 2 * ov_rows // devices)
    slots = devices * capacity

    target = intersection_dest[:, 0]
    matches = (target[:, None] == jnp.arange(devices, dtype=jnp.int32)[None, :]).astype(jnp.int32)
    position = jnp.sum((jnp.cumsum(matches, axis=0) - matches) * matches, axis=1)
    slot_index = target * capacity + position
    slot_pick = (
        jnp.arange(slots, dtype=jnp.int32)[:, None] == slot_index[None, :]
    ).astype(jnp.bfloat16)
    seg_pick = (
        intersection_seg[:, None] == jnp.arange(seg_count, dtype=jnp.int32)[None, :]
    ).astype(jnp.bfloat16)
    slot_seg = jnp.dot(slot_pick, seg_pick, preferred_element_type=jnp.float32)
    plane = chan_count * seg_width
    slot_seg16 = slot_seg.astype(jnp.bfloat16)
    out_ocean = pick_dot(slot_seg16, ocean_state.reshape(seg_count, plane))
    out_mask = select_rows(slot_seg, land_mask.astype(jnp.float32), None)
    row_high = (intersection_row // 32).astype(jnp.bfloat16)
    row_low = (intersection_row % 32).astype(jnp.bfloat16)
    row_parts = jnp.concatenate(
        [jnp.broadcast_to(row_high[:, None], (ov_rows, seg_width)),
         jnp.broadcast_to(row_low[:, None], (ov_rows, seg_width))], axis=1
    )
    out_rows = jnp.dot(slot_pick, row_parts, preferred_element_type=jnp.float32)
    out_label = 32.0 * out_rows[:, :seg_width] + out_rows[:, seg_width:]
    out_area = pick_dot(slot_pick, intersection_area)
    out_weight = out_area * out_mask
    outgoing = jnp.concatenate([out_ocean, out_weight, out_label], axis=1)
    incoming = lax.all_to_all(outgoing, ("atm", "ocn"), split_axis=0, concat_axis=0, tiled=True)

    atm_planes = jnp.transpose(atm_state, (1, 0, 2))
    both = jnp.concatenate([atm_planes, jnp.transpose(diffusivity, (1, 0, 2))], axis=0)
    sizes = (atm_count, ocn_count)
    rows_padded = -(-(row_count + 2 * EDGE) // 128) * 128
    smoothed, dtall, dside = smooth_call(sizes, both, chan_count, rows_padded)

    in_labels = jnp.max(incoming[:, plane + seg_width :], axis=1).astype(jnp.int32)
    row_pick = (
        jnp.arange(row_count, dtype=jnp.int32)[:, None] == in_labels[None, :]
    ).astype(jnp.bfloat16)
    pick_rows = row_pick.T
    air = [pick_dot(pick_rows, smoothed[c]) for c in range(chan_count)]
    ocean = [incoming[:, c * seg_width : (c + 1) * seg_width] for c in range(chan_count)]
    in_weight = incoming[:, plane : plane + seg_width]
    wind_east = air[1] - ocean[1]
    wind_north = air[2] - ocean[2]
    wind_speed = jnp.sqrt(wind_east * wind_east + wind_north * wind_north + 0.5)
    temp_gap = ocean[0] - air[0]
    factor = 1.0 + 0.5 * jnp.tanh(temp_gap / wind_speed)
    weighted = [
        in_weight * (0.8 * factor * wind_speed * temp_gap),
        in_weight * (0.6 * factor * wind_speed * wind_east),
        in_weight * (0.6 * factor * wind_speed * wind_north),
    ]
    returned = lax.all_to_all(
        jnp.concatenate(weighted, axis=1), ("atm", "ocn"), split_axis=0, concat_axis=0, tiled=True
    )
    ocean_flux = pick_dot(slot_seg16.T, returned).reshape(seg_count, chan_count, seg_width)
    signs = (1.0, -1.0, -1.0)
    forced = jnp.stack(
        [atm_planes[c] + signs[c] * pick_dot(row_pick, weighted[c])
         for c in range(chan_count)]
    )
    current = diffuse_call(sizes, forced, dtall, dside)
    return (jnp.transpose(current, (1, 0, 2)), ocean_flux)


def solution(mesh):
    placed = (
        P("atm", None, "ocn"),
        P("atm", None, "ocn"),
        P(("atm", "ocn"), None, None),
        P(("atm", "ocn"), None),
        P(("atm", "ocn"), None),
        P(("atm", "ocn")),
        P(("atm", "ocn"), None),
        P(("atm", "ocn")),
    )
    return jax.shard_map(
        per_device,
        mesh=mesh,
        in_specs=placed,
        out_specs=(P("atm", None, "ocn"), P(("atm", "ocn"), None, None)),
        check_vma=False,
    )
```

```python
import functools

import jax
import jax.numpy as jnp
from jax import lax
from jax.experimental import pallas as pl
from jax.experimental.pallas import tpu as pltpu
from jax.sharding import PartitionSpec as P

ITERS = 3
HIGHEST = lax.Precision.HIGHEST
HALO = ITERS
EDGE = 8


def with_halo(block, sides, width):
    for axis, dim in sides:
        count = lax.axis_size(axis)
        forward = [(i, i + 1) for i in range(count - 1)]
        backward = [(target, source) for source, target in forward]
        low = lax.ppermute(
            lax.slice_in_dim(block, block.shape[dim] - width, None, axis=dim), axis, forward
        )
        high = lax.ppermute(lax.slice_in_dim(block, 0, width, axis=dim), axis, backward)
        block = jnp.concatenate([low, block, high], axis=dim)
    return block


def beside_all(padded):
    return padded[2:, :, 1:-1] + padded[:-2, :, 1:-1] + padded[1:-1, :, 2:] + padded[1:-1, :, :-2]


def fluxes(ocean_part, air_part):
    wind_east = air_part[:, 1] - ocean_part[:, 1]
    wind_north = air_part[:, 2] - ocean_part[:, 2]
    wind_speed = jnp.sqrt(wind_east * wind_east + wind_north * wind_north + 0.5)
    temp_gap = ocean_part[:, 0] - air_part[:, 0]
    factor = 1.0 + 0.5 * jnp.tanh(temp_gap / wind_speed)
    return jnp.stack(
        [
            0.8 * factor * wind_speed * temp_gap,
            0.6 * factor * wind_speed * wind_east,
            0.6 * factor * wind_speed * wind_north,
        ],
        axis=1,
    )


def pick_dot(pick, values):
    parts = []
    rest = values
    for part in range(3):
        high = lax.reduce_precision(rest, exponent_bits=8, mantissa_bits=7)
        parts.append(high.astype(jnp.bfloat16))
        rest = rest - high
    total = None
    for part in parts:
        term = jnp.dot(pick, part, preferred_element_type=jnp.float32)
        total = term if total is None else total + term
    return total


def select_rows(chosen, values, precision=HIGHEST):
    flat = values.reshape(values.shape[0], -1)
    total = jnp.dot(chosen, flat, precision=precision, preferred_element_type=jnp.float32)
    return total.reshape((chosen.shape[0],) + values.shape[1:])


MESH = pl.DeviceIdType.MESH


def exchange(sizes, x_ref, rows_buf, cols_buf, colsend, tall_s, side_s, send_sem, recv_sem):
    atm_n, ocn_n = sizes
    chans, rows, width = x_ref.shape
    rows_padded = tall_s.shape[1]
    me_a = lax.axis_index("atm")
    me_o = lax.axis_index("ocn")
    up = lax.rem(me_a + atm_n - 1, atm_n)
    down = lax.rem(me_a + 1, atm_n)
    left = lax.rem(me_o + ocn_n - 1, ocn_n)
    right = lax.rem(me_o + 1, ocn_n)
    peers = ((up, me_o), (down, me_o), (me_a, left), (me_a, right),
             (up, left), (up, right), (down, left), (down, right))
    barrier = pltpu.get_barrier_semaphore()
    for peer in peers:
        pl.semaphore_signal(barrier, 1, device_id=peer, device_id_type=MESH)
    pl.semaphore_wait(barrier, len(peers))

    spare = jnp.zeros((rows_padded - rows, width), jnp.float32)
    for c in range(chans):
        flipped = jnp.concatenate([x_ref[c], spare], axis=0).T
        colsend[0, c] = flipped[:EDGE]
        colsend[1, c] = flipped[width - EDGE :]

    last = x_ref.at[:, rows - EDGE :, :]
    first = x_ref.at[:, :EDGE, :]
    plan = (
        (last, rows_buf.at[0], (down, me_o)),
        (first, rows_buf.at[1], (up, me_o)),
        (last, rows_buf.at[2], (down, right)),
        (last, rows_buf.at[3], (down, left)),
        (first, rows_buf.at[4], (up, right)),
        (first, rows_buf.at[5], (up, left)),
        (colsend.at[0], cols_buf.at[1], (me_a, left)),
        (colsend.at[1], cols_buf.at[0], (me_a, right)),
    )
    copies = []
    for k, (src, dst, peer) in enumerate(plan):
        copy = pltpu.make_async_remote_copy(
            src, dst, send_sem.at[k], recv_sem.at[k], device_id=peer, device_id_type=MESH)
        copy.start()
        copies.append(copy)
    for copy in copies:
        copy.wait()

    has_up = me_a > 0
    has_down = me_a < atm_n - 1
    has_left = me_o > 0
    has_right = me_o < ocn_n - 1
    lane = lax.broadcasted_iota(jnp.int32, (EDGE, width), 1)
    low_lanes = lane < EDGE
    high_lanes = lane >= width - EDGE
    tail = jnp.zeros((rows_padded - rows - 2 * EDGE, width), jnp.float32)
    middle = jnp.zeros((width - 2 * EDGE, rows_padded), jnp.float32)
    for c in range(chans):
        top = jnp.where(has_up, rows_buf[0, c], 0.0)
        bottom = jnp.where(has_down, rows_buf[1, c], 0.0)
        tall_s[c] = jnp.concatenate([top, x_ref[c], bottom, tail], axis=0)
        from_left = jnp.where(has_left, cols_buf[0, c], 0.0)
        from_right = jnp.where(has_right, cols_buf[1, c], 0.0)
        own = jnp.concatenate([from_right, middle, from_left], axis=0).T
        corner_top = jnp.where(
            low_lanes & (has_up & has_right), rows_buf[3, c],
            jnp.where(high_lanes & (has_up & has_left), rows_buf[2, c], 0.0))
        corner_bottom = jnp.where(
            low_lanes & (has_down & has_right), rows_buf[5, c],
            jnp.where(high_lanes & (has_down & has_left), rows_buf[4, c], 0.0))
        side_s[c] = jnp.concatenate([corner_top, own[:rows], corner_bottom, tail], axis=0)


def exchange_scratch(chans, rows_padded, width):
    return [
        pltpu.VMEM((6, chans, EDGE, width), jnp.float32),
        pltpu.VMEM((2, chans, EDGE, rows_padded), jnp.float32),
        pltpu.VMEM((2, chans, EDGE, rows_padded), jnp.float32),
        pltpu.VMEM((chans, rows_padded, width), jnp.float32),
        pltpu.VMEM((chans, rows_padded, width), jnp.float32),
        pltpu.SemaphoreType.DMA((8,)),
        pltpu.SemaphoreType.DMA((8,)),
    ]


def stencil_sum(state):
    rows_padded, lanes = state.shape
    return (
        pltpu.roll(state, rows_padded - 1, 0)
        + pltpu.roll(state, 1, 0)
        + pltpu.roll(state, lanes - 1, 1)
        + pltpu.roll(state, 1, 1)
    )


def smooth_kernel(sizes, x_ref, out_ref, tall_out, side_out, *scratch):
    rows_buf, cols_buf, colsend, tall_s, side_s, send_sem, recv_sem = scratch
    exchange(sizes, x_ref, rows_buf, cols_buf, colsend, tall_s, side_s, send_sem, recv_sem)
    rows, width = out_ref.shape[1], out_ref.shape[2]
    kept = tall_out.shape[0]
    tall_out[...] = tall_s[kept:]
    side_out[...] = side_s[kept:]
    for chan in range(out_ref.shape[0]):
        state = jnp.concatenate([tall_s[chan], side_s[chan]], axis=1)
        out_ref[chan] = (0.5 * state + 0.125 * stencil_sum(state))[EDGE : EDGE + rows, :width]


def diffuse_kernel(sizes, x_ref, dtall_ref, dside_ref, out_ref, *scratch):
    rows_buf, cols_buf, colsend, tall_s, side_s, send_sem, recv_sem = scratch
    exchange(sizes, x_ref, rows_buf, cols_buf, colsend, tall_s, side_s, send_sem, recv_sem)
    rows, width = out_ref.shape[1], out_ref.shape[2]
    first = dtall_ref.shape[0] - out_ref.shape[0]
    for chan in range(out_ref.shape[0]):
        state = jnp.concatenate([tall_s[chan], side_s[chan]], axis=1)
        diff = jnp.concatenate([dtall_ref[first + chan], dside_ref[first + chan]], axis=1)
        for iteration in range(ITERS):
            state = state + diff * (stencil_sum(state) - 4.0 * state)
        out_ref[chan] = state[EDGE : EDGE + rows, :width]


def smooth_call(sizes, both, chans, rows_padded):
    total, rows, width = both.shape
    vmem = pl.BlockSpec(memory_space=pltpu.VMEM)
    return pl.pallas_call(
        functools.partial(smooth_kernel, sizes),
        out_shape=(
            jax.ShapeDtypeStruct((chans, rows, width), jnp.float32),
            jax.ShapeDtypeStruct((total - chans, rows_padded, width), jnp.float32),
            jax.ShapeDtypeStruct((total - chans, rows_padded, width), jnp.float32),
        ),
        in_specs=[vmem],
        out_specs=(vmem, vmem, vmem),
        scratch_shapes=exchange_scratch(total, rows_padded, width),
        compiler_params=pltpu.CompilerParams(collective_id=0, has_side_effects=True),
    )(both)


def diffuse_call(sizes, forced, dtall, dside):
    chans, rows, width = forced.shape
    rows_padded = dtall.shape[1]
    vmem = pl.BlockSpec(memory_space=pltpu.VMEM)
    return pl.pallas_call(
        functools.partial(diffuse_kernel, sizes),
        out_shape=jax.ShapeDtypeStruct((chans, rows, width), jnp.float32),
        in_specs=[vmem] * 3,
        out_specs=vmem,
        scratch_shapes=exchange_scratch(chans, rows_padded, width),
        compiler_params=pltpu.CompilerParams(collective_id=1, has_side_effects=True),
    )(forced, dtall, dside)


def per_device(
    atm_state,
    diffusivity,
    ocean_state,
    land_mask,
    intersection_area,
    intersection_seg,
    intersection_dest,
    intersection_row,
):
    atm_count = lax.axis_size("atm")
    ocn_count = lax.axis_size("ocn")
    devices = atm_count * ocn_count
    row_count, chan_count, seg_width = atm_state.shape
    seg_count = ocean_state.shape[0]
    ov_rows = intersection_seg.shape[0]
    capacity = max(2, 2 * ov_rows // devices)
    slots = devices * capacity

    target = intersection_dest[:, 0]
    matches = (target[:, None] == jnp.arange(devices, dtype=jnp.int32)[None, :]).astype(jnp.int32)
    position = jnp.sum((jnp.cumsum(matches, axis=0) - matches) * matches, axis=1)
    slot_index = target * capacity + position
    slot_pick = (
        jnp.arange(slots, dtype=jnp.int32)[:, None] == slot_index[None, :]
    ).astype(jnp.bfloat16)
    seg_pick = (
        intersection_seg[:, None] == jnp.arange(seg_count, dtype=jnp.int32)[None, :]
    ).astype(jnp.bfloat16)
    slot_seg = jnp.dot(slot_pick, seg_pick, preferred_element_type=jnp.float32)
    plane = chan_count * seg_width
    out_ocean = select_rows(slot_seg, ocean_state.reshape(seg_count, plane))
    out_mask = select_rows(slot_seg, land_mask.astype(jnp.float32), None)
    row_high = (intersection_row // 32).astype(jnp.bfloat16)
    row_low = (intersection_row % 32).astype(jnp.bfloat16)
    row_parts = jnp.concatenate(
        [jnp.broadcast_to(row_high[:, None], (ov_rows, seg_width)),
         jnp.broadcast_to(row_low[:, None], (ov_rows, seg_width))], axis=1
    )
    out_rows = jnp.dot(slot_pick, row_parts, preferred_element_type=jnp.float32)
    out_label = 32.0 * out_rows[:, :seg_width] + out_rows[:, seg_width:]
    out_area = select_rows(slot_pick.astype(jnp.float32), intersection_area)
    out_weight = out_area * out_mask
    outgoing = jnp.concatenate([out_ocean, out_weight, out_label], axis=1)
    incoming = lax.all_to_all(outgoing, ("atm", "ocn"), split_axis=0, concat_axis=0, tiled=True)

    atm_planes = jnp.transpose(atm_state, (1, 0, 2))
    both = jnp.concatenate([atm_planes, jnp.transpose(diffusivity, (1, 0, 2))], axis=0)
    sizes = (atm_count, ocn_count)
    rows_padded = -(-(row_count + 2 * EDGE) // 128) * 128
    smoothed, dtall, dside = smooth_call(sizes, both, chan_count, rows_padded)

    in_labels = jnp.max(incoming[:, plane + seg_width :], axis=1).astype(jnp.int32)
    row_pick = (
        jnp.arange(row_count, dtype=jnp.int32)[:, None] == in_labels[None, :]
    ).astype(jnp.float32)
    pick_rows = row_pick.T
    air = [jnp.dot(pick_rows, smoothed[c], precision=HIGHEST, preferred_element_type=jnp.float32)
           for c in range(chan_count)]
    ocean = [incoming[:, c * seg_width : (c + 1) * seg_width] for c in range(chan_count)]
    in_weight = incoming[:, plane : plane + seg_width]
    wind_east = air[1] - ocean[1]
    wind_north = air[2] - ocean[2]
    wind_speed = jnp.sqrt(wind_east * wind_east + wind_north * wind_north + 0.5)
    temp_gap = ocean[0] - air[0]
    factor = 1.0 + 0.5 * jnp.tanh(temp_gap / wind_speed)
    weighted = [
        in_weight * (0.8 * factor * wind_speed * temp_gap),
        in_weight * (0.6 * factor * wind_speed * wind_east),
        in_weight * (0.6 * factor * wind_speed * wind_north),
    ]
    returned = lax.all_to_all(
        jnp.concatenate(weighted, axis=1), ("atm", "ocn"), split_axis=0, concat_axis=0, tiled=True
    )
    signs = (1.0, -1.0, -1.0)
    forced = jnp.stack(
        [atm_planes[c] + signs[c] * jnp.dot(row_pick, weighted[c], precision=HIGHEST,
                                             preferred_element_type=jnp.float32)
         for c in range(chan_count)]
    )
    current = diffuse_call(sizes, forced, dtall, dside)
    current, returned = lax.optimization_barrier((current, returned))
    seg_of_slot = slot_seg.T.astype(jnp.bfloat16)
    ocean_flux = pick_dot(seg_of_slot, returned).reshape(seg_count, chan_count, seg_width)
    return (jnp.transpose(current, (1, 0, 2)), ocean_flux)


def solution(mesh):
    placed = (
        P("atm", None, "ocn"),
        P("atm", None, "ocn"),
        P(("atm", "ocn"), None, None),
        P(("atm", "ocn"), None),
        P(("atm", "ocn"), None),
        P(("atm", "ocn")),
        P(("atm", "ocn"), None),
        P(("atm", "ocn")),
    )
    return jax.shard_map(
        per_device,
        mesh=mesh,
        in_specs=placed,
        out_specs=(P("atm", None, "ocn"), P(("atm", "ocn"), None, None)),
        check_vma=False,
    )
```

```python
import functools

import jax
import jax.numpy as jnp
from jax import lax
from jax.experimental import pallas as pl
from jax.experimental.pallas import tpu as pltpu
from jax.sharding import PartitionSpec as P

ITERS = 3
HIGHEST = lax.Precision.HIGHEST
HALO = ITERS
EDGE = 8


def with_halo(block, sides, width):
    for axis, dim in sides:
        count = lax.axis_size(axis)
        forward = [(i, i + 1) for i in range(count - 1)]
        backward = [(target, source) for source, target in forward]
        low = lax.ppermute(
            lax.slice_in_dim(block, block.shape[dim] - width, None, axis=dim), axis, forward
        )
        high = lax.ppermute(lax.slice_in_dim(block, 0, width, axis=dim), axis, backward)
        block = jnp.concatenate([low, block, high], axis=dim)
    return block


def beside_all(padded):
    return padded[2:, :, 1:-1] + padded[:-2, :, 1:-1] + padded[1:-1, :, 2:] + padded[1:-1, :, :-2]


def fluxes(ocean_part, air_part):
    wind_east = air_part[:, 1] - ocean_part[:, 1]
    wind_north = air_part[:, 2] - ocean_part[:, 2]
    wind_speed = jnp.sqrt(wind_east * wind_east + wind_north * wind_north + 0.5)
    temp_gap = ocean_part[:, 0] - air_part[:, 0]
    factor = 1.0 + 0.5 * jnp.tanh(temp_gap / wind_speed)
    return jnp.stack(
        [
            0.8 * factor * wind_speed * temp_gap,
            0.6 * factor * wind_speed * wind_east,
            0.6 * factor * wind_speed * wind_north,
        ],
        axis=1,
    )


def pick_dot(pick, values):
    parts = []
    rest = values
    for part in range(3):
        high = lax.reduce_precision(rest, exponent_bits=8, mantissa_bits=7)
        parts.append(high.astype(jnp.bfloat16))
        rest = rest - high
    total = None
    for part in parts:
        term = jnp.dot(pick, part, preferred_element_type=jnp.float32)
        total = term if total is None else total + term
    return total


def select_rows(chosen, values, precision=HIGHEST):
    flat = values.reshape(values.shape[0], -1)
    total = jnp.dot(chosen, flat, precision=precision, preferred_element_type=jnp.float32)
    return total.reshape((chosen.shape[0],) + values.shape[1:])


MESH = pl.DeviceIdType.MESH


def exchange(sizes, x_ref, rows_buf, cols_buf, colsend, tall_s, side_s, send_sem, recv_sem):
    atm_n, ocn_n = sizes
    chans, rows, width = x_ref.shape
    rows_padded = tall_s.shape[1]
    me_a = lax.axis_index("atm")
    me_o = lax.axis_index("ocn")
    up = lax.rem(me_a + atm_n - 1, atm_n)
    down = lax.rem(me_a + 1, atm_n)
    left = lax.rem(me_o + ocn_n - 1, ocn_n)
    right = lax.rem(me_o + 1, ocn_n)
    peers = ((up, me_o), (down, me_o), (me_a, left), (me_a, right),
             (up, left), (up, right), (down, left), (down, right))
    barrier = pltpu.get_barrier_semaphore()
    for peer in peers:
        pl.semaphore_signal(barrier, 1, device_id=peer, device_id_type=MESH)
    pl.semaphore_wait(barrier, len(peers))

    spare = jnp.zeros((rows_padded - rows, width), jnp.float32)
    for c in range(chans):
        flipped = jnp.concatenate([x_ref[c], spare], axis=0).T
        colsend[0, c] = flipped[:EDGE]
        colsend[1, c] = flipped[width - EDGE :]

    last = x_ref.at[:, rows - EDGE :, :]
    first = x_ref.at[:, :EDGE, :]
    plan = (
        (last, rows_buf.at[0], (down, me_o)),
        (first, rows_buf.at[1], (up, me_o)),
        (last, rows_buf.at[2], (down, right)),
        (last, rows_buf.at[3], (down, left)),
        (first, rows_buf.at[4], (up, right)),
        (first, rows_buf.at[5], (up, left)),
        (colsend.at[0], cols_buf.at[1], (me_a, left)),
        (colsend.at[1], cols_buf.at[0], (me_a, right)),
    )
    copies = []
    for k, (src, dst, peer) in enumerate(plan):
        copy = pltpu.make_async_remote_copy(
            src, dst, send_sem.at[k], recv_sem.at[k], device_id=peer, device_id_type=MESH)
        copy.start()
        copies.append(copy)
    for copy in copies:
        copy.wait()

    has_up = me_a > 0
    has_down = me_a < atm_n - 1
    has_left = me_o > 0
    has_right = me_o < ocn_n - 1
    lane = lax.broadcasted_iota(jnp.int32, (EDGE, width), 1)
    low_lanes = lane < EDGE
    high_lanes = lane >= width - EDGE
    tail = jnp.zeros((rows_padded - rows - 2 * EDGE, width), jnp.float32)
    middle = jnp.zeros((width - 2 * EDGE, rows_padded), jnp.float32)
    for c in range(chans):
        top = jnp.where(has_up, rows_buf[0, c], 0.0)
        bottom = jnp.where(has_down, rows_buf[1, c], 0.0)
        tall_s[c] = jnp.concatenate([top, x_ref[c], bottom, tail], axis=0)
        from_left = jnp.where(has_left, cols_buf[0, c], 0.0)
        from_right = jnp.where(has_right, cols_buf[1, c], 0.0)
        own = jnp.concatenate([from_right, middle, from_left], axis=0).T
        corner_top = jnp.where(
            low_lanes & (has_up & has_right), rows_buf[3, c],
            jnp.where(high_lanes & (has_up & has_left), rows_buf[2, c], 0.0))
        corner_bottom = jnp.where(
            low_lanes & (has_down & has_right), rows_buf[5, c],
            jnp.where(high_lanes & (has_down & has_left), rows_buf[4, c], 0.0))
        side_s[c] = jnp.concatenate([corner_top, own[:rows], corner_bottom, tail], axis=0)


def exchange_scratch(chans, rows_padded, width):
    return [
        pltpu.VMEM((6, chans, EDGE, width), jnp.float32),
        pltpu.VMEM((2, chans, EDGE, rows_padded), jnp.float32),
        pltpu.VMEM((2, chans, EDGE, rows_padded), jnp.float32),
        pltpu.VMEM((chans, rows_padded, width), jnp.float32),
        pltpu.VMEM((chans, rows_padded, width), jnp.float32),
        pltpu.SemaphoreType.DMA((8,)),
        pltpu.SemaphoreType.DMA((8,)),
    ]


def stencil_sum(state):
    rows_padded, lanes = state.shape
    return (
        pltpu.roll(state, rows_padded - 1, 0)
        + pltpu.roll(state, 1, 0)
        + pltpu.roll(state, lanes - 1, 1)
        + pltpu.roll(state, 1, 1)
    )


CHUNK = 96


def chunk_rows(rows):
    return CHUNK if rows % CHUNK == 0 else rows


def smooth_kernel(sizes, x_ref, out_ref, tall_out, side_out, *scratch):
    rows_buf, cols_buf, colsend, tall_s, side_s, send_sem, recv_sem = scratch
    exchange(sizes, x_ref, rows_buf, cols_buf, colsend, tall_s, side_s, send_sem, recv_sem)
    rows, width = out_ref.shape[1], out_ref.shape[2]
    kept = tall_out.shape[0]
    tall_out[...] = tall_s[kept:]
    side_out[...] = side_s[kept:]
    step = chunk_rows(rows)
    span = step + 2 * EDGE
    for chan in range(out_ref.shape[0]):
        def body(k, carry):
            start = pl.multiple_of(k * step, 8)
            state = jnp.concatenate(
                [tall_s[chan, pl.ds(start, span), :], side_s[chan, pl.ds(start, span), :]], axis=1)
            done = 0.5 * state + 0.125 * stencil_sum(state)
            out_ref[chan, pl.ds(start, step), :] = done[EDGE : EDGE + step, :width]
            return carry
        lax.fori_loop(0, rows // step, body, 0)


def diffuse_kernel(sizes, x_ref, dtall_ref, dside_ref, out_ref, *scratch):
    rows_buf, cols_buf, colsend, tall_s, side_s, send_sem, recv_sem = scratch
    exchange(sizes, x_ref, rows_buf, cols_buf, colsend, tall_s, side_s, send_sem, recv_sem)
    rows, width = out_ref.shape[1], out_ref.shape[2]
    first = dtall_ref.shape[0] - out_ref.shape[0]
    step = chunk_rows(rows)
    span = step + 2 * EDGE
    for chan in range(out_ref.shape[0]):
        def body(k, carry):
            start = pl.multiple_of(k * step, 8)
            window = pl.ds(start, span)
            state = jnp.concatenate(
                [tall_s[chan, window, :], side_s[chan, window, :]], axis=1)
            diff = jnp.concatenate(
                [dtall_ref[first + chan, window, :], dside_ref[first + chan, window, :]], axis=1)
            for iteration in range(ITERS):
                state = state + diff * (stencil_sum(state) - 4.0 * state)
            out_ref[chan, pl.ds(start, step), :] = state[EDGE : EDGE + step, :width]
            return carry
        lax.fori_loop(0, rows // step, body, 0)


def smooth_call(sizes, both, chans, rows_padded):
    total, rows, width = both.shape
    vmem = pl.BlockSpec(memory_space=pltpu.VMEM)
    return pl.pallas_call(
        functools.partial(smooth_kernel, sizes),
        out_shape=(
            jax.ShapeDtypeStruct((chans, rows, width), jnp.float32),
            jax.ShapeDtypeStruct((total - chans, rows_padded, width), jnp.float32),
            jax.ShapeDtypeStruct((total - chans, rows_padded, width), jnp.float32),
        ),
        in_specs=[vmem],
        out_specs=(vmem, vmem, vmem),
        scratch_shapes=exchange_scratch(total, rows_padded, width),
        compiler_params=pltpu.CompilerParams(collective_id=0, has_side_effects=True),
    )(both)


def diffuse_call(sizes, forced, dtall, dside):
    chans, rows, width = forced.shape
    rows_padded = dtall.shape[1]
    vmem = pl.BlockSpec(memory_space=pltpu.VMEM)
    return pl.pallas_call(
        functools.partial(diffuse_kernel, sizes),
        out_shape=jax.ShapeDtypeStruct((chans, rows, width), jnp.float32),
        in_specs=[vmem] * 3,
        out_specs=vmem,
        scratch_shapes=exchange_scratch(chans, rows_padded, width),
        compiler_params=pltpu.CompilerParams(collective_id=1, has_side_effects=True),
    )(forced, dtall, dside)


def per_device(
    atm_state,
    diffusivity,
    ocean_state,
    land_mask,
    intersection_area,
    intersection_seg,
    intersection_dest,
    intersection_row,
):
    atm_count = lax.axis_size("atm")
    ocn_count = lax.axis_size("ocn")
    devices = atm_count * ocn_count
    row_count, chan_count, seg_width = atm_state.shape
    seg_count = ocean_state.shape[0]
    ov_rows = intersection_seg.shape[0]
    capacity = max(2, 2 * ov_rows // devices)
    slots = devices * capacity

    target = intersection_dest[:, 0]
    matches = (target[:, None] == jnp.arange(devices, dtype=jnp.int32)[None, :]).astype(jnp.int32)
    position = jnp.sum((jnp.cumsum(matches, axis=0) - matches) * matches, axis=1)
    slot_index = target * capacity + position
    slot_pick = (
        jnp.arange(slots, dtype=jnp.int32)[:, None] == slot_index[None, :]
    ).astype(jnp.bfloat16)
    seg_pick = (
        intersection_seg[:, None] == jnp.arange(seg_count, dtype=jnp.int32)[None, :]
    ).astype(jnp.bfloat16)
    slot_seg = jnp.dot(slot_pick, seg_pick, preferred_element_type=jnp.float32)
    plane = chan_count * seg_width
    out_ocean = select_rows(slot_seg, ocean_state.reshape(seg_count, plane))
    out_mask = select_rows(slot_seg, land_mask.astype(jnp.float32), None)
    row_high = (intersection_row // 32).astype(jnp.bfloat16)
    row_low = (intersection_row % 32).astype(jnp.bfloat16)
    row_parts = jnp.concatenate(
        [jnp.broadcast_to(row_high[:, None], (ov_rows, seg_width)),
         jnp.broadcast_to(row_low[:, None], (ov_rows, seg_width))], axis=1
    )
    out_rows = jnp.dot(slot_pick, row_parts, preferred_element_type=jnp.float32)
    out_label = 32.0 * out_rows[:, :seg_width] + out_rows[:, seg_width:]
    out_area = select_rows(slot_pick.astype(jnp.float32), intersection_area)
    out_weight = out_area * out_mask
    outgoing = jnp.concatenate([out_ocean, out_weight, out_label], axis=1)
    incoming = lax.all_to_all(outgoing, ("atm", "ocn"), split_axis=0, concat_axis=0, tiled=True)

    atm_planes = jnp.transpose(atm_state, (1, 0, 2))
    both = jnp.concatenate([atm_planes, jnp.transpose(diffusivity, (1, 0, 2))], axis=0)
    sizes = (atm_count, ocn_count)
    rows_padded = -(-(row_count + 2 * EDGE) // 128) * 128
    smoothed, dtall, dside = smooth_call(sizes, both, chan_count, rows_padded)

    in_labels = jnp.max(incoming[:, plane + seg_width :], axis=1).astype(jnp.int32)
    row_pick = (
        jnp.arange(row_count, dtype=jnp.int32)[:, None] == in_labels[None, :]
    ).astype(jnp.float32)
    pick_rows = row_pick.T
    air = [jnp.dot(pick_rows, smoothed[c], precision=HIGHEST, preferred_element_type=jnp.float32)
           for c in range(chan_count)]
    ocean = [incoming[:, c * seg_width : (c + 1) * seg_width] for c in range(chan_count)]
    in_weight = incoming[:, plane : plane + seg_width]
    wind_east = air[1] - ocean[1]
    wind_north = air[2] - ocean[2]
    wind_speed = jnp.sqrt(wind_east * wind_east + wind_north * wind_north + 0.5)
    temp_gap = ocean[0] - air[0]
    factor = 1.0 + 0.5 * jnp.tanh(temp_gap / wind_speed)
    weighted = [
        in_weight * (0.8 * factor * wind_speed * temp_gap),
        in_weight * (0.6 * factor * wind_speed * wind_east),
        in_weight * (0.6 * factor * wind_speed * wind_north),
    ]
    returned = lax.all_to_all(
        jnp.concatenate(weighted, axis=1), ("atm", "ocn"), split_axis=0, concat_axis=0, tiled=True
    )
    signs = (1.0, -1.0, -1.0)
    forced = jnp.stack(
        [atm_planes[c] + signs[c] * jnp.dot(row_pick, weighted[c], precision=HIGHEST,
                                             preferred_element_type=jnp.float32)
         for c in range(chan_count)]
    )
    current = diffuse_call(sizes, forced, dtall, dside)
    current, returned = lax.optimization_barrier((current, returned))
    seg_of_slot = slot_seg.T.astype(jnp.bfloat16)
    ocean_flux = pick_dot(seg_of_slot, returned).reshape(seg_count, chan_count, seg_width)
    return (jnp.transpose(current, (1, 0, 2)), ocean_flux)


def solution(mesh):
    placed = (
        P("atm", None, "ocn"),
        P("atm", None, "ocn"),
        P(("atm", "ocn"), None, None),
        P(("atm", "ocn"), None),
        P(("atm", "ocn"), None),
        P(("atm", "ocn")),
        P(("atm", "ocn"), None),
        P(("atm", "ocn")),
    )
    return jax.shard_map(
        per_device,
        mesh=mesh,
        in_specs=placed,
        out_specs=(P("atm", None, "ocn"), P(("atm", "ocn"), None, None)),
        check_vma=False,
    )
```

```python
import functools

import jax
import jax.numpy as jnp
from jax import lax
from jax.experimental import pallas as pl
from jax.experimental.pallas import tpu as pltpu
from jax.sharding import PartitionSpec as P

ITERS = 3
HIGHEST = lax.Precision.HIGHEST
HALO = ITERS
EDGE = 8


def with_halo(block, sides, width):
    for axis, dim in sides:
        count = lax.axis_size(axis)
        forward = [(i, i + 1) for i in range(count - 1)]
        backward = [(target, source) for source, target in forward]
        low = lax.ppermute(
            lax.slice_in_dim(block, block.shape[dim] - width, None, axis=dim), axis, forward
        )
        high = lax.ppermute(lax.slice_in_dim(block, 0, width, axis=dim), axis, backward)
        block = jnp.concatenate([low, block, high], axis=dim)
    return block


def beside_all(padded):
    return padded[2:, :, 1:-1] + padded[:-2, :, 1:-1] + padded[1:-1, :, 2:] + padded[1:-1, :, :-2]


def fluxes(ocean_part, air_part):
    wind_east = air_part[:, 1] - ocean_part[:, 1]
    wind_north = air_part[:, 2] - ocean_part[:, 2]
    wind_speed = jnp.sqrt(wind_east * wind_east + wind_north * wind_north + 0.5)
    temp_gap = ocean_part[:, 0] - air_part[:, 0]
    factor = 1.0 + 0.5 * jnp.tanh(temp_gap / wind_speed)
    return jnp.stack(
        [
            0.8 * factor * wind_speed * temp_gap,
            0.6 * factor * wind_speed * wind_east,
            0.6 * factor * wind_speed * wind_north,
        ],
        axis=1,
    )


def pick_dot(pick, values):
    parts = []
    rest = values
    for part in range(3):
        high = lax.reduce_precision(rest, exponent_bits=8, mantissa_bits=7)
        parts.append(high.astype(jnp.bfloat16))
        rest = rest - high
    total = None
    for part in parts:
        term = jnp.dot(pick, part, preferred_element_type=jnp.float32)
        total = term if total is None else total + term
    return total


def select_rows(chosen, values, precision=HIGHEST):
    flat = values.reshape(values.shape[0], -1)
    total = jnp.dot(chosen, flat, precision=precision, preferred_element_type=jnp.float32)
    return total.reshape((chosen.shape[0],) + values.shape[1:])


MESH = pl.DeviceIdType.MESH


def exchange(sizes, x_ref, rows_buf, cols_buf, colsend, tall_s, side_s, send_sem, recv_sem):
    atm_n, ocn_n = sizes
    chans, rows, width = x_ref.shape
    rows_padded = tall_s.shape[1]
    me_a = lax.axis_index("atm")
    me_o = lax.axis_index("ocn")
    up = lax.rem(me_a + atm_n - 1, atm_n)
    down = lax.rem(me_a + 1, atm_n)
    left = lax.rem(me_o + ocn_n - 1, ocn_n)
    right = lax.rem(me_o + 1, ocn_n)
    peers = ((up, me_o), (down, me_o), (me_a, left), (me_a, right),
             (up, left), (up, right), (down, left), (down, right))
    barrier = pltpu.get_barrier_semaphore()
    for peer in peers:
        pl.semaphore_signal(barrier, 1, device_id=peer, device_id_type=MESH)
    pl.semaphore_wait(barrier, len(peers))

    spare = jnp.zeros((rows_padded - rows, width), jnp.float32)
    for c in range(chans):
        flipped = jnp.concatenate([x_ref[c], spare], axis=0).T
        colsend[0, c] = flipped[:EDGE]
        colsend[1, c] = flipped[width - EDGE :]

    last = x_ref.at[:, rows - EDGE :, :]
    first = x_ref.at[:, :EDGE, :]
    plan = (
        (last, rows_buf.at[0], (down, me_o)),
        (first, rows_buf.at[1], (up, me_o)),
        (last, rows_buf.at[2], (down, right)),
        (last, rows_buf.at[3], (down, left)),
        (first, rows_buf.at[4], (up, right)),
        (first, rows_buf.at[5], (up, left)),
        (colsend.at[0], cols_buf.at[1], (me_a, left)),
        (colsend.at[1], cols_buf.at[0], (me_a, right)),
    )
    copies = []
    for k, (src, dst, peer) in enumerate(plan):
        copy = pltpu.make_async_remote_copy(
            src, dst, send_sem.at[k], recv_sem.at[k], device_id=peer, device_id_type=MESH)
        copy.start()
        copies.append(copy)
    for copy in copies:
        copy.wait()

    has_up = me_a > 0
    has_down = me_a < atm_n - 1
    has_left = me_o > 0
    has_right = me_o < ocn_n - 1
    lane = lax.broadcasted_iota(jnp.int32, (EDGE, width), 1)
    low_lanes = lane < EDGE
    high_lanes = lane >= width - EDGE
    tail = jnp.zeros((rows_padded - rows - 2 * EDGE, width), jnp.float32)
    middle = jnp.zeros((width - 2 * EDGE, rows_padded), jnp.float32)
    for c in range(chans):
        top = jnp.where(has_up, rows_buf[0, c], 0.0)
        bottom = jnp.where(has_down, rows_buf[1, c], 0.0)
        tall_s[c] = jnp.concatenate([top, x_ref[c], bottom, tail], axis=0)
        from_left = jnp.where(has_left, cols_buf[0, c], 0.0)
        from_right = jnp.where(has_right, cols_buf[1, c], 0.0)
        own = jnp.concatenate([from_right, middle, from_left], axis=0).T
        corner_top = jnp.where(
            low_lanes & (has_up & has_right), rows_buf[3, c],
            jnp.where(high_lanes & (has_up & has_left), rows_buf[2, c], 0.0))
        corner_bottom = jnp.where(
            low_lanes & (has_down & has_right), rows_buf[5, c],
            jnp.where(high_lanes & (has_down & has_left), rows_buf[4, c], 0.0))
        side_s[c] = jnp.concatenate([corner_top, own[:rows], corner_bottom, tail], axis=0)


def exchange_scratch(chans, rows_padded, width):
    return [
        pltpu.VMEM((6, chans, EDGE, width), jnp.float32),
        pltpu.VMEM((2, chans, EDGE, rows_padded), jnp.float32),
        pltpu.VMEM((2, chans, EDGE, rows_padded), jnp.float32),
        pltpu.VMEM((chans, rows_padded, width), jnp.float32),
        pltpu.VMEM((chans, rows_padded, width), jnp.float32),
        pltpu.SemaphoreType.DMA((8,)),
        pltpu.SemaphoreType.DMA((8,)),
    ]


def stencil_sum(state):
    rows_padded, lanes = state.shape
    return (
        pltpu.roll(state, rows_padded - 1, 0)
        + pltpu.roll(state, 1, 0)
        + pltpu.roll(state, lanes - 1, 1)
        + pltpu.roll(state, 1, 1)
    )


def smooth_kernel(sizes, x_ref, out_ref, tall_out, side_out, *scratch):
    rows_buf, cols_buf, colsend, tall_s, side_s, send_sem, recv_sem = scratch
    exchange(sizes, x_ref, rows_buf, cols_buf, colsend, tall_s, side_s, send_sem, recv_sem)
    rows, width = out_ref.shape[1], out_ref.shape[2]
    kept = tall_out.shape[0]
    tall_out[...] = tall_s[kept:]
    side_out[...] = side_s[kept:]
    for chan in range(out_ref.shape[0]):
        state = jnp.concatenate([tall_s[chan], side_s[chan]], axis=1)
        out_ref[chan] = (0.5 * state + 0.125 * stencil_sum(state))[EDGE : EDGE + rows, :width]


def exchange_kernel(sizes, x_ref, tall_out, side_out, *scratch):
    rows_buf, cols_buf, colsend, tall_s, side_s, send_sem, recv_sem = scratch
    exchange(sizes, x_ref, rows_buf, cols_buf, colsend, tall_s, side_s, send_sem, recv_sem)
    tall_out[...] = tall_s[...]
    side_out[...] = side_s[...]


def diffuse_kernel(tall_ref, side_ref, dtall_ref, dside_ref, out_ref):
    rows, width = out_ref.shape[1], out_ref.shape[2]
    for chan in range(out_ref.shape[0]):
        state = jnp.concatenate([tall_ref[chan], side_ref[chan]], axis=1)
        diff = jnp.concatenate([dtall_ref[chan], dside_ref[chan]], axis=1)
        for iteration in range(ITERS):
            state = state + diff * (stencil_sum(state) - 4.0 * state)
        out_ref[chan] = state[EDGE : EDGE + rows, :width]


def smooth_call(sizes, both, chans, rows_padded):
    total, rows, width = both.shape
    vmem = pl.BlockSpec(memory_space=pltpu.VMEM)
    return pl.pallas_call(
        functools.partial(smooth_kernel, sizes),
        out_shape=(
            jax.ShapeDtypeStruct((chans, rows, width), jnp.float32),
            jax.ShapeDtypeStruct((total - chans, rows_padded, width), jnp.float32),
            jax.ShapeDtypeStruct((total - chans, rows_padded, width), jnp.float32),
        ),
        in_specs=[vmem],
        out_specs=(vmem, vmem, vmem),
        scratch_shapes=exchange_scratch(total, rows_padded, width),
        compiler_params=pltpu.CompilerParams(collective_id=0, has_side_effects=True),
    )(both)


def exchange_call(sizes, forced, rows_padded):
    chans, rows, width = forced.shape
    vmem = pl.BlockSpec(memory_space=pltpu.VMEM)
    plane = jax.ShapeDtypeStruct((chans, rows_padded, width), jnp.float32)
    return pl.pallas_call(
        functools.partial(exchange_kernel, sizes),
        out_shape=(plane, plane),
        in_specs=[vmem],
        out_specs=(vmem, vmem),
        scratch_shapes=exchange_scratch(chans, rows_padded, width),
        compiler_params=pltpu.CompilerParams(collective_id=1, has_side_effects=True),
    )(forced)


def diffuse_call(tall, side, dtall, dside, rows):
    chans, rows_padded, width = tall.shape
    vmem = pl.BlockSpec(memory_space=pltpu.VMEM)
    return pl.pallas_call(
        diffuse_kernel,
        out_shape=jax.ShapeDtypeStruct((chans, rows, width), jnp.float32),
        in_specs=[vmem] * 4,
        out_specs=vmem,
    )(tall, side, dtall, dside)


def per_device(
    atm_state,
    diffusivity,
    ocean_state,
    land_mask,
    intersection_area,
    intersection_seg,
    intersection_dest,
    intersection_row,
):
    atm_count = lax.axis_size("atm")
    ocn_count = lax.axis_size("ocn")
    devices = atm_count * ocn_count
    row_count, chan_count, seg_width = atm_state.shape
    seg_count = ocean_state.shape[0]
    ov_rows = intersection_seg.shape[0]
    capacity = max(2, 2 * ov_rows // devices)
    slots = devices * capacity

    target = intersection_dest[:, 0]
    matches = (target[:, None] == jnp.arange(devices, dtype=jnp.int32)[None, :]).astype(jnp.int32)
    position = jnp.sum((jnp.cumsum(matches, axis=0) - matches) * matches, axis=1)
    slot_index = target * capacity + position
    slot_pick = (
        jnp.arange(slots, dtype=jnp.int32)[:, None] == slot_index[None, :]
    ).astype(jnp.bfloat16)
    seg_pick = (
        intersection_seg[:, None] == jnp.arange(seg_count, dtype=jnp.int32)[None, :]
    ).astype(jnp.bfloat16)
    slot_seg = jnp.dot(slot_pick, seg_pick, preferred_element_type=jnp.float32)
    plane = chan_count * seg_width
    out_ocean = select_rows(slot_seg, ocean_state.reshape(seg_count, plane))
    out_mask = select_rows(slot_seg, land_mask.astype(jnp.float32), None)
    row_high = (intersection_row // 32).astype(jnp.bfloat16)
    row_low = (intersection_row % 32).astype(jnp.bfloat16)
    row_parts = jnp.concatenate(
        [jnp.broadcast_to(row_high[:, None], (ov_rows, seg_width)),
         jnp.broadcast_to(row_low[:, None], (ov_rows, seg_width))], axis=1
    )
    out_rows = jnp.dot(slot_pick, row_parts, preferred_element_type=jnp.float32)
    out_label = 32.0 * out_rows[:, :seg_width] + out_rows[:, seg_width:]
    out_area = select_rows(slot_pick.astype(jnp.float32), intersection_area)
    out_weight = out_area * out_mask
    outgoing = jnp.concatenate([out_ocean, out_weight, out_label], axis=1)
    incoming = lax.all_to_all(outgoing, ("atm", "ocn"), split_axis=0, concat_axis=0, tiled=True)

    atm_planes = jnp.transpose(atm_state, (1, 0, 2))
    both = jnp.concatenate([atm_planes, jnp.transpose(diffusivity, (1, 0, 2))], axis=0)
    sizes = (atm_count, ocn_count)
    rows_padded = -(-(row_count + 2 * EDGE) // 128) * 128
    smoothed, dtall, dside = smooth_call(sizes, both, chan_count, rows_padded)

    in_labels = jnp.max(incoming[:, plane + seg_width :], axis=1).astype(jnp.int32)
    row_pick = (
        jnp.arange(row_count, dtype=jnp.int32)[:, None] == in_labels[None, :]
    ).astype(jnp.float32)
    pick_rows = row_pick.T
    air = [jnp.dot(pick_rows, smoothed[c], precision=HIGHEST, preferred_element_type=jnp.float32)
           for c in range(chan_count)]
    ocean = [incoming[:, c * seg_width : (c + 1) * seg_width] for c in range(chan_count)]
    in_weight = incoming[:, plane : plane + seg_width]
    wind_east = air[1] - ocean[1]
    wind_north = air[2] - ocean[2]
    wind_speed = jnp.sqrt(wind_east * wind_east + wind_north * wind_north + 0.5)
    temp_gap = ocean[0] - air[0]
    factor = 1.0 + 0.5 * jnp.tanh(temp_gap / wind_speed)
    weighted = [
        in_weight * (0.8 * factor * wind_speed * temp_gap),
        in_weight * (0.6 * factor * wind_speed * wind_east),
        in_weight * (0.6 * factor * wind_speed * wind_north),
    ]
    signs = (1.0, -1.0, -1.0)
    forced = jnp.stack(
        [atm_planes[c] + signs[c] * jnp.dot(row_pick, weighted[c], precision=HIGHEST,
                                             preferred_element_type=jnp.float32)
         for c in range(chan_count)]
    )
    tall, side = exchange_call(sizes, forced, rows_padded)
    sent, tall, side = lax.optimization_barrier((jnp.concatenate(weighted, axis=1), tall, side))
    returned = lax.all_to_all(sent, ("atm", "ocn"), split_axis=0, concat_axis=0, tiled=True)
    current = diffuse_call(tall, side, dtall, dside, row_count)
    current, returned = lax.optimization_barrier((current, returned))
    seg_of_slot = slot_seg.T.astype(jnp.bfloat16)
    ocean_flux = pick_dot(seg_of_slot, returned).reshape(seg_count, chan_count, seg_width)
    return (jnp.transpose(current, (1, 0, 2)), ocean_flux)


def solution(mesh):
    placed = (
        P("atm", None, "ocn"),
        P("atm", None, "ocn"),
        P(("atm", "ocn"), None, None),
        P(("atm", "ocn"), None),
        P(("atm", "ocn"), None),
        P(("atm", "ocn")),
        P(("atm", "ocn"), None),
        P(("atm", "ocn")),
    )
    return jax.shard_map(
        per_device,
        mesh=mesh,
        in_specs=placed,
        out_specs=(P("atm", None, "ocn"), P(("atm", "ocn"), None, None)),
        check_vma=False,
    )
```

```python
import functools

import jax
import jax.numpy as jnp
from jax import lax
from jax.experimental import pallas as pl
from jax.experimental.pallas import tpu as pltpu
from jax.sharding import PartitionSpec as P

ITERS = 3
HIGHEST = lax.Precision.HIGHEST
HALO = ITERS
EDGE = 8


def with_halo(block, sides, width):
    for axis, dim in sides:
        count = lax.axis_size(axis)
        forward = [(i, i + 1) for i in range(count - 1)]
        backward = [(target, source) for source, target in forward]
        low = lax.ppermute(
            lax.slice_in_dim(block, block.shape[dim] - width, None, axis=dim), axis, forward
        )
        high = lax.ppermute(lax.slice_in_dim(block, 0, width, axis=dim), axis, backward)
        block = jnp.concatenate([low, block, high], axis=dim)
    return block


def beside_all(padded):
    return padded[2:, :, 1:-1] + padded[:-2, :, 1:-1] + padded[1:-1, :, 2:] + padded[1:-1, :, :-2]


def fluxes(ocean_part, air_part):
    wind_east = air_part[:, 1] - ocean_part[:, 1]
    wind_north = air_part[:, 2] - ocean_part[:, 2]
    wind_speed = jnp.sqrt(wind_east * wind_east + wind_north * wind_north + 0.5)
    temp_gap = ocean_part[:, 0] - air_part[:, 0]
    factor = 1.0 + 0.5 * jnp.tanh(temp_gap / wind_speed)
    return jnp.stack(
        [
            0.8 * factor * wind_speed * temp_gap,
            0.6 * factor * wind_speed * wind_east,
            0.6 * factor * wind_speed * wind_north,
        ],
        axis=1,
    )


def pick_dot(pick, values):
    parts = []
    rest = values
    for part in range(3):
        high = lax.reduce_precision(rest, exponent_bits=8, mantissa_bits=7)
        parts.append(high.astype(jnp.bfloat16))
        rest = rest - high
    total = None
    for part in parts:
        term = jnp.dot(pick, part, preferred_element_type=jnp.float32)
        total = term if total is None else total + term
    return total


def select_rows(chosen, values, precision=HIGHEST):
    flat = values.reshape(values.shape[0], -1)
    total = jnp.dot(chosen, flat, precision=precision, preferred_element_type=jnp.float32)
    return total.reshape((chosen.shape[0],) + values.shape[1:])


MESH = pl.DeviceIdType.MESH


def exchange(sizes, x_ref, rows_buf, cols_buf, colsend, tall_s, side_s, send_sem, recv_sem):
    atm_n, ocn_n = sizes
    chans, rows, width = x_ref.shape
    rows_padded = tall_s.shape[1]
    me_a = lax.axis_index("atm")
    me_o = lax.axis_index("ocn")
    up = lax.rem(me_a + atm_n - 1, atm_n)
    down = lax.rem(me_a + 1, atm_n)
    left = lax.rem(me_o + ocn_n - 1, ocn_n)
    right = lax.rem(me_o + 1, ocn_n)
    peers = ((up, me_o), (down, me_o), (me_a, left), (me_a, right),
             (up, left), (up, right), (down, left), (down, right))
    barrier = pltpu.get_barrier_semaphore()
    for peer in peers:
        pl.semaphore_signal(barrier, 1, device_id=peer, device_id_type=MESH)
    pl.semaphore_wait(barrier, len(peers))

    spare = jnp.zeros((rows_padded - rows, width), jnp.float32)
    for c in range(chans):
        flipped = jnp.concatenate([x_ref[c], spare], axis=0).T
        colsend[0, c] = flipped[:EDGE]
        colsend[1, c] = flipped[width - EDGE :]

    last = x_ref.at[:, rows - EDGE :, :]
    first = x_ref.at[:, :EDGE, :]
    plan = (
        (last, rows_buf.at[0], (down, me_o)),
        (first, rows_buf.at[1], (up, me_o)),
        (last, rows_buf.at[2], (down, right)),
        (last, rows_buf.at[3], (down, left)),
        (first, rows_buf.at[4], (up, right)),
        (first, rows_buf.at[5], (up, left)),
        (colsend.at[0], cols_buf.at[1], (me_a, left)),
        (colsend.at[1], cols_buf.at[0], (me_a, right)),
    )
    copies = []
    for k, (src, dst, peer) in enumerate(plan):
        copy = pltpu.make_async_remote_copy(
            src, dst, send_sem.at[k], recv_sem.at[k], device_id=peer, device_id_type=MESH)
        copy.start()
        copies.append(copy)
    for copy in copies:
        copy.wait()

    has_up = me_a > 0
    has_down = me_a < atm_n - 1
    has_left = me_o > 0
    has_right = me_o < ocn_n - 1
    lane = lax.broadcasted_iota(jnp.int32, (EDGE, width), 1)
    low_lanes = lane < EDGE
    high_lanes = lane >= width - EDGE
    tail = jnp.zeros((rows_padded - rows - 2 * EDGE, width), jnp.float32)
    middle = jnp.zeros((width - 2 * EDGE, rows_padded), jnp.float32)
    for c in range(chans):
        top = jnp.where(has_up, rows_buf[0, c], 0.0)
        bottom = jnp.where(has_down, rows_buf[1, c], 0.0)
        tall_s[c] = jnp.concatenate([top, x_ref[c], bottom, tail], axis=0)
        from_left = jnp.where(has_left, cols_buf[0, c], 0.0)
        from_right = jnp.where(has_right, cols_buf[1, c], 0.0)
        own = jnp.concatenate([from_right, middle, from_left], axis=0).T
        corner_top = jnp.where(
            low_lanes & (has_up & has_right), rows_buf[3, c],
            jnp.where(high_lanes & (has_up & has_left), rows_buf[2, c], 0.0))
        corner_bottom = jnp.where(
            low_lanes & (has_down & has_right), rows_buf[5, c],
            jnp.where(high_lanes & (has_down & has_left), rows_buf[4, c], 0.0))
        side_s[c] = jnp.concatenate([corner_top, own[:rows], corner_bottom, tail], axis=0)


def exchange_scratch(chans, rows_padded, width):
    return [
        pltpu.VMEM((6, chans, EDGE, width), jnp.float32),
        pltpu.VMEM((2, chans, EDGE, rows_padded), jnp.float32),
        pltpu.VMEM((2, chans, EDGE, rows_padded), jnp.float32),
        pltpu.VMEM((chans, rows_padded, width), jnp.float32),
        pltpu.VMEM((chans, rows_padded, width), jnp.float32),
        pltpu.SemaphoreType.DMA((8,)),
        pltpu.SemaphoreType.DMA((8,)),
    ]


def stencil_sum(state):
    rows_padded, lanes = state.shape
    return (
        pltpu.roll(state, rows_padded - 1, 0)
        + pltpu.roll(state, 1, 0)
        + pltpu.roll(state, lanes - 1, 1)
        + pltpu.roll(state, 1, 1)
    )


def smooth_kernel(sizes, x_ref, out_ref, tall_out, side_out, *scratch):
    rows_buf, cols_buf, colsend, tall_s, side_s, send_sem, recv_sem = scratch
    exchange(sizes, x_ref, rows_buf, cols_buf, colsend, tall_s, side_s, send_sem, recv_sem)
    rows, width = out_ref.shape[1], out_ref.shape[2]
    kept = tall_out.shape[0]
    tall_out[...] = tall_s[kept:]
    side_out[...] = side_s[kept:]
    for chan in range(out_ref.shape[0]):
        state = jnp.concatenate([tall_s[chan], side_s[chan]], axis=1)
        out_ref[chan] = (0.5 * state + 0.125 * stencil_sum(state))[EDGE : EDGE + rows, :width]


def diffuse_kernel(sizes, x_ref, dtall_ref, dside_ref, out_ref, *scratch):
    rows_buf, cols_buf, colsend, tall_s, side_s, send_sem, recv_sem = scratch
    exchange(sizes, x_ref, rows_buf, cols_buf, colsend, tall_s, side_s, send_sem, recv_sem)
    rows, width = out_ref.shape[1], out_ref.shape[2]
    first = dtall_ref.shape[0] - out_ref.shape[0]
    for chan in range(out_ref.shape[0]):
        state = jnp.concatenate([tall_s[chan], side_s[chan]], axis=1)
        diff = jnp.concatenate([dtall_ref[first + chan], dside_ref[first + chan]], axis=1)
        for iteration in range(ITERS):
            state = state + diff * (stencil_sum(state) - 4.0 * state)
        out_ref[chan] = state[EDGE : EDGE + rows, :width]


def smooth_call(sizes, both, chans, rows_padded):
    total, rows, width = both.shape
    vmem = pl.BlockSpec(memory_space=pltpu.VMEM)
    return pl.pallas_call(
        functools.partial(smooth_kernel, sizes),
        out_shape=(
            jax.ShapeDtypeStruct((chans, rows, width), jnp.float32),
            jax.ShapeDtypeStruct((total - chans, rows_padded, width), jnp.float32),
            jax.ShapeDtypeStruct((total - chans, rows_padded, width), jnp.float32),
        ),
        in_specs=[vmem],
        out_specs=(vmem, vmem, vmem),
        scratch_shapes=exchange_scratch(total, rows_padded, width),
        compiler_params=pltpu.CompilerParams(collective_id=0, has_side_effects=True),
    )(both)


def diffuse_call(sizes, forced, dtall, dside):
    chans, rows, width = forced.shape
    rows_padded = dtall.shape[1]
    vmem = pl.BlockSpec(memory_space=pltpu.VMEM)
    return pl.pallas_call(
        functools.partial(diffuse_kernel, sizes),
        out_shape=jax.ShapeDtypeStruct((chans, rows, width), jnp.float32),
        in_specs=[vmem] * 3,
        out_specs=vmem,
        scratch_shapes=exchange_scratch(chans, rows_padded, width),
        compiler_params=pltpu.CompilerParams(collective_id=1, has_side_effects=True),
    )(forced, dtall, dside)


def per_device(
    atm_state,
    diffusivity,
    ocean_state,
    land_mask,
    intersection_area,
    intersection_seg,
    intersection_dest,
    intersection_row,
):
    atm_count = lax.axis_size("atm")
    ocn_count = lax.axis_size("ocn")
    devices = atm_count * ocn_count
    row_count, chan_count, seg_width = atm_state.shape
    seg_count = ocean_state.shape[0]
    ov_rows = intersection_seg.shape[0]
    capacity = max(2, 2 * ov_rows // devices)
    slots = devices * capacity

    target = intersection_dest[:, 0]
    matches = (target[:, None] == jnp.arange(devices, dtype=jnp.int32)[None, :]).astype(jnp.int32)
    position = jnp.sum((jnp.cumsum(matches, axis=0) - matches) * matches, axis=1)
    slot_index = target * capacity + position
    slot_pick = (
        jnp.arange(slots, dtype=jnp.int32)[:, None] == slot_index[None, :]
    ).astype(jnp.bfloat16)
    seg_pick = (
        intersection_seg[:, None] == jnp.arange(seg_count, dtype=jnp.int32)[None, :]
    ).astype(jnp.bfloat16)
    slot_seg = jnp.dot(slot_pick, seg_pick, preferred_element_type=jnp.float32)
    plane = chan_count * seg_width
    out_ocean = select_rows(slot_seg, ocean_state.reshape(seg_count, plane))
    out_mask = select_rows(slot_seg, land_mask.astype(jnp.float32), None)
    row_high = (intersection_row // 32).astype(jnp.bfloat16)
    row_low = (intersection_row % 32).astype(jnp.bfloat16)
    row_parts = jnp.concatenate(
        [jnp.broadcast_to(row_high[:, None], (ov_rows, seg_width)),
         jnp.broadcast_to(row_low[:, None], (ov_rows, seg_width))], axis=1
    )
    out_rows = jnp.dot(slot_pick, row_parts, preferred_element_type=jnp.float32)
    out_label = 32.0 * out_rows[:, :seg_width] + out_rows[:, seg_width:]
    out_area = select_rows(slot_pick.astype(jnp.float32), intersection_area)
    out_weight = out_area * out_mask
    slot_label = out_label[:, 0].astype(jnp.int32).reshape(devices, capacity)
    in_labels = lax.all_to_all(
        slot_label, ("atm", "ocn"), split_axis=0, concat_axis=0, tiled=True).reshape(slots)
    outgoing = jnp.concatenate([out_ocean, out_weight], axis=1)
    incoming = lax.all_to_all(outgoing, ("atm", "ocn"), split_axis=0, concat_axis=0, tiled=True)

    atm_planes = jnp.transpose(atm_state, (1, 0, 2))
    both = jnp.concatenate([atm_planes, jnp.transpose(diffusivity, (1, 0, 2))], axis=0)
    sizes = (atm_count, ocn_count)
    rows_padded = -(-(row_count + 2 * EDGE) // 128) * 128
    smoothed, dtall, dside = smooth_call(sizes, both, chan_count, rows_padded)

    row_pick = (
        jnp.arange(row_count, dtype=jnp.int32)[:, None] == in_labels[None, :]
    ).astype(jnp.float32)
    pick_rows = row_pick.T
    air = [jnp.dot(pick_rows, smoothed[c], precision=HIGHEST, preferred_element_type=jnp.float32)
           for c in range(chan_count)]
    ocean = [incoming[:, c * seg_width : (c + 1) * seg_width] for c in range(chan_count)]
    in_weight = incoming[:, plane : plane + seg_width]
    wind_east = air[1] - ocean[1]
    wind_north = air[2] - ocean[2]
    wind_speed = jnp.sqrt(wind_east * wind_east + wind_north * wind_north + 0.5)
    temp_gap = ocean[0] - air[0]
    factor = 1.0 + 0.5 * jnp.tanh(temp_gap / wind_speed)
    weighted = [
        in_weight * (0.8 * factor * wind_speed * temp_gap),
        in_weight * (0.6 * factor * wind_speed * wind_east),
        in_weight * (0.6 * factor * wind_speed * wind_north),
    ]
    returned = lax.all_to_all(
        jnp.concatenate(weighted, axis=1), ("atm", "ocn"), split_axis=0, concat_axis=0, tiled=True
    )
    signs = (1.0, -1.0, -1.0)
    forced = jnp.stack(
        [atm_planes[c] + signs[c] * jnp.dot(row_pick, weighted[c], precision=HIGHEST,
                                             preferred_element_type=jnp.float32)
         for c in range(chan_count)]
    )
    current = diffuse_call(sizes, forced, dtall, dside)
    current, returned = lax.optimization_barrier((current, returned))
    seg_of_slot = slot_seg.T.astype(jnp.bfloat16)
    ocean_flux = pick_dot(seg_of_slot, returned).reshape(seg_count, chan_count, seg_width)
    return (jnp.transpose(current, (1, 0, 2)), ocean_flux)


def solution(mesh):
    placed = (
        P("atm", None, "ocn"),
        P("atm", None, "ocn"),
        P(("atm", "ocn"), None, None),
        P(("atm", "ocn"), None),
        P(("atm", "ocn"), None),
        P(("atm", "ocn")),
        P(("atm", "ocn"), None),
        P(("atm", "ocn")),
    )
    return jax.shard_map(
        per_device,
        mesh=mesh,
        in_specs=placed,
        out_specs=(P("atm", None, "ocn"), P(("atm", "ocn"), None, None)),
        check_vma=False,
    )
```

```python
import functools

import jax
import jax.numpy as jnp
from jax import lax
from jax.experimental import pallas as pl
from jax.experimental.pallas import tpu as pltpu
from jax.sharding import PartitionSpec as P

ITERS = 3
HIGHEST = lax.Precision.HIGHEST
HALO = ITERS
EDGE = 8


def with_halo(block, sides, width):
    for axis, dim in sides:
        count = lax.axis_size(axis)
        forward = [(i, i + 1) for i in range(count - 1)]
        backward = [(target, source) for source, target in forward]
        low = lax.ppermute(
            lax.slice_in_dim(block, block.shape[dim] - width, None, axis=dim), axis, forward
        )
        high = lax.ppermute(lax.slice_in_dim(block, 0, width, axis=dim), axis, backward)
        block = jnp.concatenate([low, block, high], axis=dim)
    return block


def beside_all(padded):
    return padded[2:, :, 1:-1] + padded[:-2, :, 1:-1] + padded[1:-1, :, 2:] + padded[1:-1, :, :-2]


def fluxes(ocean_part, air_part):
    wind_east = air_part[:, 1] - ocean_part[:, 1]
    wind_north = air_part[:, 2] - ocean_part[:, 2]
    wind_speed = jnp.sqrt(wind_east * wind_east + wind_north * wind_north + 0.5)
    temp_gap = ocean_part[:, 0] - air_part[:, 0]
    factor = 1.0 + 0.5 * jnp.tanh(temp_gap / wind_speed)
    return jnp.stack(
        [
            0.8 * factor * wind_speed * temp_gap,
            0.6 * factor * wind_speed * wind_east,
            0.6 * factor * wind_speed * wind_north,
        ],
        axis=1,
    )


def pick_dot(pick, values):
    parts = []
    rest = values
    for part in range(3):
        high = lax.reduce_precision(rest, exponent_bits=8, mantissa_bits=7)
        parts.append(high.astype(jnp.bfloat16))
        rest = rest - high
    total = None
    for part in parts:
        term = jnp.dot(pick, part, preferred_element_type=jnp.float32)
        total = term if total is None else total + term
    return total


def select_rows(chosen, values, precision=HIGHEST):
    flat = values.reshape(values.shape[0], -1)
    total = jnp.dot(chosen, flat, precision=precision, preferred_element_type=jnp.float32)
    return total.reshape((chosen.shape[0],) + values.shape[1:])


MESH = pl.DeviceIdType.MESH


def exchange(sizes, x_ref, rows_buf, cols_buf, colsend, tall_s, side_s, send_sem, recv_sem):
    atm_n, ocn_n = sizes
    chans, rows, width = x_ref.shape
    rows_padded = tall_s.shape[1]
    me_a = lax.axis_index("atm")
    me_o = lax.axis_index("ocn")
    up = lax.rem(me_a + atm_n - 1, atm_n)
    down = lax.rem(me_a + 1, atm_n)
    left = lax.rem(me_o + ocn_n - 1, ocn_n)
    right = lax.rem(me_o + 1, ocn_n)
    peers = ((up, me_o), (down, me_o), (me_a, left), (me_a, right),
             (up, left), (up, right), (down, left), (down, right))
    barrier = pltpu.get_barrier_semaphore()
    for peer in peers:
        pl.semaphore_signal(barrier, 1, device_id=peer, device_id_type=MESH)
    pl.semaphore_wait(barrier, len(peers))

    spare = jnp.zeros((rows_padded - rows, width), jnp.float32)
    for c in range(chans):
        flipped = jnp.concatenate([x_ref[c], spare], axis=0).T
        colsend[0, c] = flipped[:EDGE]
        colsend[1, c] = flipped[width - EDGE :]

    last = x_ref.at[:, rows - EDGE :, :]
    first = x_ref.at[:, :EDGE, :]
    plan = (
        (last, rows_buf.at[0], (down, me_o)),
        (first, rows_buf.at[1], (up, me_o)),
        (last, rows_buf.at[2], (down, right)),
        (last, rows_buf.at[3], (down, left)),
        (first, rows_buf.at[4], (up, right)),
        (first, rows_buf.at[5], (up, left)),
        (colsend.at[0], cols_buf.at[1], (me_a, left)),
        (colsend.at[1], cols_buf.at[0], (me_a, right)),
    )
    copies = []
    for k, (src, dst, peer) in enumerate(plan):
        copy = pltpu.make_async_remote_copy(
            src, dst, send_sem.at[k], recv_sem.at[k], device_id=peer, device_id_type=MESH)
        copy.start()
        copies.append(copy)
    for copy in copies:
        copy.wait()

    has_up = me_a > 0
    has_down = me_a < atm_n - 1
    has_left = me_o > 0
    has_right = me_o < ocn_n - 1
    lane = lax.broadcasted_iota(jnp.int32, (EDGE, width), 1)
    low_lanes = lane < EDGE
    high_lanes = lane >= width - EDGE
    tail = jnp.zeros((rows_padded - rows - 2 * EDGE, width), jnp.float32)
    middle = jnp.zeros((width - 2 * EDGE, rows_padded), jnp.float32)
    for c in range(chans):
        top = jnp.where(has_up, rows_buf[0, c], 0.0)
        bottom = jnp.where(has_down, rows_buf[1, c], 0.0)
        tall_s[c] = jnp.concatenate([top, x_ref[c], bottom, tail], axis=0)
        from_left = jnp.where(has_left, cols_buf[0, c], 0.0)
        from_right = jnp.where(has_right, cols_buf[1, c], 0.0)
        own = jnp.concatenate([from_right, middle, from_left], axis=0).T
        corner_top = jnp.where(
            low_lanes & (has_up & has_right), rows_buf[3, c],
            jnp.where(high_lanes & (has_up & has_left), rows_buf[2, c], 0.0))
        corner_bottom = jnp.where(
            low_lanes & (has_down & has_right), rows_buf[5, c],
            jnp.where(high_lanes & (has_down & has_left), rows_buf[4, c], 0.0))
        side_s[c] = jnp.concatenate([corner_top, own[:rows], corner_bottom, tail], axis=0)


def exchange_scratch(chans, rows_padded, width):
    return [
        pltpu.VMEM((6, chans, EDGE, width), jnp.float32),
        pltpu.VMEM((2, chans, EDGE, rows_padded), jnp.float32),
        pltpu.VMEM((2, chans, EDGE, rows_padded), jnp.float32),
        pltpu.VMEM((chans, rows_padded, width), jnp.float32),
        pltpu.VMEM((chans, rows_padded, width), jnp.float32),
        pltpu.SemaphoreType.DMA((8,)),
        pltpu.SemaphoreType.DMA((8,)),
    ]


def stencil_sum(state):
    rows_padded, lanes = state.shape
    return (
        pltpu.roll(state, rows_padded - 1, 0)
        + pltpu.roll(state, 1, 0)
        + pltpu.roll(state, lanes - 1, 1)
        + pltpu.roll(state, 1, 1)
    )


def smooth_kernel(sizes, x_ref, out_ref, tall_out, side_out, *scratch):
    rows_buf, cols_buf, colsend, tall_s, side_s, send_sem, recv_sem = scratch
    exchange(sizes, x_ref, rows_buf, cols_buf, colsend, tall_s, side_s, send_sem, recv_sem)
    kept = tall_out.shape[0]
    rows, width = out_ref.shape[0], out_ref.shape[1] // kept
    tall_out[...] = tall_s[kept:]
    side_out[...] = side_s[kept:]
    for chan in range(kept):
        state = jnp.concatenate([tall_s[chan], side_s[chan]], axis=1)
        done = 0.5 * state + 0.125 * stencil_sum(state)
        out_ref[:, chan * width : (chan + 1) * width] = done[EDGE : EDGE + rows, :width]


def diffuse_kernel(sizes, x_ref, dtall_ref, dside_ref, out_ref, *scratch):
    rows_buf, cols_buf, colsend, tall_s, side_s, send_sem, recv_sem = scratch
    exchange(sizes, x_ref, rows_buf, cols_buf, colsend, tall_s, side_s, send_sem, recv_sem)
    rows, width = out_ref.shape[1], out_ref.shape[2]
    first = dtall_ref.shape[0] - out_ref.shape[0]
    for chan in range(out_ref.shape[0]):
        state = jnp.concatenate([tall_s[chan], side_s[chan]], axis=1)
        diff = jnp.concatenate([dtall_ref[first + chan], dside_ref[first + chan]], axis=1)
        for iteration in range(ITERS):
            state = state + diff * (stencil_sum(state) - 4.0 * state)
        out_ref[chan] = state[EDGE : EDGE + rows, :width]


def smooth_call(sizes, both, chans, rows_padded):
    total, rows, width = both.shape
    vmem = pl.BlockSpec(memory_space=pltpu.VMEM)
    return pl.pallas_call(
        functools.partial(smooth_kernel, sizes),
        out_shape=(
            jax.ShapeDtypeStruct((rows, chans * width), jnp.float32),
            jax.ShapeDtypeStruct((total - chans, rows_padded, width), jnp.float32),
            jax.ShapeDtypeStruct((total - chans, rows_padded, width), jnp.float32),
        ),
        in_specs=[vmem],
        out_specs=(vmem, vmem, vmem),
        scratch_shapes=exchange_scratch(total, rows_padded, width),
        compiler_params=pltpu.CompilerParams(collective_id=0, has_side_effects=True),
    )(both)


def diffuse_call(sizes, forced, dtall, dside):
    chans, rows, width = forced.shape
    rows_padded = dtall.shape[1]
    vmem = pl.BlockSpec(memory_space=pltpu.VMEM)
    return pl.pallas_call(
        functools.partial(diffuse_kernel, sizes),
        out_shape=jax.ShapeDtypeStruct((chans, rows, width), jnp.float32),
        in_specs=[vmem] * 3,
        out_specs=vmem,
        scratch_shapes=exchange_scratch(chans, rows_padded, width),
        compiler_params=pltpu.CompilerParams(collective_id=1, has_side_effects=True),
    )(forced, dtall, dside)


def per_device(
    atm_state,
    diffusivity,
    ocean_state,
    land_mask,
    intersection_area,
    intersection_seg,
    intersection_dest,
    intersection_row,
):
    atm_count = lax.axis_size("atm")
    ocn_count = lax.axis_size("ocn")
    devices = atm_count * ocn_count
    row_count, chan_count, seg_width = atm_state.shape
    seg_count = ocean_state.shape[0]
    ov_rows = intersection_seg.shape[0]
    capacity = max(2, 2 * ov_rows // devices)
    slots = devices * capacity

    target = intersection_dest[:, 0]
    matches = (target[:, None] == jnp.arange(devices, dtype=jnp.int32)[None, :]).astype(jnp.int32)
    position = jnp.sum((jnp.cumsum(matches, axis=0) - matches) * matches, axis=1)
    slot_index = target * capacity + position
    slot_pick = (
        jnp.arange(slots, dtype=jnp.int32)[:, None] == slot_index[None, :]
    ).astype(jnp.bfloat16)
    seg_pick = (
        intersection_seg[:, None] == jnp.arange(seg_count, dtype=jnp.int32)[None, :]
    ).astype(jnp.bfloat16)
    slot_seg = jnp.dot(slot_pick, seg_pick, preferred_element_type=jnp.float32)
    plane = chan_count * seg_width
    out_ocean = select_rows(slot_seg, ocean_state.reshape(seg_count, plane))
    out_mask = select_rows(slot_seg, land_mask.astype(jnp.float32), None)
    row_high = (intersection_row // 32).astype(jnp.bfloat16)
    row_low = (intersection_row % 32).astype(jnp.bfloat16)
    row_parts = jnp.concatenate(
        [jnp.broadcast_to(row_high[:, None], (ov_rows, seg_width)),
         jnp.broadcast_to(row_low[:, None], (ov_rows, seg_width))], axis=1
    )
    out_rows = jnp.dot(slot_pick, row_parts, preferred_element_type=jnp.float32)
    out_label = 32.0 * out_rows[:, :seg_width] + out_rows[:, seg_width:]
    out_area = select_rows(slot_pick.astype(jnp.float32), intersection_area)
    out_weight = out_area * out_mask
    outgoing = jnp.concatenate([out_ocean, out_weight, out_label], axis=1)
    incoming = lax.all_to_all(outgoing, ("atm", "ocn"), split_axis=0, concat_axis=0, tiled=True)

    atm_planes = jnp.transpose(atm_state, (1, 0, 2))
    both = jnp.concatenate([atm_planes, jnp.transpose(diffusivity, (1, 0, 2))], axis=0)
    sizes = (atm_count, ocn_count)
    rows_padded = -(-(row_count + 2 * EDGE) // 128) * 128
    smoothed, dtall, dside = smooth_call(sizes, both, chan_count, rows_padded)

    in_labels = jnp.max(incoming[:, plane + seg_width :], axis=1).astype(jnp.int32)
    row_pick = (
        jnp.arange(row_count, dtype=jnp.int32)[:, None] == in_labels[None, :]
    ).astype(jnp.float32)
    pick_rows = row_pick.T
    air_all = jnp.dot(pick_rows, smoothed, precision=HIGHEST, preferred_element_type=jnp.float32)
    air = [air_all[:, c * seg_width : (c + 1) * seg_width] for c in range(chan_count)]
    ocean = [incoming[:, c * seg_width : (c + 1) * seg_width] for c in range(chan_count)]
    in_weight = incoming[:, plane : plane + seg_width]
    wind_east = air[1] - ocean[1]
    wind_north = air[2] - ocean[2]
    wind_speed = jnp.sqrt(wind_east * wind_east + wind_north * wind_north + 0.5)
    temp_gap = ocean[0] - air[0]
    factor = 1.0 + 0.5 * jnp.tanh(temp_gap / wind_speed)
    weighted = [
        in_weight * (0.8 * factor * wind_speed * temp_gap),
        in_weight * (0.6 * factor * wind_speed * wind_east),
        in_weight * (0.6 * factor * wind_speed * wind_north),
    ]
    returned = lax.all_to_all(
        jnp.concatenate(weighted, axis=1), ("atm", "ocn"), split_axis=0, concat_axis=0, tiled=True
    )
    signs = (1.0, -1.0, -1.0)
    sent = jnp.concatenate(weighted, axis=1)
    air_sum = jnp.dot(row_pick, sent, precision=HIGHEST, preferred_element_type=jnp.float32)
    forced = jnp.stack(
        [atm_planes[c] + signs[c] * air_sum[:, c * seg_width : (c + 1) * seg_width]
         for c in range(chan_count)]
    )
    current = diffuse_call(sizes, forced, dtall, dside)
    current, returned = lax.optimization_barrier((current, returned))
    seg_of_slot = slot_seg.T.astype(jnp.bfloat16)
    ocean_flux = pick_dot(seg_of_slot, returned).reshape(seg_count, chan_count, seg_width)
    return (jnp.transpose(current, (1, 0, 2)), ocean_flux)


def solution(mesh):
    placed = (
        P("atm", None, "ocn"),
        P("atm", None, "ocn"),
        P(("atm", "ocn"), None, None),
        P(("atm", "ocn"), None),
        P(("atm", "ocn"), None),
        P(("atm", "ocn")),
        P(("atm", "ocn"), None),
        P(("atm", "ocn")),
    )
    return jax.shard_map(
        per_device,
        mesh=mesh,
        in_specs=placed,
        out_specs=(P("atm", None, "ocn"), P(("atm", "ocn"), None, None)),
        check_vma=False,
    )
```

```python
import functools

import jax
import jax.numpy as jnp
from jax import lax
from jax.experimental import pallas as pl
from jax.experimental.pallas import tpu as pltpu
from jax.sharding import PartitionSpec as P

ITERS = 3
HIGHEST = lax.Precision.HIGHEST
HALO = ITERS
EDGE = 8


def with_halo(block, sides, width):
    for axis, dim in sides:
        count = lax.axis_size(axis)
        forward = [(i, i + 1) for i in range(count - 1)]
        backward = [(target, source) for source, target in forward]
        low = lax.ppermute(
            lax.slice_in_dim(block, block.shape[dim] - width, None, axis=dim), axis, forward
        )
        high = lax.ppermute(lax.slice_in_dim(block, 0, width, axis=dim), axis, backward)
        block = jnp.concatenate([low, block, high], axis=dim)
    return block


def beside_all(padded):
    return padded[2:, :, 1:-1] + padded[:-2, :, 1:-1] + padded[1:-1, :, 2:] + padded[1:-1, :, :-2]


def fluxes(ocean_part, air_part):
    wind_east = air_part[:, 1] - ocean_part[:, 1]
    wind_north = air_part[:, 2] - ocean_part[:, 2]
    wind_speed = jnp.sqrt(wind_east * wind_east + wind_north * wind_north + 0.5)
    temp_gap = ocean_part[:, 0] - air_part[:, 0]
    factor = 1.0 + 0.5 * jnp.tanh(temp_gap / wind_speed)
    return jnp.stack(
        [
            0.8 * factor * wind_speed * temp_gap,
            0.6 * factor * wind_speed * wind_east,
            0.6 * factor * wind_speed * wind_north,
        ],
        axis=1,
    )


def pick_dot(pick, values):
    parts = []
    rest = values
    for part in range(3):
        high = lax.reduce_precision(rest, exponent_bits=8, mantissa_bits=7)
        parts.append(high.astype(jnp.bfloat16))
        rest = rest - high
    total = None
    for part in parts:
        term = jnp.dot(pick, part, preferred_element_type=jnp.float32)
        total = term if total is None else total + term
    return total


def select_rows(chosen, values, precision=HIGHEST):
    flat = values.reshape(values.shape[0], -1)
    total = jnp.dot(chosen, flat, precision=precision, preferred_element_type=jnp.float32)
    return total.reshape((chosen.shape[0],) + values.shape[1:])


MESH = pl.DeviceIdType.MESH


def exchange(sizes, x_ref, rows_buf, cols_buf, colsend, tall_s, side_s, send_sem, recv_sem):
    atm_n, ocn_n = sizes
    chans, rows, width = x_ref.shape
    rows_padded = tall_s.shape[1]
    me_a = lax.axis_index("atm")
    me_o = lax.axis_index("ocn")
    up = lax.rem(me_a + atm_n - 1, atm_n)
    down = lax.rem(me_a + 1, atm_n)
    left = lax.rem(me_o + ocn_n - 1, ocn_n)
    right = lax.rem(me_o + 1, ocn_n)
    peers = ((up, me_o), (down, me_o), (me_a, left), (me_a, right),
             (up, left), (up, right), (down, left), (down, right))
    barrier = pltpu.get_barrier_semaphore()
    for peer in peers:
        pl.semaphore_signal(barrier, 1, device_id=peer, device_id_type=MESH)
    pl.semaphore_wait(barrier, len(peers))

    spare = jnp.zeros((rows_padded - rows, width), jnp.float32)
    for c in range(chans):
        flipped = jnp.concatenate([x_ref[c], spare], axis=0).T
        colsend[0, c] = flipped[:EDGE]
        colsend[1, c] = flipped[width - EDGE :]

    last = x_ref.at[:, rows - EDGE :, :]
    first = x_ref.at[:, :EDGE, :]
    plan = (
        (last, rows_buf.at[0], (down, me_o)),
        (first, rows_buf.at[1], (up, me_o)),
        (last, rows_buf.at[2], (down, right)),
        (last, rows_buf.at[3], (down, left)),
        (first, rows_buf.at[4], (up, right)),
        (first, rows_buf.at[5], (up, left)),
        (colsend.at[0], cols_buf.at[1], (me_a, left)),
        (colsend.at[1], cols_buf.at[0], (me_a, right)),
    )
    copies = []
    for k, (src, dst, peer) in enumerate(plan):
        copy = pltpu.make_async_remote_copy(
            src, dst, send_sem.at[k], recv_sem.at[k], device_id=peer, device_id_type=MESH)
        copy.start()
        copies.append(copy)
    for copy in copies:
        copy.wait()

    has_up = me_a > 0
    has_down = me_a < atm_n - 1
    has_left = me_o > 0
    has_right = me_o < ocn_n - 1
    lane = lax.broadcasted_iota(jnp.int32, (EDGE, width), 1)
    low_lanes = lane < EDGE
    high_lanes = lane >= width - EDGE
    tail = jnp.zeros((rows_padded - rows - 2 * EDGE, width), jnp.float32)
    middle = jnp.zeros((width - 2 * EDGE, rows_padded), jnp.float32)
    for c in range(chans):
        top = jnp.where(has_up, rows_buf[0, c], 0.0)
        bottom = jnp.where(has_down, rows_buf[1, c], 0.0)
        tall_s[c] = jnp.concatenate([top, x_ref[c], bottom, tail], axis=0)
        from_left = jnp.where(has_left, cols_buf[0, c], 0.0)
        from_right = jnp.where(has_right, cols_buf[1, c], 0.0)
        own = jnp.concatenate([from_right, middle, from_left], axis=0).T
        corner_top = jnp.where(
            low_lanes & (has_up & has_right), rows_buf[3, c],
            jnp.where(high_lanes & (has_up & has_left), rows_buf[2, c], 0.0))
        corner_bottom = jnp.where(
            low_lanes & (has_down & has_right), rows_buf[5, c],
            jnp.where(high_lanes & (has_down & has_left), rows_buf[4, c], 0.0))
        side_s[c] = jnp.concatenate([corner_top, own[:rows], corner_bottom, tail], axis=0)


def exchange_scratch(chans, rows_padded, width):
    return [
        pltpu.VMEM((6, chans, EDGE, width), jnp.float32),
        pltpu.VMEM((2, chans, EDGE, rows_padded), jnp.float32),
        pltpu.VMEM((2, chans, EDGE, rows_padded), jnp.float32),
        pltpu.VMEM((chans, rows_padded, width), jnp.float32),
        pltpu.VMEM((chans, rows_padded, width), jnp.float32),
        pltpu.SemaphoreType.DMA((8,)),
        pltpu.SemaphoreType.DMA((8,)),
    ]


def stencil_sum(state):
    rows_padded, lanes = state.shape
    return (
        pltpu.roll(state, rows_padded - 1, 0)
        + pltpu.roll(state, 1, 0)
        + pltpu.roll(state, lanes - 1, 1)
        + pltpu.roll(state, 1, 1)
    )


def smooth_kernel(sizes, x_ref, out_ref, tall_out, side_out, *scratch):
    rows_buf, cols_buf, colsend, tall_s, side_s, send_sem, recv_sem = scratch
    exchange(sizes, x_ref, rows_buf, cols_buf, colsend, tall_s, side_s, send_sem, recv_sem)
    kept = tall_out.shape[0]
    rows, width = out_ref.shape[0], out_ref.shape[1] // kept
    tall_out[...] = tall_s[kept:]
    side_out[...] = side_s[kept:]
    for chan in range(kept):
        state = jnp.concatenate([tall_s[chan], side_s[chan]], axis=1)
        done = 0.5 * state + 0.125 * stencil_sum(state)
        out_ref[:, chan * width : (chan + 1) * width] = done[EDGE : EDGE + rows, :width]


def diffuse_kernel(sizes, x_ref, dtall_ref, dside_ref, out_ref, *scratch):
    rows_buf, cols_buf, colsend, tall_s, side_s, send_sem, recv_sem = scratch
    exchange(sizes, x_ref, rows_buf, cols_buf, colsend, tall_s, side_s, send_sem, recv_sem)
    rows, width = out_ref.shape[1], out_ref.shape[2]
    first = dtall_ref.shape[0] - out_ref.shape[0]
    for chan in range(out_ref.shape[0]):
        state = jnp.concatenate([tall_s[chan], side_s[chan]], axis=1)
        diff = jnp.concatenate([dtall_ref[first + chan], dside_ref[first + chan]], axis=1)
        keep = 1.0 - 4.0 * diff
        for iteration in range(ITERS):
            state = state * keep + diff * stencil_sum(state)
        out_ref[chan] = state[EDGE : EDGE + rows, :width]


def smooth_call(sizes, both, chans, rows_padded):
    total, rows, width = both.shape
    vmem = pl.BlockSpec(memory_space=pltpu.VMEM)
    return pl.pallas_call(
        functools.partial(smooth_kernel, sizes),
        out_shape=(
            jax.ShapeDtypeStruct((rows, chans * width), jnp.float32),
            jax.ShapeDtypeStruct((total - chans, rows_padded, width), jnp.float32),
            jax.ShapeDtypeStruct((total - chans, rows_padded, width), jnp.float32),
        ),
        in_specs=[vmem],
        out_specs=(vmem, vmem, vmem),
        scratch_shapes=exchange_scratch(total, rows_padded, width),
        compiler_params=pltpu.CompilerParams(collective_id=0, has_side_effects=True),
    )(both)


def diffuse_call(sizes, forced, dtall, dside):
    chans, rows, width = forced.shape
    rows_padded = dtall.shape[1]
    vmem = pl.BlockSpec(memory_space=pltpu.VMEM)
    return pl.pallas_call(
        functools.partial(diffuse_kernel, sizes),
        out_shape=jax.ShapeDtypeStruct((chans, rows, width), jnp.float32),
        in_specs=[vmem] * 3,
        out_specs=vmem,
        scratch_shapes=exchange_scratch(chans, rows_padded, width),
        compiler_params=pltpu.CompilerParams(collective_id=1, has_side_effects=True),
    )(forced, dtall, dside)


def per_device(
    atm_state,
    diffusivity,
    ocean_state,
    land_mask,
    intersection_area,
    intersection_seg,
    intersection_dest,
    intersection_row,
):
    atm_count = lax.axis_size("atm")
    ocn_count = lax.axis_size("ocn")
    devices = atm_count * ocn_count
    row_count, chan_count, seg_width = atm_state.shape
    seg_count = ocean_state.shape[0]
    ov_rows = intersection_seg.shape[0]
    capacity = max(2, 2 * ov_rows // devices)
    slots = devices * capacity

    target = intersection_dest[:, 0]
    matches = (target[:, None] == jnp.arange(devices, dtype=jnp.int32)[None, :]).astype(jnp.int32)
    position = jnp.sum((jnp.cumsum(matches, axis=0) - matches) * matches, axis=1)
    slot_index = target * capacity + position
    slot_pick = (
        jnp.arange(slots, dtype=jnp.int32)[:, None] == slot_index[None, :]
    ).astype(jnp.bfloat16)
    seg_pick = (
        intersection_seg[:, None] == jnp.arange(seg_count, dtype=jnp.int32)[None, :]
    ).astype(jnp.bfloat16)
    slot_seg = jnp.dot(slot_pick, seg_pick, preferred_element_type=jnp.float32)
    plane = chan_count * seg_width
    out_ocean = select_rows(slot_seg, ocean_state.reshape(seg_count, plane))
    out_mask = select_rows(slot_seg, land_mask.astype(jnp.float32), None)
    row_high = (intersection_row // 32).astype(jnp.bfloat16)
    row_low = (intersection_row % 32).astype(jnp.bfloat16)
    row_parts = jnp.concatenate(
        [jnp.broadcast_to(row_high[:, None], (ov_rows, seg_width)),
         jnp.broadcast_to(row_low[:, None], (ov_rows, seg_width))], axis=1
    )
    out_rows = jnp.dot(slot_pick, row_parts, preferred_element_type=jnp.float32)
    out_label = 32.0 * out_rows[:, :seg_width] + out_rows[:, seg_width:]
    out_area = select_rows(slot_pick.astype(jnp.float32), intersection_area)
    out_weight = out_area * out_mask
    outgoing = jnp.concatenate([out_ocean, out_weight, out_label], axis=1)
    incoming = lax.all_to_all(outgoing, ("atm", "ocn"), split_axis=0, concat_axis=0, tiled=True)

    atm_planes = jnp.transpose(atm_state, (1, 0, 2))
    both = jnp.concatenate([atm_planes, jnp.transpose(diffusivity, (1, 0, 2))], axis=0)
    sizes = (atm_count, ocn_count)
    rows_padded = -(-(row_count + 2 * EDGE) // 128) * 128
    smoothed, dtall, dside = smooth_call(sizes, both, chan_count, rows_padded)

    in_labels = jnp.max(incoming[:, plane + seg_width :], axis=1).astype(jnp.int32)
    row_pick = (
        jnp.arange(row_count, dtype=jnp.int32)[:, None] == in_labels[None, :]
    ).astype(jnp.float32)
    pick_rows = row_pick.T
    air_all = jnp.dot(pick_rows, smoothed, precision=HIGHEST, preferred_element_type=jnp.float32)
    air = [air_all[:, c * seg_width : (c + 1) * seg_width] for c in range(chan_count)]
    ocean = [incoming[:, c * seg_width : (c + 1) * seg_width] for c in range(chan_count)]
    in_weight = incoming[:, plane : plane + seg_width]
    wind_east = air[1] - ocean[1]
    wind_north = air[2] - ocean[2]
    wind_speed = jnp.sqrt(wind_east * wind_east + wind_north * wind_north + 0.5)
    temp_gap = ocean[0] - air[0]
    factor = 1.0 + 0.5 * jnp.tanh(temp_gap / wind_speed)
    weighted = [
        in_weight * (0.8 * factor * wind_speed * temp_gap),
        in_weight * (0.6 * factor * wind_speed * wind_east),
        in_weight * (0.6 * factor * wind_speed * wind_north),
    ]
    returned = lax.all_to_all(
        jnp.concatenate(weighted, axis=1), ("atm", "ocn"), split_axis=0, concat_axis=0, tiled=True
    )
    signs = (1.0, -1.0, -1.0)
    sent = jnp.concatenate(weighted, axis=1)
    air_sum = jnp.dot(row_pick, sent, precision=HIGHEST, preferred_element_type=jnp.float32)
    forced = jnp.stack(
        [atm_planes[c] + signs[c] * air_sum[:, c * seg_width : (c + 1) * seg_width]
         for c in range(chan_count)]
    )
    current = diffuse_call(sizes, forced, dtall, dside)
    current, returned = lax.optimization_barrier((current, returned))
    seg_of_slot = slot_seg.T.astype(jnp.bfloat16)
    ocean_flux = pick_dot(seg_of_slot, returned).reshape(seg_count, chan_count, seg_width)
    return (jnp.transpose(current, (1, 0, 2)), ocean_flux)


def solution(mesh):
    placed = (
        P("atm", None, "ocn"),
        P("atm", None, "ocn"),
        P(("atm", "ocn"), None, None),
        P(("atm", "ocn"), None),
        P(("atm", "ocn"), None),
        P(("atm", "ocn")),
        P(("atm", "ocn"), None),
        P(("atm", "ocn")),
    )
    return jax.shard_map(
        per_device,
        mesh=mesh,
        in_specs=placed,
        out_specs=(P("atm", None, "ocn"), P(("atm", "ocn"), None, None)),
        check_vma=False,
    )
```

```python
import functools

import jax
import jax.numpy as jnp
from jax import lax
from jax.experimental import pallas as pl
from jax.experimental.pallas import tpu as pltpu
from jax.sharding import PartitionSpec as P

ITERS = 3
HIGHEST = lax.Precision.HIGHEST
HALO = ITERS
EDGE = 8


def with_halo(block, sides, width):
    for axis, dim in sides:
        count = lax.axis_size(axis)
        forward = [(i, i + 1) for i in range(count - 1)]
        backward = [(target, source) for source, target in forward]
        low = lax.ppermute(
            lax.slice_in_dim(block, block.shape[dim] - width, None, axis=dim), axis, forward
        )
        high = lax.ppermute(lax.slice_in_dim(block, 0, width, axis=dim), axis, backward)
        block = jnp.concatenate([low, block, high], axis=dim)
    return block


def beside_all(padded):
    return padded[2:, :, 1:-1] + padded[:-2, :, 1:-1] + padded[1:-1, :, 2:] + padded[1:-1, :, :-2]


def fluxes(ocean_part, air_part):
    wind_east = air_part[:, 1] - ocean_part[:, 1]
    wind_north = air_part[:, 2] - ocean_part[:, 2]
    wind_speed = jnp.sqrt(wind_east * wind_east + wind_north * wind_north + 0.5)
    temp_gap = ocean_part[:, 0] - air_part[:, 0]
    factor = 1.0 + 0.5 * jnp.tanh(temp_gap / wind_speed)
    return jnp.stack(
        [
            0.8 * factor * wind_speed * temp_gap,
            0.6 * factor * wind_speed * wind_east,
            0.6 * factor * wind_speed * wind_north,
        ],
        axis=1,
    )


def pick_dot(pick, values):
    parts = []
    rest = values
    for part in range(3):
        high = lax.reduce_precision(rest, exponent_bits=8, mantissa_bits=7)
        parts.append(high.astype(jnp.bfloat16))
        rest = rest - high
    total = None
    for part in parts:
        term = jnp.dot(pick, part, preferred_element_type=jnp.float32)
        total = term if total is None else total + term
    return total


def select_rows(chosen, values, precision=HIGHEST):
    flat = values.reshape(values.shape[0], -1)
    total = jnp.dot(chosen, flat, precision=precision, preferred_element_type=jnp.float32)
    return total.reshape((chosen.shape[0],) + values.shape[1:])


MESH = pl.DeviceIdType.MESH


def exchange(sizes, x_ref, rows_buf, cols_buf, colsend, tall_s, side_s, send_sem, recv_sem):
    atm_n, ocn_n = sizes
    chans, rows, width = x_ref.shape
    rows_padded = tall_s.shape[1]
    me_a = lax.axis_index("atm")
    me_o = lax.axis_index("ocn")
    up = lax.rem(me_a + atm_n - 1, atm_n)
    down = lax.rem(me_a + 1, atm_n)
    left = lax.rem(me_o + ocn_n - 1, ocn_n)
    right = lax.rem(me_o + 1, ocn_n)
    peers = ((up, me_o), (down, me_o), (me_a, left), (me_a, right),
             (up, left), (up, right), (down, left), (down, right))
    barrier = pltpu.get_barrier_semaphore()
    for peer in peers:
        pl.semaphore_signal(barrier, 1, device_id=peer, device_id_type=MESH)
    pl.semaphore_wait(barrier, len(peers))

    spare = jnp.zeros((rows_padded - rows, width), jnp.float32)
    for c in range(chans):
        flipped = jnp.concatenate([x_ref[c], spare], axis=0).T
        colsend[0, c] = flipped[:EDGE]
        colsend[1, c] = flipped[width - EDGE :]

    last = x_ref.at[:, rows - EDGE :, :]
    first = x_ref.at[:, :EDGE, :]
    plan = (
        (last, rows_buf.at[0], (down, me_o)),
        (first, rows_buf.at[1], (up, me_o)),
        (last, rows_buf.at[2], (down, right)),
        (last, rows_buf.at[3], (down, left)),
        (first, rows_buf.at[4], (up, right)),
        (first, rows_buf.at[5], (up, left)),
        (colsend.at[0], cols_buf.at[1], (me_a, left)),
        (colsend.at[1], cols_buf.at[0], (me_a, right)),
    )
    copies = []
    for k, (src, dst, peer) in enumerate(plan):
        copy = pltpu.make_async_remote_copy(
            src, dst, send_sem.at[k], recv_sem.at[k], device_id=peer, device_id_type=MESH)
        copy.start()
        copies.append(copy)
    for copy in copies:
        copy.wait()

    has_up = me_a > 0
    has_down = me_a < atm_n - 1
    has_left = me_o > 0
    has_right = me_o < ocn_n - 1
    lane = lax.broadcasted_iota(jnp.int32, (EDGE, width), 1)
    low_lanes = lane < EDGE
    high_lanes = lane >= width - EDGE
    tail = jnp.zeros((rows_padded - rows - 2 * EDGE, width), jnp.float32)
    middle = jnp.zeros((width - 2 * EDGE, rows_padded), jnp.float32)
    for c in range(chans):
        top = jnp.where(has_up, rows_buf[0, c], 0.0)
        bottom = jnp.where(has_down, rows_buf[1, c], 0.0)
        tall_s[c] = jnp.concatenate([top, x_ref[c], bottom, tail], axis=0)
        from_left = jnp.where(has_left, cols_buf[0, c], 0.0)
        from_right = jnp.where(has_right, cols_buf[1, c], 0.0)
        own = jnp.concatenate([from_right, middle, from_left], axis=0).T
        corner_top = jnp.where(
            low_lanes & (has_up & has_right), rows_buf[3, c],
            jnp.where(high_lanes & (has_up & has_left), rows_buf[2, c], 0.0))
        corner_bottom = jnp.where(
            low_lanes & (has_down & has_right), rows_buf[5, c],
            jnp.where(high_lanes & (has_down & has_left), rows_buf[4, c], 0.0))
        side_s[c] = jnp.concatenate([corner_top, own[:rows], corner_bottom, tail], axis=0)


def exchange_scratch(chans, rows_padded, width):
    return [
        pltpu.VMEM((6, chans, EDGE, width), jnp.float32),
        pltpu.VMEM((2, chans, EDGE, rows_padded), jnp.float32),
        pltpu.VMEM((2, chans, EDGE, rows_padded), jnp.float32),
        pltpu.VMEM((chans, rows_padded, width), jnp.float32),
        pltpu.VMEM((chans, rows_padded, width), jnp.float32),
        pltpu.SemaphoreType.DMA((8,)),
        pltpu.SemaphoreType.DMA((8,)),
    ]


def stencil_sum(state):
    rows_padded, lanes = state.shape
    return (
        pltpu.roll(state, rows_padded - 1, 0)
        + pltpu.roll(state, 1, 0)
        + pltpu.roll(state, lanes - 1, 1)
        + pltpu.roll(state, 1, 1)
    )


def smooth_kernel(sizes, x_ref, out_ref, tall_out, side_out, *scratch):
    rows_buf, cols_buf, colsend, tall_s, side_s, send_sem, recv_sem = scratch
    exchange(sizes, x_ref, rows_buf, cols_buf, colsend, tall_s, side_s, send_sem, recv_sem)
    kept = tall_out.shape[0]
    rows, width = out_ref.shape[0], out_ref.shape[1] // kept
    tall_out[...] = tall_s[kept:]
    side_out[...] = side_s[kept:]
    for chan in range(kept):
        state = jnp.concatenate([tall_s[chan], side_s[chan]], axis=1)
        done = 0.5 * state + 0.125 * stencil_sum(state)
        out_ref[:, chan * width : (chan + 1) * width] = done[EDGE : EDGE + rows, :width]


SIGNS = (1.0, -1.0, -1.0)


def diffuse_kernel(sizes, both_ref, sum_ref, dtall_ref, dside_ref, out_ref, forced_s, *scratch):
    rows_buf, cols_buf, colsend, tall_s, side_s, send_sem, recv_sem = scratch
    rows, width = out_ref.shape[1], out_ref.shape[2]
    for chan in range(out_ref.shape[0]):
        forced_s[chan] = both_ref[chan] + SIGNS[chan] * sum_ref[:, chan * width : (chan + 1) * width]
    exchange(sizes, forced_s, rows_buf, cols_buf, colsend, tall_s, side_s, send_sem, recv_sem)
    for chan in range(out_ref.shape[0]):
        state = jnp.concatenate([tall_s[chan], side_s[chan]], axis=1)
        diff = jnp.concatenate([dtall_ref[chan], dside_ref[chan]], axis=1)
        for iteration in range(ITERS):
            state = state + diff * (stencil_sum(state) - 4.0 * state)
        out_ref[chan] = state[EDGE : EDGE + rows, :width]


def smooth_call(sizes, both, chans, rows_padded):
    total, rows, width = both.shape
    vmem = pl.BlockSpec(memory_space=pltpu.VMEM)
    return pl.pallas_call(
        functools.partial(smooth_kernel, sizes),
        out_shape=(
            jax.ShapeDtypeStruct((rows, chans * width), jnp.float32),
            jax.ShapeDtypeStruct((total - chans, rows_padded, width), jnp.float32),
            jax.ShapeDtypeStruct((total - chans, rows_padded, width), jnp.float32),
        ),
        in_specs=[vmem],
        out_specs=(vmem, vmem, vmem),
        scratch_shapes=exchange_scratch(total, rows_padded, width),
        compiler_params=pltpu.CompilerParams(collective_id=0, has_side_effects=True),
    )(both)


def diffuse_call(sizes, both, air_sum, dtall, dside):
    chans, rows_padded, width = dtall.shape
    rows = both.shape[1]
    vmem = pl.BlockSpec(memory_space=pltpu.VMEM)
    return pl.pallas_call(
        functools.partial(diffuse_kernel, sizes),
        out_shape=jax.ShapeDtypeStruct((chans, rows, width), jnp.float32),
        in_specs=[vmem] * 4,
        out_specs=vmem,
        scratch_shapes=[pltpu.VMEM((chans, rows, width), jnp.float32)]
        + exchange_scratch(chans, rows_padded, width),
        compiler_params=pltpu.CompilerParams(collective_id=1, has_side_effects=True),
    )(both, air_sum, dtall, dside)


def per_device(
    atm_state,
    diffusivity,
    ocean_state,
    land_mask,
    intersection_area,
    intersection_seg,
    intersection_dest,
    intersection_row,
):
    atm_count = lax.axis_size("atm")
    ocn_count = lax.axis_size("ocn")
    devices = atm_count * ocn_count
    row_count, chan_count, seg_width = atm_state.shape
    seg_count = ocean_state.shape[0]
    ov_rows = intersection_seg.shape[0]
    capacity = max(2, 2 * ov_rows // devices)
    slots = devices * capacity

    target = intersection_dest[:, 0]
    matches = (target[:, None] == jnp.arange(devices, dtype=jnp.int32)[None, :]).astype(jnp.int32)
    position = jnp.sum((jnp.cumsum(matches, axis=0) - matches) * matches, axis=1)
    slot_index = target * capacity + position
    slot_pick = (
        jnp.arange(slots, dtype=jnp.int32)[:, None] == slot_index[None, :]
    ).astype(jnp.bfloat16)
    seg_pick = (
        intersection_seg[:, None] == jnp.arange(seg_count, dtype=jnp.int32)[None, :]
    ).astype(jnp.bfloat16)
    slot_seg = jnp.dot(slot_pick, seg_pick, preferred_element_type=jnp.float32)
    plane = chan_count * seg_width
    out_ocean = select_rows(slot_seg, ocean_state.reshape(seg_count, plane))
    out_mask = select_rows(slot_seg, land_mask.astype(jnp.float32), None)
    row_high = (intersection_row // 32).astype(jnp.bfloat16)
    row_low = (intersection_row % 32).astype(jnp.bfloat16)
    row_parts = jnp.concatenate(
        [jnp.broadcast_to(row_high[:, None], (ov_rows, seg_width)),
         jnp.broadcast_to(row_low[:, None], (ov_rows, seg_width))], axis=1
    )
    out_rows = jnp.dot(slot_pick, row_parts, preferred_element_type=jnp.float32)
    out_label = 32.0 * out_rows[:, :seg_width] + out_rows[:, seg_width:]
    out_area = select_rows(slot_pick.astype(jnp.float32), intersection_area)
    out_weight = out_area * out_mask
    outgoing = jnp.concatenate([out_ocean, out_weight, out_label], axis=1)
    incoming = lax.all_to_all(outgoing, ("atm", "ocn"), split_axis=0, concat_axis=0, tiled=True)

    atm_planes = jnp.transpose(atm_state, (1, 0, 2))
    both = jnp.concatenate([atm_planes, jnp.transpose(diffusivity, (1, 0, 2))], axis=0)
    sizes = (atm_count, ocn_count)
    rows_padded = -(-(row_count + 2 * EDGE) // 128) * 128
    smoothed, dtall, dside = smooth_call(sizes, both, chan_count, rows_padded)

    in_labels = jnp.max(incoming[:, plane + seg_width :], axis=1).astype(jnp.int32)
    row_pick = (
        jnp.arange(row_count, dtype=jnp.int32)[:, None] == in_labels[None, :]
    ).astype(jnp.float32)
    pick_rows = row_pick.T
    air_all = jnp.dot(pick_rows, smoothed, precision=HIGHEST, preferred_element_type=jnp.float32)
    air = [air_all[:, c * seg_width : (c + 1) * seg_width] for c in range(chan_count)]
    ocean = [incoming[:, c * seg_width : (c + 1) * seg_width] for c in range(chan_count)]
    in_weight = incoming[:, plane : plane + seg_width]
    wind_east = air[1] - ocean[1]
    wind_north = air[2] - ocean[2]
    wind_speed = jnp.sqrt(wind_east * wind_east + wind_north * wind_north + 0.5)
    temp_gap = ocean[0] - air[0]
    factor = 1.0 + 0.5 * jnp.tanh(temp_gap / wind_speed)
    weighted = [
        in_weight * (0.8 * factor * wind_speed * temp_gap),
        in_weight * (0.6 * factor * wind_speed * wind_east),
        in_weight * (0.6 * factor * wind_speed * wind_north),
    ]
    returned = lax.all_to_all(
        jnp.concatenate(weighted, axis=1), ("atm", "ocn"), split_axis=0, concat_axis=0, tiled=True
    )
    sent = jnp.concatenate(weighted, axis=1)
    air_sum = jnp.dot(row_pick, sent, precision=HIGHEST, preferred_element_type=jnp.float32)
    current = diffuse_call(sizes, both, air_sum, dtall, dside)
    current, returned = lax.optimization_barrier((current, returned))
    seg_of_slot = slot_seg.T.astype(jnp.bfloat16)
    ocean_flux = pick_dot(seg_of_slot, returned).reshape(seg_count, chan_count, seg_width)
    return (jnp.transpose(current, (1, 0, 2)), ocean_flux)


def solution(mesh):
    placed = (
        P("atm", None, "ocn"),
        P("atm", None, "ocn"),
        P(("atm", "ocn"), None, None),
        P(("atm", "ocn"), None),
        P(("atm", "ocn"), None),
        P(("atm", "ocn")),
        P(("atm", "ocn"), None),
        P(("atm", "ocn")),
    )
    return jax.shard_map(
        per_device,
        mesh=mesh,
        in_specs=placed,
        out_specs=(P("atm", None, "ocn"), P(("atm", "ocn"), None, None)),
        check_vma=False,
    )
```

```python
import functools

import jax
import jax.numpy as jnp
from jax import lax
from jax.experimental import pallas as pl
from jax.experimental.pallas import tpu as pltpu
from jax.sharding import PartitionSpec as P

ITERS = 3
HIGHEST = lax.Precision.HIGHEST
HALO = ITERS
EDGE = 8


def with_halo(block, sides, width):
    for axis, dim in sides:
        count = lax.axis_size(axis)
        forward = [(i, i + 1) for i in range(count - 1)]
        backward = [(target, source) for source, target in forward]
        low = lax.ppermute(
            lax.slice_in_dim(block, block.shape[dim] - width, None, axis=dim), axis, forward
        )
        high = lax.ppermute(lax.slice_in_dim(block, 0, width, axis=dim), axis, backward)
        block = jnp.concatenate([low, block, high], axis=dim)
    return block


def beside_all(padded):
    return padded[2:, :, 1:-1] + padded[:-2, :, 1:-1] + padded[1:-1, :, 2:] + padded[1:-1, :, :-2]


def fluxes(ocean_part, air_part):
    wind_east = air_part[:, 1] - ocean_part[:, 1]
    wind_north = air_part[:, 2] - ocean_part[:, 2]
    wind_speed = jnp.sqrt(wind_east * wind_east + wind_north * wind_north + 0.5)
    temp_gap = ocean_part[:, 0] - air_part[:, 0]
    factor = 1.0 + 0.5 * jnp.tanh(temp_gap / wind_speed)
    return jnp.stack(
        [
            0.8 * factor * wind_speed * temp_gap,
            0.6 * factor * wind_speed * wind_east,
            0.6 * factor * wind_speed * wind_north,
        ],
        axis=1,
    )


def pick_dot(pick, values):
    parts = []
    rest = values
    for part in range(3):
        high = lax.reduce_precision(rest, exponent_bits=8, mantissa_bits=7)
        parts.append(high.astype(jnp.bfloat16))
        rest = rest - high
    total = None
    for part in parts:
        term = jnp.dot(pick, part, preferred_element_type=jnp.float32)
        total = term if total is None else total + term
    return total


def pick_wide(pick, values):
    parts = []
    rest = values
    for part in range(3):
        high = lax.reduce_precision(rest, exponent_bits=8, mantissa_bits=7)
        parts.append(high.astype(jnp.bfloat16))
        rest = rest - high
    width = values.shape[1]
    total = jnp.dot(pick, jnp.concatenate(parts, axis=1), preferred_element_type=jnp.float32)
    return (total[:, :width] + total[:, width : 2 * width]) + total[:, 2 * width :]


def select_rows(chosen, values, precision=HIGHEST):
    flat = values.reshape(values.shape[0], -1)
    total = jnp.dot(chosen, flat, precision=precision, preferred_element_type=jnp.float32)
    return total.reshape((chosen.shape[0],) + values.shape[1:])


MESH = pl.DeviceIdType.MESH


def exchange(sizes, x_ref, rows_buf, cols_buf, colsend, tall_s, side_s, send_sem, recv_sem):
    atm_n, ocn_n = sizes
    chans, rows, width = x_ref.shape
    rows_padded = tall_s.shape[1]
    me_a = lax.axis_index("atm")
    me_o = lax.axis_index("ocn")
    up = lax.rem(me_a + atm_n - 1, atm_n)
    down = lax.rem(me_a + 1, atm_n)
    left = lax.rem(me_o + ocn_n - 1, ocn_n)
    right = lax.rem(me_o + 1, ocn_n)
    peers = ((up, me_o), (down, me_o), (me_a, left), (me_a, right),
             (up, left), (up, right), (down, left), (down, right))
    barrier = pltpu.get_barrier_semaphore()
    for peer in peers:
        pl.semaphore_signal(barrier, 1, device_id=peer, device_id_type=MESH)
    pl.semaphore_wait(barrier, len(peers))

    spare = jnp.zeros((rows_padded - rows, width), jnp.float32)
    for c in range(chans):
        flipped = jnp.concatenate([x_ref[c], spare], axis=0).T
        colsend[0, c] = flipped[:EDGE]
        colsend[1, c] = flipped[width - EDGE :]

    last = x_ref.at[:, rows - EDGE :, :]
    first = x_ref.at[:, :EDGE, :]
    plan = (
        (last, rows_buf.at[0], (down, me_o)),
        (first, rows_buf.at[1], (up, me_o)),
        (last, rows_buf.at[2], (down, right)),
        (last, rows_buf.at[3], (down, left)),
        (first, rows_buf.at[4], (up, right)),
        (first, rows_buf.at[5], (up, left)),
        (colsend.at[0], cols_buf.at[1], (me_a, left)),
        (colsend.at[1], cols_buf.at[0], (me_a, right)),
    )
    copies = []
    for k, (src, dst, peer) in enumerate(plan):
        copy = pltpu.make_async_remote_copy(
            src, dst, send_sem.at[k], recv_sem.at[k], device_id=peer, device_id_type=MESH)
        copy.start()
        copies.append(copy)
    for copy in copies:
        copy.wait()

    has_up = me_a > 0
    has_down = me_a < atm_n - 1
    has_left = me_o > 0
    has_right = me_o < ocn_n - 1
    lane = lax.broadcasted_iota(jnp.int32, (EDGE, width), 1)
    low_lanes = lane < EDGE
    high_lanes = lane >= width - EDGE
    tail = jnp.zeros((rows_padded - rows - 2 * EDGE, width), jnp.float32)
    middle = jnp.zeros((width - 2 * EDGE, rows_padded), jnp.float32)
    for c in range(chans):
        top = jnp.where(has_up, rows_buf[0, c], 0.0)
        bottom = jnp.where(has_down, rows_buf[1, c], 0.0)
        tall_s[c] = jnp.concatenate([top, x_ref[c], bottom, tail], axis=0)
        from_left = jnp.where(has_left, cols_buf[0, c], 0.0)
        from_right = jnp.where(has_right, cols_buf[1, c], 0.0)
        own = jnp.concatenate([from_right, middle, from_left], axis=0).T
        corner_top = jnp.where(
            low_lanes & (has_up & has_right), rows_buf[3, c],
            jnp.where(high_lanes & (has_up & has_left), rows_buf[2, c], 0.0))
        corner_bottom = jnp.where(
            low_lanes & (has_down & has_right), rows_buf[5, c],
            jnp.where(high_lanes & (has_down & has_left), rows_buf[4, c], 0.0))
        side_s[c] = jnp.concatenate([corner_top, own[:rows], corner_bottom, tail], axis=0)


def exchange_scratch(chans, rows_padded, width):
    return [
        pltpu.VMEM((6, chans, EDGE, width), jnp.float32),
        pltpu.VMEM((2, chans, EDGE, rows_padded), jnp.float32),
        pltpu.VMEM((2, chans, EDGE, rows_padded), jnp.float32),
        pltpu.VMEM((chans, rows_padded, width), jnp.float32),
        pltpu.VMEM((chans, rows_padded, width), jnp.float32),
        pltpu.SemaphoreType.DMA((8,)),
        pltpu.SemaphoreType.DMA((8,)),
    ]


def stencil_sum(state):
    rows_padded, lanes = state.shape
    return (
        pltpu.roll(state, rows_padded - 1, 0)
        + pltpu.roll(state, 1, 0)
        + pltpu.roll(state, lanes - 1, 1)
        + pltpu.roll(state, 1, 1)
    )


def smooth_kernel(sizes, x_ref, out_ref, tall_out, side_out, *scratch):
    rows_buf, cols_buf, colsend, tall_s, side_s, send_sem, recv_sem = scratch
    exchange(sizes, x_ref, rows_buf, cols_buf, colsend, tall_s, side_s, send_sem, recv_sem)
    kept = tall_out.shape[0]
    rows, width = out_ref.shape[0], out_ref.shape[1] // kept
    tall_out[...] = tall_s[kept:]
    side_out[...] = side_s[kept:]
    for chan in range(kept):
        state = jnp.concatenate([tall_s[chan], side_s[chan]], axis=1)
        done = 0.5 * state + 0.125 * stencil_sum(state)
        out_ref[:, chan * width : (chan + 1) * width] = done[EDGE : EDGE + rows, :width]


SIGNS = (1.0, -1.0, -1.0)


def diffuse_kernel(sizes, both_ref, sum_ref, dtall_ref, dside_ref, out_ref, forced_s, *scratch):
    rows_buf, cols_buf, colsend, tall_s, side_s, send_sem, recv_sem = scratch
    rows, width = out_ref.shape[1], out_ref.shape[2]
    for chan in range(out_ref.shape[0]):
        forced_s[chan] = both_ref[chan] + SIGNS[chan] * sum_ref[:, chan * width : (chan + 1) * width]
    exchange(sizes, forced_s, rows_buf, cols_buf, colsend, tall_s, side_s, send_sem, recv_sem)
    for chan in range(out_ref.shape[0]):
        state = jnp.concatenate([tall_s[chan], side_s[chan]], axis=1)
        diff = jnp.concatenate([dtall_ref[chan], dside_ref[chan]], axis=1)
        for iteration in range(ITERS):
            state = state + diff * (stencil_sum(state) - 4.0 * state)
        out_ref[chan] = state[EDGE : EDGE + rows, :width]


def smooth_call(sizes, both, chans, rows_padded):
    total, rows, width = both.shape
    vmem = pl.BlockSpec(memory_space=pltpu.VMEM)
    return pl.pallas_call(
        functools.partial(smooth_kernel, sizes),
        out_shape=(
            jax.ShapeDtypeStruct((rows, chans * width), jnp.float32),
            jax.ShapeDtypeStruct((total - chans, rows_padded, width), jnp.float32),
            jax.ShapeDtypeStruct((total - chans, rows_padded, width), jnp.float32),
        ),
        in_specs=[vmem],
        out_specs=(vmem, vmem, vmem),
        scratch_shapes=exchange_scratch(total, rows_padded, width),
        compiler_params=pltpu.CompilerParams(collective_id=0, has_side_effects=True),
    )(both)


def diffuse_call(sizes, both, air_sum, dtall, dside):
    chans, rows_padded, width = dtall.shape
    rows = both.shape[1]
    vmem = pl.BlockSpec(memory_space=pltpu.VMEM)
    return pl.pallas_call(
        functools.partial(diffuse_kernel, sizes),
        out_shape=jax.ShapeDtypeStruct((chans, rows, width), jnp.float32),
        in_specs=[vmem] * 4,
        out_specs=vmem,
        scratch_shapes=[pltpu.VMEM((chans, rows, width), jnp.float32)]
        + exchange_scratch(chans, rows_padded, width),
        compiler_params=pltpu.CompilerParams(collective_id=1, has_side_effects=True),
    )(both, air_sum, dtall, dside)


def per_device(
    atm_state,
    diffusivity,
    ocean_state,
    land_mask,
    intersection_area,
    intersection_seg,
    intersection_dest,
    intersection_row,
):
    atm_count = lax.axis_size("atm")
    ocn_count = lax.axis_size("ocn")
    devices = atm_count * ocn_count
    row_count, chan_count, seg_width = atm_state.shape
    seg_count = ocean_state.shape[0]
    ov_rows = intersection_seg.shape[0]
    capacity = max(2, 2 * ov_rows // devices)
    slots = devices * capacity

    target = intersection_dest[:, 0]
    matches = (target[:, None] == jnp.arange(devices, dtype=jnp.int32)[None, :]).astype(jnp.int32)
    position = jnp.sum((jnp.cumsum(matches, axis=0) - matches) * matches, axis=1)
    slot_index = target * capacity + position
    slot_pick = (
        jnp.arange(slots, dtype=jnp.int32)[:, None] == slot_index[None, :]
    ).astype(jnp.bfloat16)
    seg_pick = (
        intersection_seg[:, None] == jnp.arange(seg_count, dtype=jnp.int32)[None, :]
    ).astype(jnp.bfloat16)
    slot_seg = jnp.dot(slot_pick, seg_pick, preferred_element_type=jnp.float32)
    plane = chan_count * seg_width
    out_ocean = select_rows(slot_seg, ocean_state.reshape(seg_count, plane))
    out_mask = select_rows(slot_seg, land_mask.astype(jnp.float32), None)
    row_high = (intersection_row // 32).astype(jnp.bfloat16)
    row_low = (intersection_row % 32).astype(jnp.bfloat16)
    row_parts = jnp.concatenate(
        [jnp.broadcast_to(row_high[:, None], (ov_rows, seg_width)),
         jnp.broadcast_to(row_low[:, None], (ov_rows, seg_width))], axis=1
    )
    out_rows = jnp.dot(slot_pick, row_parts, preferred_element_type=jnp.float32)
    out_label = 32.0 * out_rows[:, :seg_width] + out_rows[:, seg_width:]
    out_area = select_rows(slot_pick.astype(jnp.float32), intersection_area)
    out_weight = out_area * out_mask
    outgoing = jnp.concatenate([out_ocean, out_weight, out_label], axis=1)
    incoming = lax.all_to_all(outgoing, ("atm", "ocn"), split_axis=0, concat_axis=0, tiled=True)

    atm_planes = jnp.transpose(atm_state, (1, 0, 2))
    both = jnp.concatenate([atm_planes, jnp.transpose(diffusivity, (1, 0, 2))], axis=0)
    sizes = (atm_count, ocn_count)
    rows_padded = -(-(row_count + 2 * EDGE) // 128) * 128
    smoothed, dtall, dside = smooth_call(sizes, both, chan_count, rows_padded)

    in_labels = jnp.max(incoming[:, plane + seg_width :], axis=1).astype(jnp.int32)
    row_pick = (
        jnp.arange(row_count, dtype=jnp.int32)[:, None] == in_labels[None, :]
    ).astype(jnp.float32)
    pick_rows = row_pick.T
    air_all = pick_wide(pick_rows.astype(jnp.bfloat16), smoothed)
    air = [air_all[:, c * seg_width : (c + 1) * seg_width] for c in range(chan_count)]
    ocean = [incoming[:, c * seg_width : (c + 1) * seg_width] for c in range(chan_count)]
    in_weight = incoming[:, plane : plane + seg_width]
    wind_east = air[1] - ocean[1]
    wind_north = air[2] - ocean[2]
    wind_speed = jnp.sqrt(wind_east * wind_east + wind_north * wind_north + 0.5)
    temp_gap = ocean[0] - air[0]
    factor = 1.0 + 0.5 * jnp.tanh(temp_gap / wind_speed)
    weighted = [
        in_weight * (0.8 * factor * wind_speed * temp_gap),
        in_weight * (0.6 * factor * wind_speed * wind_east),
        in_weight * (0.6 * factor * wind_speed * wind_north),
    ]
    returned = lax.all_to_all(
        jnp.concatenate(weighted, axis=1), ("atm", "ocn"), split_axis=0, concat_axis=0, tiled=True
    )
    sent = jnp.concatenate(weighted, axis=1)
    air_sum = pick_wide(row_pick.astype(jnp.bfloat16), sent)
    current = diffuse_call(sizes, both, air_sum, dtall, dside)
    current, returned = lax.optimization_barrier((current, returned))
    seg_of_slot = slot_seg.T.astype(jnp.bfloat16)
    ocean_flux = pick_dot(seg_of_slot, returned).reshape(seg_count, chan_count, seg_width)
    return (jnp.transpose(current, (1, 0, 2)), ocean_flux)


def solution(mesh):
    placed = (
        P("atm", None, "ocn"),
        P("atm", None, "ocn"),
        P(("atm", "ocn"), None, None),
        P(("atm", "ocn"), None),
        P(("atm", "ocn"), None),
        P(("atm", "ocn")),
        P(("atm", "ocn"), None),
        P(("atm", "ocn")),
    )
    return jax.shard_map(
        per_device,
        mesh=mesh,
        in_specs=placed,
        out_specs=(P("atm", None, "ocn"), P(("atm", "ocn"), None, None)),
        check_vma=False,
    )
```

```python
import functools

import jax
import jax.numpy as jnp
from jax import lax
from jax.experimental import pallas as pl
from jax.experimental.pallas import tpu as pltpu
from jax.sharding import PartitionSpec as P

ITERS = 3
HIGHEST = lax.Precision.HIGHEST
HALO = ITERS
EDGE = 8


def with_halo(block, sides, width):
    for axis, dim in sides:
        count = lax.axis_size(axis)
        forward = [(i, i + 1) for i in range(count - 1)]
        backward = [(target, source) for source, target in forward]
        low = lax.ppermute(
            lax.slice_in_dim(block, block.shape[dim] - width, None, axis=dim), axis, forward
        )
        high = lax.ppermute(lax.slice_in_dim(block, 0, width, axis=dim), axis, backward)
        block = jnp.concatenate([low, block, high], axis=dim)
    return block


def beside_all(padded):
    return padded[2:, :, 1:-1] + padded[:-2, :, 1:-1] + padded[1:-1, :, 2:] + padded[1:-1, :, :-2]


def fluxes(ocean_part, air_part):
    wind_east = air_part[:, 1] - ocean_part[:, 1]
    wind_north = air_part[:, 2] - ocean_part[:, 2]
    wind_speed = jnp.sqrt(wind_east * wind_east + wind_north * wind_north + 0.5)
    temp_gap = ocean_part[:, 0] - air_part[:, 0]
    factor = 1.0 + 0.5 * jnp.tanh(temp_gap / wind_speed)
    return jnp.stack(
        [
            0.8 * factor * wind_speed * temp_gap,
            0.6 * factor * wind_speed * wind_east,
            0.6 * factor * wind_speed * wind_north,
        ],
        axis=1,
    )


def pick_dot(pick, values):
    parts = []
    rest = values
    for part in range(3):
        high = lax.reduce_precision(rest, exponent_bits=8, mantissa_bits=7)
        parts.append(high.astype(jnp.bfloat16))
        rest = rest - high
    total = None
    for part in parts:
        term = jnp.dot(pick, part, preferred_element_type=jnp.float32)
        total = term if total is None else total + term
    return total


def select_rows(chosen, values, precision=HIGHEST):
    flat = values.reshape(values.shape[0], -1)
    total = jnp.dot(chosen, flat, precision=precision, preferred_element_type=jnp.float32)
    return total.reshape((chosen.shape[0],) + values.shape[1:])


MESH = pl.DeviceIdType.MESH


def exchange(sizes, x_ref, rows_buf, cols_buf, colsend, tall_s, side_s, send_sem, recv_sem):
    atm_n, ocn_n = sizes
    chans, rows, width = x_ref.shape
    rows_padded = tall_s.shape[1]
    me_a = lax.axis_index("atm")
    me_o = lax.axis_index("ocn")
    up = lax.rem(me_a + atm_n - 1, atm_n)
    down = lax.rem(me_a + 1, atm_n)
    left = lax.rem(me_o + ocn_n - 1, ocn_n)
    right = lax.rem(me_o + 1, ocn_n)
    peers = ((up, me_o), (down, me_o), (me_a, left), (me_a, right),
             (up, left), (up, right), (down, left), (down, right))
    barrier = pltpu.get_barrier_semaphore()
    for peer in peers:
        pl.semaphore_signal(barrier, 1, device_id=peer, device_id_type=MESH)
    pl.semaphore_wait(barrier, len(peers))

    spare = jnp.zeros((rows_padded - rows, width), jnp.float32)
    for c in range(chans):
        flipped = jnp.concatenate([x_ref[c], spare], axis=0).T
        colsend[0, c] = flipped[:EDGE]
        colsend[1, c] = flipped[width - EDGE :]

    last = x_ref.at[:, rows - EDGE :, :]
    first = x_ref.at[:, :EDGE, :]
    plan = (
        (last, rows_buf.at[0], (down, me_o)),
        (first, rows_buf.at[1], (up, me_o)),
        (last, rows_buf.at[2], (down, right)),
        (last, rows_buf.at[3], (down, left)),
        (first, rows_buf.at[4], (up, right)),
        (first, rows_buf.at[5], (up, left)),
        (colsend.at[0], cols_buf.at[1], (me_a, left)),
        (colsend.at[1], cols_buf.at[0], (me_a, right)),
    )
    copies = []
    for k, (src, dst, peer) in enumerate(plan):
        copy = pltpu.make_async_remote_copy(
            src, dst, send_sem.at[k], recv_sem.at[k], device_id=peer, device_id_type=MESH)
        copy.start()
        copies.append(copy)
    for copy in copies:
        copy.wait()

    has_up = me_a > 0
    has_down = me_a < atm_n - 1
    has_left = me_o > 0
    has_right = me_o < ocn_n - 1
    lane = lax.broadcasted_iota(jnp.int32, (EDGE, width), 1)
    low_lanes = lane < EDGE
    high_lanes = lane >= width - EDGE
    tail = jnp.zeros((rows_padded - rows - 2 * EDGE, width), jnp.float32)
    middle = jnp.zeros((width - 2 * EDGE, rows_padded), jnp.float32)
    for c in range(chans):
        top = jnp.where(has_up, rows_buf[0, c], 0.0)
        bottom = jnp.where(has_down, rows_buf[1, c], 0.0)
        tall_s[c] = jnp.concatenate([top, x_ref[c], bottom, tail], axis=0)
        from_left = jnp.where(has_left, cols_buf[0, c], 0.0)
        from_right = jnp.where(has_right, cols_buf[1, c], 0.0)
        own = jnp.concatenate([from_right, middle, from_left], axis=0).T
        corner_top = jnp.where(
            low_lanes & (has_up & has_right), rows_buf[3, c],
            jnp.where(high_lanes & (has_up & has_left), rows_buf[2, c], 0.0))
        corner_bottom = jnp.where(
            low_lanes & (has_down & has_right), rows_buf[5, c],
            jnp.where(high_lanes & (has_down & has_left), rows_buf[4, c], 0.0))
        side_s[c] = jnp.concatenate([corner_top, own[:rows], corner_bottom, tail], axis=0)


def exchange_scratch(chans, rows_padded, width):
    return [
        pltpu.VMEM((6, chans, EDGE, width), jnp.float32),
        pltpu.VMEM((2, chans, EDGE, rows_padded), jnp.float32),
        pltpu.VMEM((2, chans, EDGE, rows_padded), jnp.float32),
        pltpu.VMEM((chans, rows_padded, width), jnp.float32),
        pltpu.VMEM((chans, rows_padded, width), jnp.float32),
        pltpu.SemaphoreType.DMA((8,)),
        pltpu.SemaphoreType.DMA((8,)),
    ]


def stencil_sum(state):
    rows_padded, lanes = state.shape
    return (
        pltpu.roll(state, rows_padded - 1, 0)
        + pltpu.roll(state, 1, 0)
        + pltpu.roll(state, lanes - 1, 1)
        + pltpu.roll(state, 1, 1)
    )


def smooth_kernel(sizes, x_ref, out_ref, *scratch):
    rows_buf, cols_buf, colsend, tall_s, side_s, send_sem, recv_sem = scratch
    exchange(sizes, x_ref, rows_buf, cols_buf, colsend, tall_s, side_s, send_sem, recv_sem)
    chans = x_ref.shape[0]
    rows, width = out_ref.shape[0], out_ref.shape[1] // chans
    for chan in range(chans):
        state = jnp.concatenate([tall_s[chan], side_s[chan]], axis=1)
        done = 0.5 * state + 0.125 * stencil_sum(state)
        out_ref[:, chan * width : (chan + 1) * width] = done[EDGE : EDGE + rows, :width]


SIGNS = (1.0, -1.0, -1.0)


def diffuse_kernel(sizes, both_ref, sum_ref, out_ref, forced_s, *scratch):
    rows_buf, cols_buf, colsend, tall_s, side_s, send_sem, recv_sem = scratch
    chans, rows, width = out_ref.shape
    for chan in range(chans):
        forced_s[chan] = both_ref[chan] + SIGNS[chan] * sum_ref[:, chan * width : (chan + 1) * width]
        forced_s[chans + chan] = both_ref[chans + chan]
    exchange(sizes, forced_s, rows_buf, cols_buf, colsend, tall_s, side_s, send_sem, recv_sem)
    for chan in range(chans):
        state = jnp.concatenate([tall_s[chan], side_s[chan]], axis=1)
        diff = jnp.concatenate([tall_s[chans + chan], side_s[chans + chan]], axis=1)
        for iteration in range(ITERS):
            state = state + diff * (stencil_sum(state) - 4.0 * state)
        out_ref[chan] = state[EDGE : EDGE + rows, :width]


def smooth_call(sizes, planes, rows_padded):
    chans, rows, width = planes.shape
    vmem = pl.BlockSpec(memory_space=pltpu.VMEM)
    return pl.pallas_call(
        functools.partial(smooth_kernel, sizes),
        out_shape=jax.ShapeDtypeStruct((rows, chans * width), jnp.float32),
        in_specs=[vmem],
        out_specs=vmem,
        scratch_shapes=exchange_scratch(chans, rows_padded, width),
        compiler_params=pltpu.CompilerParams(collective_id=0, has_side_effects=True),
    )(planes)


def diffuse_call(sizes, both, air_sum, rows_padded):
    total, rows, width = both.shape
    chans = total // 2
    vmem = pl.BlockSpec(memory_space=pltpu.VMEM)
    return pl.pallas_call(
        functools.partial(diffuse_kernel, sizes),
        out_shape=jax.ShapeDtypeStruct((chans, rows, width), jnp.float32),
        in_specs=[vmem] * 2,
        out_specs=vmem,
        scratch_shapes=[pltpu.VMEM((total, rows, width), jnp.float32)]
        + exchange_scratch(total, rows_padded, width),
        compiler_params=pltpu.CompilerParams(collective_id=1, has_side_effects=True),
    )(both, air_sum)


def per_device(
    atm_state,
    diffusivity,
    ocean_state,
    land_mask,
    intersection_area,
    intersection_seg,
    intersection_dest,
    intersection_row,
):
    atm_count = lax.axis_size("atm")
    ocn_count = lax.axis_size("ocn")
    devices = atm_count * ocn_count
    row_count, chan_count, seg_width = atm_state.shape
    seg_count = ocean_state.shape[0]
    ov_rows = intersection_seg.shape[0]
    capacity = max(2, 2 * ov_rows // devices)
    slots = devices * capacity

    target = intersection_dest[:, 0]
    matches = (target[:, None] == jnp.arange(devices, dtype=jnp.int32)[None, :]).astype(jnp.int32)
    position = jnp.sum((jnp.cumsum(matches, axis=0) - matches) * matches, axis=1)
    slot_index = target * capacity + position
    slot_pick = (
        jnp.arange(slots, dtype=jnp.int32)[:, None] == slot_index[None, :]
    ).astype(jnp.bfloat16)
    seg_pick = (
        intersection_seg[:, None] == jnp.arange(seg_count, dtype=jnp.int32)[None, :]
    ).astype(jnp.bfloat16)
    slot_seg = jnp.dot(slot_pick, seg_pick, preferred_element_type=jnp.float32)
    plane = chan_count * seg_width
    out_ocean = select_rows(slot_seg, ocean_state.reshape(seg_count, plane))
    out_mask = select_rows(slot_seg, land_mask.astype(jnp.float32), None)
    row_high = (intersection_row // 32).astype(jnp.bfloat16)
    row_low = (intersection_row % 32).astype(jnp.bfloat16)
    row_parts = jnp.concatenate(
        [jnp.broadcast_to(row_high[:, None], (ov_rows, seg_width)),
         jnp.broadcast_to(row_low[:, None], (ov_rows, seg_width))], axis=1
    )
    out_rows = jnp.dot(slot_pick, row_parts, preferred_element_type=jnp.float32)
    out_label = 32.0 * out_rows[:, :seg_width] + out_rows[:, seg_width:]
    out_area = select_rows(slot_pick.astype(jnp.float32), intersection_area)
    out_weight = out_area * out_mask
    outgoing = jnp.concatenate([out_ocean, out_weight, out_label], axis=1)
    incoming = lax.all_to_all(outgoing, ("atm", "ocn"), split_axis=0, concat_axis=0, tiled=True)

    atm_planes = jnp.transpose(atm_state, (1, 0, 2))
    both = jnp.concatenate([atm_planes, jnp.transpose(diffusivity, (1, 0, 2))], axis=0)
    sizes = (atm_count, ocn_count)
    rows_padded = -(-(row_count + 2 * EDGE) // 128) * 128
    smoothed = smooth_call(sizes, atm_planes, rows_padded)

    in_labels = jnp.max(incoming[:, plane + seg_width :], axis=1).astype(jnp.int32)
    row_pick = (
        jnp.arange(row_count, dtype=jnp.int32)[:, None] == in_labels[None, :]
    ).astype(jnp.float32)
    pick_rows = row_pick.T
    air_all = jnp.dot(pick_rows, smoothed, precision=HIGHEST, preferred_element_type=jnp.float32)
    air = [air_all[:, c * seg_width : (c + 1) * seg_width] for c in range(chan_count)]
    ocean = [incoming[:, c * seg_width : (c + 1) * seg_width] for c in range(chan_count)]
    in_weight = incoming[:, plane : plane + seg_width]
    wind_east = air[1] - ocean[1]
    wind_north = air[2] - ocean[2]
    wind_speed = jnp.sqrt(wind_east * wind_east + wind_north * wind_north + 0.5)
    temp_gap = ocean[0] - air[0]
    factor = 1.0 + 0.5 * jnp.tanh(temp_gap / wind_speed)
    weighted = [
        in_weight * (0.8 * factor * wind_speed * temp_gap),
        in_weight * (0.6 * factor * wind_speed * wind_east),
        in_weight * (0.6 * factor * wind_speed * wind_north),
    ]
    returned = lax.all_to_all(
        jnp.concatenate(weighted, axis=1), ("atm", "ocn"), split_axis=0, concat_axis=0, tiled=True
    )
    sent = jnp.concatenate(weighted, axis=1)
    air_sum = jnp.dot(row_pick, sent, precision=HIGHEST, preferred_element_type=jnp.float32)
    current = diffuse_call(sizes, both, air_sum, rows_padded)
    current, returned = lax.optimization_barrier((current, returned))
    seg_of_slot = slot_seg.T.astype(jnp.bfloat16)
    ocean_flux = pick_dot(seg_of_slot, returned).reshape(seg_count, chan_count, seg_width)
    return (jnp.transpose(current, (1, 0, 2)), ocean_flux)


def solution(mesh):
    placed = (
        P("atm", None, "ocn"),
        P("atm", None, "ocn"),
        P(("atm", "ocn"), None, None),
        P(("atm", "ocn"), None),
        P(("atm", "ocn"), None),
        P(("atm", "ocn")),
        P(("atm", "ocn"), None),
        P(("atm", "ocn")),
    )
    return jax.shard_map(
        per_device,
        mesh=mesh,
        in_specs=placed,
        out_specs=(P("atm", None, "ocn"), P(("atm", "ocn"), None, None)),
        check_vma=False,
    )
```

```python
import functools

import jax
import jax.numpy as jnp
from jax import lax
from jax.experimental import pallas as pl
from jax.experimental.pallas import tpu as pltpu
from jax.sharding import PartitionSpec as P

ITERS = 3
HIGHEST = lax.Precision.HIGHEST
HALO = ITERS
EDGE = 8


def with_halo(block, sides, width):
    for axis, dim in sides:
        count = lax.axis_size(axis)
        forward = [(i, i + 1) for i in range(count - 1)]
        backward = [(target, source) for source, target in forward]
        low = lax.ppermute(
            lax.slice_in_dim(block, block.shape[dim] - width, None, axis=dim), axis, forward
        )
        high = lax.ppermute(lax.slice_in_dim(block, 0, width, axis=dim), axis, backward)
        block = jnp.concatenate([low, block, high], axis=dim)
    return block


def beside_all(padded):
    return padded[2:, :, 1:-1] + padded[:-2, :, 1:-1] + padded[1:-1, :, 2:] + padded[1:-1, :, :-2]


def fluxes(ocean_part, air_part):
    wind_east = air_part[:, 1] - ocean_part[:, 1]
    wind_north = air_part[:, 2] - ocean_part[:, 2]
    wind_speed = jnp.sqrt(wind_east * wind_east + wind_north * wind_north + 0.5)
    temp_gap = ocean_part[:, 0] - air_part[:, 0]
    factor = 1.0 + 0.5 * jnp.tanh(temp_gap / wind_speed)
    return jnp.stack(
        [
            0.8 * factor * wind_speed * temp_gap,
            0.6 * factor * wind_speed * wind_east,
            0.6 * factor * wind_speed * wind_north,
        ],
        axis=1,
    )


def pick_dot(pick, values):
    parts = []
    rest = values
    for part in range(3):
        high = lax.reduce_precision(rest, exponent_bits=8, mantissa_bits=7)
        parts.append(high.astype(jnp.bfloat16))
        rest = rest - high
    total = None
    for part in parts:
        term = jnp.dot(pick, part, preferred_element_type=jnp.float32)
        total = term if total is None else total + term
    return total


def select_rows(chosen, values, precision=HIGHEST):
    flat = values.reshape(values.shape[0], -1)
    total = jnp.dot(chosen, flat, precision=precision, preferred_element_type=jnp.float32)
    return total.reshape((chosen.shape[0],) + values.shape[1:])


MESH = pl.DeviceIdType.MESH


def exchange(sizes, x_ref, rows_buf, cols_buf, colsend, tall_s, side_s, send_sem, recv_sem):
    atm_n, ocn_n = sizes
    chans, rows, width = x_ref.shape
    rows_padded = tall_s.shape[1]
    me_a = lax.axis_index("atm")
    me_o = lax.axis_index("ocn")
    up = lax.rem(me_a + atm_n - 1, atm_n)
    down = lax.rem(me_a + 1, atm_n)
    left = lax.rem(me_o + ocn_n - 1, ocn_n)
    right = lax.rem(me_o + 1, ocn_n)
    peers = ((up, me_o), (down, me_o), (me_a, left), (me_a, right),
             (up, left), (up, right), (down, left), (down, right))
    barrier = pltpu.get_barrier_semaphore()
    for peer in peers:
        pl.semaphore_signal(barrier, 1, device_id=peer, device_id_type=MESH)
    pl.semaphore_wait(barrier, len(peers))

    spare = jnp.zeros((rows_padded - rows, width), jnp.float32)
    for c in range(chans):
        flipped = jnp.concatenate([x_ref[c], spare], axis=0).T
        colsend[0, c] = flipped[:EDGE]
        colsend[1, c] = flipped[width - EDGE :]

    last = x_ref.at[:, rows - EDGE :, :]
    first = x_ref.at[:, :EDGE, :]
    plan = (
        (last, rows_buf.at[0], (down, me_o)),
        (first, rows_buf.at[1], (up, me_o)),
        (last, rows_buf.at[2], (down, right)),
        (last, rows_buf.at[3], (down, left)),
        (first, rows_buf.at[4], (up, right)),
        (first, rows_buf.at[5], (up, left)),
        (colsend.at[0], cols_buf.at[1], (me_a, left)),
        (colsend.at[1], cols_buf.at[0], (me_a, right)),
    )
    copies = []
    for k, (src, dst, peer) in enumerate(plan):
        copy = pltpu.make_async_remote_copy(
            src, dst, send_sem.at[k], recv_sem.at[k], device_id=peer, device_id_type=MESH)
        copy.start()
        copies.append(copy)
    for copy in copies:
        copy.wait()

    has_up = me_a > 0
    has_down = me_a < atm_n - 1
    has_left = me_o > 0
    has_right = me_o < ocn_n - 1
    lane = lax.broadcasted_iota(jnp.int32, (EDGE, width), 1)
    low_lanes = lane < EDGE
    high_lanes = lane >= width - EDGE
    tail = jnp.zeros((rows_padded - rows - 2 * EDGE, width), jnp.float32)
    middle = jnp.zeros((width - 2 * EDGE, rows_padded), jnp.float32)
    for c in range(chans):
        top = jnp.where(has_up, rows_buf[0, c], 0.0)
        bottom = jnp.where(has_down, rows_buf[1, c], 0.0)
        tall_s[c] = jnp.concatenate([top, x_ref[c], bottom, tail], axis=0)
        from_left = jnp.where(has_left, cols_buf[0, c], 0.0)
        from_right = jnp.where(has_right, cols_buf[1, c], 0.0)
        own = jnp.concatenate([from_right, middle, from_left], axis=0).T
        corner_top = jnp.where(
            low_lanes & (has_up & has_right), rows_buf[3, c],
            jnp.where(high_lanes & (has_up & has_left), rows_buf[2, c], 0.0))
        corner_bottom = jnp.where(
            low_lanes & (has_down & has_right), rows_buf[5, c],
            jnp.where(high_lanes & (has_down & has_left), rows_buf[4, c], 0.0))
        side_s[c] = jnp.concatenate([corner_top, own[:rows], corner_bottom, tail], axis=0)


def exchange_scratch(chans, rows_padded, width):
    return [
        pltpu.VMEM((6, chans, EDGE, width), jnp.float32),
        pltpu.VMEM((2, chans, EDGE, rows_padded), jnp.float32),
        pltpu.VMEM((2, chans, EDGE, rows_padded), jnp.float32),
        pltpu.VMEM((chans, rows_padded, width), jnp.float32),
        pltpu.VMEM((chans, rows_padded, width), jnp.float32),
        pltpu.SemaphoreType.DMA((8,)),
        pltpu.SemaphoreType.DMA((8,)),
    ]


def stencil_sum(state):
    rows_padded, lanes = state.shape
    return (
        pltpu.roll(state, rows_padded - 1, 0)
        + pltpu.roll(state, 1, 0)
        + pltpu.roll(state, lanes - 1, 1)
        + pltpu.roll(state, 1, 1)
    )


def smooth_kernel(sizes, x_ref, out_ref, *scratch):
    rows_buf, cols_buf, colsend, tall_s, side_s, send_sem, recv_sem = scratch
    exchange(sizes, x_ref, rows_buf, cols_buf, colsend, tall_s, side_s, send_sem, recv_sem)
    chans = x_ref.shape[0]
    rows, width = out_ref.shape[0], out_ref.shape[1] // chans
    for chan in range(chans):
        state = jnp.concatenate([tall_s[chan], side_s[chan]], axis=1)
        done = 0.5 * state + 0.125 * stencil_sum(state)
        out_ref[:, chan * width : (chan + 1) * width] = done[EDGE : EDGE + rows, :width]


SIGNS = (1.0, -1.0, -1.0)


def diffuse_kernel(sizes, both_ref, sum_ref, out_ref, forced_s, *scratch):
    rows_buf, cols_buf, colsend, tall_s, side_s, send_sem, recv_sem = scratch
    chans, rows, width = out_ref.shape
    for chan in range(chans):
        forced_s[chan] = both_ref[chan] + SIGNS[chan] * sum_ref[:, chan * width : (chan + 1) * width]
        forced_s[chans + chan] = both_ref[chans + chan]
    exchange(sizes, forced_s, rows_buf, cols_buf, colsend, tall_s, side_s, send_sem, recv_sem)
    for chan in range(chans):
        state = jnp.concatenate([tall_s[chan], side_s[chan]], axis=1)
        diff = jnp.concatenate([tall_s[chans + chan], side_s[chans + chan]], axis=1)
        for iteration in range(ITERS):
            state = state + diff * (stencil_sum(state) - 4.0 * state)
        out_ref[chan] = state[EDGE : EDGE + rows, :width]


def smooth_call(sizes, planes, rows_padded):
    chans, rows, width = planes.shape
    vmem = pl.BlockSpec(memory_space=pltpu.VMEM)
    return pl.pallas_call(
        functools.partial(smooth_kernel, sizes),
        out_shape=jax.ShapeDtypeStruct((rows, chans * width), jnp.float32),
        in_specs=[vmem],
        out_specs=vmem,
        scratch_shapes=exchange_scratch(chans, rows_padded, width),
        compiler_params=pltpu.CompilerParams(collective_id=0, has_side_effects=True),
    )(planes)


def diffuse_call(sizes, both, air_sum, rows_padded):
    total, rows, width = both.shape
    chans = total // 2
    vmem = pl.BlockSpec(memory_space=pltpu.VMEM)
    return pl.pallas_call(
        functools.partial(diffuse_kernel, sizes),
        out_shape=jax.ShapeDtypeStruct((chans, rows, width), jnp.float32),
        in_specs=[vmem] * 2,
        out_specs=vmem,
        scratch_shapes=[pltpu.VMEM((total, rows, width), jnp.float32)]
        + exchange_scratch(total, rows_padded, width),
        compiler_params=pltpu.CompilerParams(collective_id=1, has_side_effects=True),
    )(both, air_sum)


def per_device(
    atm_state,
    diffusivity,
    ocean_state,
    land_mask,
    intersection_area,
    intersection_seg,
    intersection_dest,
    intersection_row,
):
    atm_count = lax.axis_size("atm")
    ocn_count = lax.axis_size("ocn")
    devices = atm_count * ocn_count
    row_count, chan_count, seg_width = atm_state.shape
    seg_count = ocean_state.shape[0]
    ov_rows = intersection_seg.shape[0]
    capacity = max(2, 2 * ov_rows // devices)
    slots = devices * capacity

    target = intersection_dest[:, 0]
    matches = (target[:, None] == jnp.arange(devices, dtype=jnp.int32)[None, :]).astype(jnp.int32)
    position = jnp.sum((jnp.cumsum(matches, axis=0) - matches) * matches, axis=1)
    slot_index = target * capacity + position
    slot_pick = (
        jnp.arange(slots, dtype=jnp.int32)[:, None] == slot_index[None, :]
    ).astype(jnp.bfloat16)
    seg_pick = (
        intersection_seg[:, None] == jnp.arange(seg_count, dtype=jnp.int32)[None, :]
    ).astype(jnp.bfloat16)
    slot_seg = jnp.dot(slot_pick, seg_pick, preferred_element_type=jnp.float32)
    plane = chan_count * seg_width
    out_ocean = select_rows(slot_seg, ocean_state.reshape(seg_count, plane))
    out_mask = select_rows(slot_seg, land_mask.astype(jnp.float32), None)
    row_high = (intersection_row // 32).astype(jnp.bfloat16)
    row_low = (intersection_row % 32).astype(jnp.bfloat16)
    row_parts = jnp.concatenate(
        [jnp.broadcast_to(row_high[:, None], (ov_rows, seg_width)),
         jnp.broadcast_to(row_low[:, None], (ov_rows, seg_width))], axis=1
    )
    out_rows = jnp.dot(slot_pick, row_parts, preferred_element_type=jnp.float32)
    out_label = 32.0 * out_rows[:, :seg_width] + out_rows[:, seg_width:]
    out_area = select_rows(slot_pick.astype(jnp.float32), intersection_area)
    out_weight = out_area * out_mask
    outgoing = jnp.concatenate([out_ocean, out_weight, out_label], axis=1)
    incoming = lax.all_to_all(outgoing, ("atm", "ocn"), split_axis=0, concat_axis=0, tiled=True)

    atm_planes = jnp.transpose(atm_state, (1, 0, 2))
    both = jnp.concatenate([atm_planes, jnp.transpose(diffusivity, (1, 0, 2))], axis=0)
    sizes = (atm_count, ocn_count)
    rows_padded = -(-(row_count + 2 * EDGE) // 128) * 128
    atm_planes, both = lax.optimization_barrier((atm_planes, both))
    smoothed = smooth_call(sizes, atm_planes, rows_padded)

    in_labels = jnp.max(incoming[:, plane + seg_width :], axis=1).astype(jnp.int32)
    row_pick = (
        jnp.arange(row_count, dtype=jnp.int32)[:, None] == in_labels[None, :]
    ).astype(jnp.float32)
    pick_rows = row_pick.T
    air_all = jnp.dot(pick_rows, smoothed, precision=HIGHEST, preferred_element_type=jnp.float32)
    air = [air_all[:, c * seg_width : (c + 1) * seg_width] for c in range(chan_count)]
    ocean = [incoming[:, c * seg_width : (c + 1) * seg_width] for c in range(chan_count)]
    in_weight = incoming[:, plane : plane + seg_width]
    wind_east = air[1] - ocean[1]
    wind_north = air[2] - ocean[2]
    wind_speed = jnp.sqrt(wind_east * wind_east + wind_north * wind_north + 0.5)
    temp_gap = ocean[0] - air[0]
    factor = 1.0 + 0.5 * jnp.tanh(temp_gap / wind_speed)
    weighted = [
        in_weight * (0.8 * factor * wind_speed * temp_gap),
        in_weight * (0.6 * factor * wind_speed * wind_east),
        in_weight * (0.6 * factor * wind_speed * wind_north),
    ]
    returned = lax.all_to_all(
        jnp.concatenate(weighted, axis=1), ("atm", "ocn"), split_axis=0, concat_axis=0, tiled=True
    )
    sent = jnp.concatenate(weighted, axis=1)
    air_sum = jnp.dot(row_pick, sent, precision=HIGHEST, preferred_element_type=jnp.float32)
    current = diffuse_call(sizes, both, air_sum, rows_padded)
    current, returned = lax.optimization_barrier((current, returned))
    seg_of_slot = slot_seg.T.astype(jnp.bfloat16)
    ocean_flux = pick_dot(seg_of_slot, returned).reshape(seg_count, chan_count, seg_width)
    return (jnp.transpose(current, (1, 0, 2)), ocean_flux)


def solution(mesh):
    placed = (
        P("atm", None, "ocn"),
        P("atm", None, "ocn"),
        P(("atm", "ocn"), None, None),
        P(("atm", "ocn"), None),
        P(("atm", "ocn"), None),
        P(("atm", "ocn")),
        P(("atm", "ocn"), None),
        P(("atm", "ocn")),
    )
    return jax.shard_map(
        per_device,
        mesh=mesh,
        in_specs=placed,
        out_specs=(P("atm", None, "ocn"), P(("atm", "ocn"), None, None)),
        check_vma=False,
    )
```

```python
import functools

import jax
import jax.numpy as jnp
from jax import lax
from jax.experimental import pallas as pl
from jax.experimental.pallas import tpu as pltpu
from jax.sharding import PartitionSpec as P

ITERS = 3
HIGHEST = lax.Precision.HIGHEST
HALO = ITERS
EDGE = 8


def with_halo(block, sides, width):
    for axis, dim in sides:
        count = lax.axis_size(axis)
        forward = [(i, i + 1) for i in range(count - 1)]
        backward = [(target, source) for source, target in forward]
        low = lax.ppermute(
            lax.slice_in_dim(block, block.shape[dim] - width, None, axis=dim), axis, forward
        )
        high = lax.ppermute(lax.slice_in_dim(block, 0, width, axis=dim), axis, backward)
        block = jnp.concatenate([low, block, high], axis=dim)
    return block


def beside_all(padded):
    return padded[2:, :, 1:-1] + padded[:-2, :, 1:-1] + padded[1:-1, :, 2:] + padded[1:-1, :, :-2]


def fluxes(ocean_part, air_part):
    wind_east = air_part[:, 1] - ocean_part[:, 1]
    wind_north = air_part[:, 2] - ocean_part[:, 2]
    wind_speed = jnp.sqrt(wind_east * wind_east + wind_north * wind_north + 0.5)
    temp_gap = ocean_part[:, 0] - air_part[:, 0]
    factor = 1.0 + 0.5 * jnp.tanh(temp_gap / wind_speed)
    return jnp.stack(
        [
            0.8 * factor * wind_speed * temp_gap,
            0.6 * factor * wind_speed * wind_east,
            0.6 * factor * wind_speed * wind_north,
        ],
        axis=1,
    )


def pick_dot(pick, values):
    parts = []
    rest = values
    for part in range(3):
        high = lax.reduce_precision(rest, exponent_bits=8, mantissa_bits=7)
        parts.append(high.astype(jnp.bfloat16))
        rest = rest - high
    total = None
    for part in parts:
        term = jnp.dot(pick, part, preferred_element_type=jnp.float32)
        total = term if total is None else total + term
    return total


def select_rows(chosen, values, precision=HIGHEST):
    flat = values.reshape(values.shape[0], -1)
    total = jnp.dot(chosen, flat, precision=precision, preferred_element_type=jnp.float32)
    return total.reshape((chosen.shape[0],) + values.shape[1:])


MESH = pl.DeviceIdType.MESH


def exchange(sizes, x_ref, rows_buf, cols_buf, colsend, tall_s, side_s, send_sem, recv_sem):
    atm_n, ocn_n = sizes
    chans, rows, width = x_ref.shape
    rows_padded = tall_s.shape[1]
    me_a = lax.axis_index("atm")
    me_o = lax.axis_index("ocn")
    up = lax.rem(me_a + atm_n - 1, atm_n)
    down = lax.rem(me_a + 1, atm_n)
    left = lax.rem(me_o + ocn_n - 1, ocn_n)
    right = lax.rem(me_o + 1, ocn_n)
    peers = ((up, me_o), (down, me_o), (me_a, left), (me_a, right),
             (up, left), (up, right), (down, left), (down, right))
    barrier = pltpu.get_barrier_semaphore()
    for peer in peers:
        pl.semaphore_signal(barrier, 1, device_id=peer, device_id_type=MESH)
    pl.semaphore_wait(barrier, len(peers))

    spare = jnp.zeros((rows_padded - rows, width), jnp.float32)
    for c in range(chans):
        flipped = jnp.concatenate([x_ref[c], spare], axis=0).T
        colsend[0, c] = flipped[:EDGE]
        colsend[1, c] = flipped[width - EDGE :]

    last = x_ref.at[:, rows - EDGE :, :]
    first = x_ref.at[:, :EDGE, :]
    plan = (
        (last, rows_buf.at[0], (down, me_o)),
        (first, rows_buf.at[1], (up, me_o)),
        (last, rows_buf.at[2], (down, right)),
        (last, rows_buf.at[3], (down, left)),
        (first, rows_buf.at[4], (up, right)),
        (first, rows_buf.at[5], (up, left)),
        (colsend.at[0], cols_buf.at[1], (me_a, left)),
        (colsend.at[1], cols_buf.at[0], (me_a, right)),
    )
    copies = []
    for k, (src, dst, peer) in enumerate(plan):
        copy = pltpu.make_async_remote_copy(
            src, dst, send_sem.at[k], recv_sem.at[k], device_id=peer, device_id_type=MESH)
        copy.start()
        copies.append(copy)
    for copy in copies:
        copy.wait()

    has_up = me_a > 0
    has_down = me_a < atm_n - 1
    has_left = me_o > 0
    has_right = me_o < ocn_n - 1
    lane = lax.broadcasted_iota(jnp.int32, (EDGE, width), 1)
    low_lanes = lane < EDGE
    high_lanes = lane >= width - EDGE
    tail = jnp.zeros((rows_padded - rows - 2 * EDGE, width), jnp.float32)
    middle = jnp.zeros((width - 2 * EDGE, rows_padded), jnp.float32)
    for c in range(chans):
        top = jnp.where(has_up, rows_buf[0, c], 0.0)
        bottom = jnp.where(has_down, rows_buf[1, c], 0.0)
        tall_s[c] = jnp.concatenate([top, x_ref[c], bottom, tail], axis=0)
        from_left = jnp.where(has_left, cols_buf[0, c], 0.0)
        from_right = jnp.where(has_right, cols_buf[1, c], 0.0)
        own = jnp.concatenate([from_right, middle, from_left], axis=0).T
        corner_top = jnp.where(
            low_lanes & (has_up & has_right), rows_buf[3, c],
            jnp.where(high_lanes & (has_up & has_left), rows_buf[2, c], 0.0))
        corner_bottom = jnp.where(
            low_lanes & (has_down & has_right), rows_buf[5, c],
            jnp.where(high_lanes & (has_down & has_left), rows_buf[4, c], 0.0))
        side_s[c] = jnp.concatenate([corner_top, own[:rows], corner_bottom, tail], axis=0)


def exchange_scratch(chans, rows_padded, width):
    return [
        pltpu.VMEM((6, chans, EDGE, width), jnp.float32),
        pltpu.VMEM((2, chans, EDGE, rows_padded), jnp.float32),
        pltpu.VMEM((2, chans, EDGE, rows_padded), jnp.float32),
        pltpu.VMEM((chans, rows_padded, width), jnp.float32),
        pltpu.VMEM((chans, rows_padded, width), jnp.float32),
        pltpu.SemaphoreType.DMA((8,)),
        pltpu.SemaphoreType.DMA((8,)),
    ]


def stencil_sum(state):
    rows_padded, lanes = state.shape
    return (
        pltpu.roll(state, rows_padded - 1, 0)
        + pltpu.roll(state, 1, 0)
        + pltpu.roll(state, lanes - 1, 1)
        + pltpu.roll(state, 1, 1)
    )


def smooth_kernel(sizes, x_ref, out_ref, *scratch):
    rows_buf, cols_buf, colsend, tall_s, side_s, send_sem, recv_sem = scratch
    exchange(sizes, x_ref, rows_buf, cols_buf, colsend, tall_s, side_s, send_sem, recv_sem)
    chans = x_ref.shape[0]
    rows, width = out_ref.shape[0], out_ref.shape[1] // chans
    for chan in range(chans):
        state = jnp.concatenate([tall_s[chan], side_s[chan]], axis=1)
        done = 0.5 * state + 0.125 * stencil_sum(state)
        out_ref[:, chan * width : (chan + 1) * width] = done[EDGE : EDGE + rows, :width]


SIGNS = (1.0, -1.0, -1.0)


def diffuse_kernel(sizes, both_ref, sum_ref, out_ref, forced_s, *scratch):
    rows_buf, cols_buf, colsend, tall_s, side_s, send_sem, recv_sem = scratch
    chans, rows, width = out_ref.shape
    for chan in range(chans):
        forced_s[chan] = both_ref[chan] + SIGNS[chan] * sum_ref[:, chan * width : (chan + 1) * width]
        forced_s[chans + chan] = both_ref[chans + chan]
    exchange(sizes, forced_s, rows_buf, cols_buf, colsend, tall_s, side_s, send_sem, recv_sem)
    for chan in range(chans):
        state = jnp.concatenate([tall_s[chan], side_s[chan]], axis=1)
        diff = jnp.concatenate([tall_s[chans + chan], side_s[chans + chan]], axis=1)
        for iteration in range(ITERS):
            state = state + diff * (stencil_sum(state) - 4.0 * state)
        out_ref[chan] = state[EDGE : EDGE + rows, :width]


def smooth_call(sizes, planes, rows_padded):
    chans, rows, width = planes.shape
    vmem = pl.BlockSpec(memory_space=pltpu.VMEM)
    return pl.pallas_call(
        functools.partial(smooth_kernel, sizes),
        out_shape=jax.ShapeDtypeStruct((rows, chans * width), jnp.float32),
        in_specs=[vmem],
        out_specs=vmem,
        scratch_shapes=exchange_scratch(chans, rows_padded, width),
        compiler_params=pltpu.CompilerParams(collective_id=0, has_side_effects=True),
    )(planes)


def diffuse_call(sizes, both, air_sum, rows_padded):
    total, rows, width = both.shape
    chans = total // 2
    vmem = pl.BlockSpec(memory_space=pltpu.VMEM)
    return pl.pallas_call(
        functools.partial(diffuse_kernel, sizes),
        out_shape=jax.ShapeDtypeStruct((chans, rows, width), jnp.float32),
        in_specs=[vmem] * 2,
        out_specs=vmem,
        scratch_shapes=[pltpu.VMEM((total, rows, width), jnp.float32)]
        + exchange_scratch(total, rows_padded, width),
        compiler_params=pltpu.CompilerParams(collective_id=1, has_side_effects=True),
    )(both, air_sum)


def per_device(
    atm_state,
    diffusivity,
    ocean_state,
    land_mask,
    intersection_area,
    intersection_seg,
    intersection_dest,
    intersection_row,
):
    atm_count = lax.axis_size("atm")
    ocn_count = lax.axis_size("ocn")
    devices = atm_count * ocn_count
    row_count, chan_count, seg_width = atm_state.shape
    seg_count = ocean_state.shape[0]
    ov_rows = intersection_seg.shape[0]
    capacity = max(2, 2 * ov_rows // devices)
    slots = devices * capacity

    target = intersection_dest[:, 0]
    matches = (target[:, None] == jnp.arange(devices, dtype=jnp.int32)[None, :]).astype(jnp.int32)
    position = jnp.sum((jnp.cumsum(matches, axis=0) - matches) * matches, axis=1)
    slot_index = target * capacity + position
    slot_pick = (
        jnp.arange(slots, dtype=jnp.int32)[:, None] == slot_index[None, :]
    ).astype(jnp.bfloat16)
    seg_pick = (
        intersection_seg[:, None] == jnp.arange(seg_count, dtype=jnp.int32)[None, :]
    ).astype(jnp.bfloat16)
    slot_seg = jnp.dot(slot_pick, seg_pick, preferred_element_type=jnp.float32)
    plane = chan_count * seg_width
    out_ocean = select_rows(slot_seg, ocean_state.reshape(seg_count, plane))
    out_mask = select_rows(slot_seg, land_mask.astype(jnp.float32), None)
    row_high = (intersection_row // 32).astype(jnp.bfloat16)
    row_low = (intersection_row % 32).astype(jnp.bfloat16)
    row_parts = jnp.concatenate(
        [jnp.broadcast_to(row_high[:, None], (ov_rows, seg_width)),
         jnp.broadcast_to(row_low[:, None], (ov_rows, seg_width))], axis=1
    )
    out_rows = jnp.dot(slot_pick, row_parts, preferred_element_type=jnp.float32)
    out_label = 32.0 * out_rows[:, :seg_width] + out_rows[:, seg_width:]
    out_area = select_rows(slot_pick.astype(jnp.float32), intersection_area)
    out_weight = out_area * out_mask
    outgoing = jnp.concatenate([out_ocean, out_weight, out_label], axis=1)
    incoming = lax.all_to_all(outgoing, ("atm", "ocn"), split_axis=0, concat_axis=0, tiled=True)

    atm_planes = jnp.transpose(atm_state, (1, 0, 2))
    both = jnp.concatenate([atm_planes, jnp.transpose(diffusivity, (1, 0, 2))], axis=0)
    sizes = (atm_count, ocn_count)
    rows_padded = -(-(row_count + 2 * EDGE) // 128) * 128
    smoothed = smooth_call(sizes, atm_planes, rows_padded)

    in_labels = jnp.max(incoming[:, plane + seg_width :], axis=1).astype(jnp.int32)
    row_pick = (
        jnp.arange(row_count, dtype=jnp.int32)[:, None] == in_labels[None, :]
    ).astype(jnp.float32)
    pick_rows = row_pick.T
    air_all = jnp.dot(pick_rows, smoothed, precision=HIGHEST, preferred_element_type=jnp.float32)
    air = [air_all[:, c * seg_width : (c + 1) * seg_width] for c in range(chan_count)]
    ocean = [incoming[:, c * seg_width : (c + 1) * seg_width] for c in range(chan_count)]
    in_weight = incoming[:, plane : plane + seg_width]
    wind_east = air[1] - ocean[1]
    wind_north = air[2] - ocean[2]
    wind_speed = jnp.sqrt(wind_east * wind_east + wind_north * wind_north + 0.5)
    temp_gap = ocean[0] - air[0]
    factor = 1.0 + 0.5 * jnp.tanh(temp_gap / wind_speed)
    shared = in_weight * factor * wind_speed
    gap = air_all - incoming[:, :plane]
    block = lax.broadcasted_iota(jnp.int32, (1, plane), 1) // seg_width
    scale = jnp.where(block == 0, -0.8, 0.6).astype(jnp.float32)
    sent = jnp.concatenate([shared] * chan_count, axis=1) * (scale * gap)
    returned = lax.all_to_all(sent, ("atm", "ocn"), split_axis=0, concat_axis=0, tiled=True)
    air_sum = jnp.dot(row_pick, sent, precision=HIGHEST, preferred_element_type=jnp.float32)
    current = diffuse_call(sizes, both, air_sum, rows_padded)
    current, returned = lax.optimization_barrier((current, returned))
    seg_of_slot = slot_seg.T.astype(jnp.bfloat16)
    ocean_flux = pick_dot(seg_of_slot, returned).reshape(seg_count, chan_count, seg_width)
    return (jnp.transpose(current, (1, 0, 2)), ocean_flux)


def solution(mesh):
    placed = (
        P("atm", None, "ocn"),
        P("atm", None, "ocn"),
        P(("atm", "ocn"), None, None),
        P(("atm", "ocn"), None),
        P(("atm", "ocn"), None),
        P(("atm", "ocn")),
        P(("atm", "ocn"), None),
        P(("atm", "ocn")),
    )
    return jax.shard_map(
        per_device,
        mesh=mesh,
        in_specs=placed,
        out_specs=(P("atm", None, "ocn"), P(("atm", "ocn"), None, None)),
        check_vma=False,
    )
```

```python
import functools

import jax
import jax.numpy as jnp
from jax import lax
from jax.experimental import pallas as pl
from jax.experimental.pallas import tpu as pltpu
from jax.sharding import PartitionSpec as P

ITERS = 3
HIGHEST = lax.Precision.HIGHEST
HALO = ITERS
EDGE = 8


def with_halo(block, sides, width):
    for axis, dim in sides:
        count = lax.axis_size(axis)
        forward = [(i, i + 1) for i in range(count - 1)]
        backward = [(target, source) for source, target in forward]
        low = lax.ppermute(
            lax.slice_in_dim(block, block.shape[dim] - width, None, axis=dim), axis, forward
        )
        high = lax.ppermute(lax.slice_in_dim(block, 0, width, axis=dim), axis, backward)
        block = jnp.concatenate([low, block, high], axis=dim)
    return block


def beside_all(padded):
    return padded[2:, :, 1:-1] + padded[:-2, :, 1:-1] + padded[1:-1, :, 2:] + padded[1:-1, :, :-2]


def fluxes(ocean_part, air_part):
    wind_east = air_part[:, 1] - ocean_part[:, 1]
    wind_north = air_part[:, 2] - ocean_part[:, 2]
    wind_speed = jnp.sqrt(wind_east * wind_east + wind_north * wind_north + 0.5)
    temp_gap = ocean_part[:, 0] - air_part[:, 0]
    factor = 1.0 + 0.5 * jnp.tanh(temp_gap / wind_speed)
    return jnp.stack(
        [
            0.8 * factor * wind_speed * temp_gap,
            0.6 * factor * wind_speed * wind_east,
            0.6 * factor * wind_speed * wind_north,
        ],
        axis=1,
    )


def pick_dot(pick, values):
    parts = []
    rest = values
    for part in range(3):
        high = lax.reduce_precision(rest, exponent_bits=8, mantissa_bits=7)
        parts.append(high.astype(jnp.bfloat16))
        rest = rest - high
    total = None
    for part in parts:
        term = jnp.dot(pick, part, preferred_element_type=jnp.float32)
        total = term if total is None else total + term
    return total


def select_rows(chosen, values, precision=HIGHEST):
    flat = values.reshape(values.shape[0], -1)
    total = jnp.dot(chosen, flat, precision=precision, preferred_element_type=jnp.float32)
    return total.reshape((chosen.shape[0],) + values.shape[1:])


MESH = pl.DeviceIdType.MESH


def exchange(sizes, x_ref, rows_buf, cols_buf, colsend, tall_s, side_s, send_sem, recv_sem):
    atm_n, ocn_n = sizes
    chans, rows, width = x_ref.shape
    rows_padded = tall_s.shape[1]
    me_a = lax.axis_index("atm")
    me_o = lax.axis_index("ocn")
    up = lax.rem(me_a + atm_n - 1, atm_n)
    down = lax.rem(me_a + 1, atm_n)
    left = lax.rem(me_o + ocn_n - 1, ocn_n)
    right = lax.rem(me_o + 1, ocn_n)
    peers = ((up, me_o), (down, me_o), (me_a, left), (me_a, right),
             (up, left), (up, right), (down, left), (down, right))
    barrier = pltpu.get_barrier_semaphore()
    for peer in peers:
        pl.semaphore_signal(barrier, 1, device_id=peer, device_id_type=MESH)
    pl.semaphore_wait(barrier, len(peers))

    spare = jnp.zeros((rows_padded - rows, width), jnp.float32)
    for c in range(chans):
        flipped = jnp.concatenate([x_ref[c], spare], axis=0).T
        colsend[0, c] = flipped[:EDGE]
        colsend[1, c] = flipped[width - EDGE :]

    last = x_ref.at[:, rows - EDGE :, :]
    first = x_ref.at[:, :EDGE, :]
    plan = (
        (last, rows_buf.at[0], (down, me_o)),
        (first, rows_buf.at[1], (up, me_o)),
        (last, rows_buf.at[2], (down, right)),
        (last, rows_buf.at[3], (down, left)),
        (first, rows_buf.at[4], (up, right)),
        (first, rows_buf.at[5], (up, left)),
        (colsend.at[0], cols_buf.at[1], (me_a, left)),
        (colsend.at[1], cols_buf.at[0], (me_a, right)),
    )
    copies = []
    for k, (src, dst, peer) in enumerate(plan):
        copy = pltpu.make_async_remote_copy(
            src, dst, send_sem.at[k], recv_sem.at[k], device_id=peer, device_id_type=MESH)
        copy.start()
        copies.append(copy)
    for copy in copies:
        copy.wait()

    has_up = me_a > 0
    has_down = me_a < atm_n - 1
    has_left = me_o > 0
    has_right = me_o < ocn_n - 1
    lane = lax.broadcasted_iota(jnp.int32, (EDGE, width), 1)
    low_lanes = lane < EDGE
    high_lanes = lane >= width - EDGE
    tail = jnp.zeros((rows_padded - rows - 2 * EDGE, width), jnp.float32)
    middle = jnp.zeros((width - 2 * EDGE, rows_padded), jnp.float32)
    for c in range(chans):
        top = jnp.where(has_up, rows_buf[0, c], 0.0)
        bottom = jnp.where(has_down, rows_buf[1, c], 0.0)
        tall_s[c] = jnp.concatenate([top, x_ref[c], bottom, tail], axis=0)
        from_left = jnp.where(has_left, cols_buf[0, c], 0.0)
        from_right = jnp.where(has_right, cols_buf[1, c], 0.0)
        own = jnp.concatenate([from_right, middle, from_left], axis=0).T
        corner_top = jnp.where(
            low_lanes & (has_up & has_right), rows_buf[3, c],
            jnp.where(high_lanes & (has_up & has_left), rows_buf[2, c], 0.0))
        corner_bottom = jnp.where(
            low_lanes & (has_down & has_right), rows_buf[5, c],
            jnp.where(high_lanes & (has_down & has_left), rows_buf[4, c], 0.0))
        side_s[c] = jnp.concatenate([corner_top, own[:rows], corner_bottom, tail], axis=0)


def exchange_scratch(chans, rows_padded, width):
    return [
        pltpu.VMEM((6, chans, EDGE, width), jnp.float32),
        pltpu.VMEM((2, chans, EDGE, rows_padded), jnp.float32),
        pltpu.VMEM((2, chans, EDGE, rows_padded), jnp.float32),
        pltpu.VMEM((chans, rows_padded, width), jnp.float32),
        pltpu.VMEM((chans, rows_padded, width), jnp.float32),
        pltpu.SemaphoreType.DMA((8,)),
        pltpu.SemaphoreType.DMA((8,)),
    ]


def stencil_sum(state):
    rows_padded, lanes = state.shape
    return (
        pltpu.roll(state, rows_padded - 1, 0)
        + pltpu.roll(state, 1, 0)
        + pltpu.roll(state, lanes - 1, 1)
        + pltpu.roll(state, 1, 1)
    )


def smooth_kernel(sizes, x_ref, out_ref, *scratch):
    rows_buf, cols_buf, colsend, tall_s, side_s, send_sem, recv_sem = scratch
    exchange(sizes, x_ref, rows_buf, cols_buf, colsend, tall_s, side_s, send_sem, recv_sem)
    chans = x_ref.shape[0]
    rows, width = out_ref.shape[0], out_ref.shape[1] // chans
    for chan in range(chans):
        state = jnp.concatenate([tall_s[chan], side_s[chan]], axis=1)
        done = 0.5 * state + 0.125 * stencil_sum(state)
        out_ref[:, chan * width : (chan + 1) * width] = done[EDGE : EDGE + rows, :width]


SIGNS = (1.0, -1.0, -1.0)


def diffuse_kernel(sizes, both_ref, sum_ref, out_ref, forced_s, *scratch):
    rows_buf, cols_buf, colsend, tall_s, side_s, send_sem, recv_sem = scratch
    chans, rows, width = out_ref.shape
    for chan in range(chans):
        forced_s[chan] = both_ref[chan] + SIGNS[chan] * sum_ref[:, chan * width : (chan + 1) * width]
        forced_s[chans + chan] = both_ref[chans + chan]
    exchange(sizes, forced_s, rows_buf, cols_buf, colsend, tall_s, side_s, send_sem, recv_sem)
    for chan in range(chans):
        state = jnp.concatenate([tall_s[chan], side_s[chan]], axis=1)
        diff = jnp.concatenate([tall_s[chans + chan], side_s[chans + chan]], axis=1)
        for iteration in range(ITERS):
            state = state + diff * (stencil_sum(state) - 4.0 * state)
        out_ref[chan] = state[EDGE : EDGE + rows, :width]


def smooth_call(sizes, planes, rows_padded):
    chans, rows, width = planes.shape
    vmem = pl.BlockSpec(memory_space=pltpu.VMEM)
    return pl.pallas_call(
        functools.partial(smooth_kernel, sizes),
        out_shape=jax.ShapeDtypeStruct((rows, chans * width), jnp.float32),
        in_specs=[vmem],
        out_specs=vmem,
        scratch_shapes=exchange_scratch(chans, rows_padded, width),
        compiler_params=pltpu.CompilerParams(collective_id=0, has_side_effects=True),
    )(planes)


def diffuse_call(sizes, both, air_sum, rows_padded):
    total, rows, width = both.shape
    chans = total // 2
    vmem = pl.BlockSpec(memory_space=pltpu.VMEM)
    return pl.pallas_call(
        functools.partial(diffuse_kernel, sizes),
        out_shape=jax.ShapeDtypeStruct((chans, rows, width), jnp.float32),
        in_specs=[vmem] * 2,
        out_specs=vmem,
        scratch_shapes=[pltpu.VMEM((total, rows, width), jnp.float32)]
        + exchange_scratch(total, rows_padded, width),
        compiler_params=pltpu.CompilerParams(collective_id=1, has_side_effects=True),
    )(both, air_sum)


def per_device(
    atm_state,
    diffusivity,
    ocean_state,
    land_mask,
    intersection_area,
    intersection_seg,
    intersection_dest,
    intersection_row,
):
    atm_count = lax.axis_size("atm")
    ocn_count = lax.axis_size("ocn")
    devices = atm_count * ocn_count
    row_count, chan_count, seg_width = atm_state.shape
    seg_count = ocean_state.shape[0]
    ov_rows = intersection_seg.shape[0]
    capacity = max(2, 2 * ov_rows // devices)
    slots = devices * capacity

    target = intersection_dest[:, 0]
    matches = (target[:, None] == jnp.arange(devices, dtype=jnp.int32)[None, :]).astype(jnp.int32)
    position = jnp.sum((jnp.cumsum(matches, axis=0) - matches) * matches, axis=1)
    slot_index = target * capacity + position
    slot_pick = (
        jnp.arange(slots, dtype=jnp.int32)[:, None] == slot_index[None, :]
    ).astype(jnp.bfloat16)
    seg_pick = (
        intersection_seg[:, None] == jnp.arange(seg_count, dtype=jnp.int32)[None, :]
    ).astype(jnp.bfloat16)
    slot_seg = jnp.dot(slot_pick, seg_pick, preferred_element_type=jnp.float32)
    plane = chan_count * seg_width
    out_ocean = select_rows(slot_seg, ocean_state.reshape(seg_count, plane))
    out_mask = select_rows(slot_seg, land_mask.astype(jnp.float32), None)
    row_high = (intersection_row // 32).astype(jnp.bfloat16)
    row_low = (intersection_row % 32).astype(jnp.bfloat16)
    row_parts = jnp.concatenate(
        [jnp.broadcast_to(row_high[:, None], (ov_rows, seg_width)),
         jnp.broadcast_to(row_low[:, None], (ov_rows, seg_width))], axis=1
    )
    out_rows = jnp.dot(slot_pick, row_parts, preferred_element_type=jnp.float32)
    out_label = 32.0 * out_rows[:, :seg_width] + out_rows[:, seg_width:]
    out_area = select_rows(slot_pick.astype(jnp.float32), intersection_area)
    out_weight = out_area * out_mask
    outgoing = jnp.concatenate([out_ocean, out_weight, out_label], axis=1)
    incoming = lax.all_to_all(outgoing, ("atm", "ocn"), split_axis=0, concat_axis=0, tiled=True)

    atm_planes = jnp.transpose(atm_state, (1, 0, 2))
    both = jnp.concatenate([atm_planes, jnp.transpose(diffusivity, (1, 0, 2))], axis=0)
    sizes = (atm_count, ocn_count)
    rows_padded = -(-(row_count + 2 * EDGE) // 128) * 128
    smoothed = smooth_call(sizes, atm_planes, rows_padded)

    in_labels = jnp.max(incoming[:, plane + seg_width :], axis=1).astype(jnp.int32)
    row_pick = (
        jnp.arange(row_count, dtype=jnp.int32)[:, None] == in_labels[None, :]
    ).astype(jnp.float32)
    pick_rows = (
        in_labels[:, None] == jnp.arange(row_count, dtype=jnp.int32)[None, :]
    ).astype(jnp.float32)
    air_all = jnp.dot(pick_rows, smoothed, precision=HIGHEST, preferred_element_type=jnp.float32)
    air = [air_all[:, c * seg_width : (c + 1) * seg_width] for c in range(chan_count)]
    ocean = [incoming[:, c * seg_width : (c + 1) * seg_width] for c in range(chan_count)]
    in_weight = incoming[:, plane : plane + seg_width]
    wind_east = air[1] - ocean[1]
    wind_north = air[2] - ocean[2]
    wind_speed = jnp.sqrt(wind_east * wind_east + wind_north * wind_north + 0.5)
    temp_gap = ocean[0] - air[0]
    factor = 1.0 + 0.5 * jnp.tanh(temp_gap / wind_speed)
    shared = in_weight * factor * wind_speed
    gap = air_all - incoming[:, :plane]
    block = lax.broadcasted_iota(jnp.int32, (1, plane), 1) // seg_width
    scale = jnp.where(block == 0, -0.8, 0.6).astype(jnp.float32)
    sent = jnp.concatenate([shared] * chan_count, axis=1) * (scale * gap)
    returned = lax.all_to_all(sent, ("atm", "ocn"), split_axis=0, concat_axis=0, tiled=True)
    air_sum = jnp.dot(row_pick, sent, precision=HIGHEST, preferred_element_type=jnp.float32)
    current = diffuse_call(sizes, both, air_sum, rows_padded)
    current, returned = lax.optimization_barrier((current, returned))
    seg_of_slot = slot_seg.T.astype(jnp.bfloat16)
    ocean_flux = pick_dot(seg_of_slot, returned).reshape(seg_count, chan_count, seg_width)
    return (jnp.transpose(current, (1, 0, 2)), ocean_flux)


def solution(mesh):
    placed = (
        P("atm", None, "ocn"),
        P("atm", None, "ocn"),
        P(("atm", "ocn"), None, None),
        P(("atm", "ocn"), None),
        P(("atm", "ocn"), None),
        P(("atm", "ocn")),
        P(("atm", "ocn"), None),
        P(("atm", "ocn")),
    )
    return jax.shard_map(
        per_device,
        mesh=mesh,
        in_specs=placed,
        out_specs=(P("atm", None, "ocn"), P(("atm", "ocn"), None, None)),
        check_vma=False,
    )
```
